128 devices in a mesh: row: 16 (over x, y), col: 8 (over z, core).
Axes of the slice: x: 4, y: 4, z: 4, core: 2. Of those that a mesh axis runs over, the one named last changes fastest.
Arguments:
- saved_factor: float32 [8192, 8192], P('row', 'col'), may hold values from -1 to 3, as said below
- cotangent: float32 [8192, 8192], P('row', 'col'), may hold values from -6 to 6
Outputs:
- adjoint: float32 [8192, 8192], P('row', 'col')
The draws below stay inside these ranges and needn't reach their ends.
Inputs may be any that keep to these rules, and one draw needn't show every extreme that they name: `saved_factor`: entry (i, j) is zero where j > i + 8192 - 3 * 512, and 1 or more where j = i + 8192 - 3 * 512.
All inputs are finite; a program needn't handle non-finite values.
Results may differ from the reference program's by a relative error of at most 0.0001.
Values sent between devices are 32-bit elements; how exact they have to be, the bound alone decides.
A program may use at most 128 MiB of HBM per device.

```python
import math
import jax
import jax.numpy as jnp
from jax import lax

NB = 512
NP = 3
ORDER = 8192


def draw_saved_factor(key, part):
    first_key = jax.random.fold_in(key, 11)
    second_key = jax.random.fold_in(key, 23)
    spread = jax.random.normal(first_key, (ORDER, ORDER), jnp.float32)
    diagonal = jax.random.uniform(second_key, (ORDER,), jnp.float32, 1.0, 2.0)
    gap = ORDER - NP * NB
    row_pos = jnp.arange(ORDER, dtype=jnp.int32)[:, None]
    col_pos = jnp.arange(ORDER, dtype=jnp.int32)[None, :]
    lower_part = jnp.where(col_pos < row_pos + gap, spread, 0.0) * (0.3 / math.sqrt(NB))
    on_diag = jnp.where(col_pos == row_pos + gap, diagonal[:, None], 0.0)
    return (lower_part + on_diag).astype(jnp.float32)


def block_levels(own_key, shape, cuts, smallest, top_value):
    def one(position, blocks):
        draws = jax.random.uniform(jax.random.fold_in(jax.random.fold_in(own_key, 6), position), (blocks,), jnp.float32, smallest / len(cuts), top_value / len(cuts))
        return jnp.repeat(jnp.exp(draws), shape[position] // blocks).reshape((-1,) + (1,) * (len(shape) - position - 1))

    gain = one(*cuts[0])
    for cut in cuts[1:]:
        gain = gain * one(*cut)
    return gain


def noise(key, shape, scale, bound, pieces=(), kind=jnp.bfloat16):
    values = scale * jax.random.normal(key, shape, jnp.float32)
    if pieces:
        values = values * block_levels(key, shape, pieces, -0.22, 0.18)
    return jnp.clip(values, -bound, bound).astype(kind)


def setup_inputs(seed: int = 0) -> dict:
    keys = jax.random.split(jax.random.key(seed), 3)
    return {
        "saved_factor": draw_saved_factor(jax.random.fold_in(keys[2], 71), 0),
        "cotangent": noise(keys[1], (ORDER, ORDER), 1.0, 6.0, ((0, 16), (1, 8)), jnp.float32),
    }


precise = lax.Precision.HIGHEST

def matmul(left_side, right_side):
    return jnp.dot(left_side.astype(jnp.float32), right_side.astype(jnp.float32), precision=precise, preferred_element_type=jnp.float32)

def inner_rows(left_side, right_side):
    return lax.dot_general(left_side.astype(jnp.float32), right_side.astype(jnp.float32), (((0,), (0,)), ((), ())), precision=precise, preferred_element_type=jnp.float32)

def lower_half(matrix):
    return jnp.tril(matrix) - 0.5 * jnp.diag(jnp.diag(matrix))

def reference(saved_factor, cotangent):
    full_order = saved_factor.shape[0]
    identity = jnp.eye(NB, dtype=saved_factor.dtype)
    running = cotangent
    for number in range(NP):
        row_start = (NP - 1 - number) * NB
        row_end = row_start + NB
        col_start = full_order - (number + 1) * NB
        col_end = col_start + NB
        diag_factor = saved_factor[row_start:row_end, col_start:col_end]
        inverse = lax.linalg.triangular_solve(diag_factor, identity, left_side=True, lower=True)
        solved = matmul(running[row_end:, col_start:col_end], inverse)
        running = running.at[row_end:, col_start:col_end].set(solved)
        running = running.at[row_end:, :col_start].add(-matmul(solved, saved_factor[row_start:row_end, :col_start]))
        diag_grad = jnp.tril(running[row_start:row_end, col_start:col_end]) - jnp.tril(inner_rows(solved, saved_factor[row_end:, col_start:col_end]))
        diag_adj = lower_half(matmul(matmul(inverse.T, lower_half(matmul(diag_factor.T, diag_grad))), inverse))
        running = running.at[row_start:row_end, col_start:col_end].set(diag_adj)
        symmetric = diag_adj + diag_adj.T
        running = running.at[row_start:row_end, :col_start].add(-(inner_rows(solved, saved_factor[row_end:, :col_start]) + matmul(symmetric, saved_factor[row_start:row_end, :col_start])))
    return running
```

```python
import jax
import jax.numpy as jnp
from jax import lax
from jax.experimental import pallas as pl
from jax.experimental.pallas import tpu as pltpu
from jax.sharding import PartitionSpec as P

NB = 512
NP = 3
MESH = pl.DeviceIdType.MESH
HI = lax.Precision.HIGHEST
MID = lax.Precision.HIGH
F32 = jnp.float32


def dot(a, b, precision=MID):
    return jnp.dot(a, b, precision=precision, preferred_element_type=F32)


def dot_t(a, b, precision=MID):
    return lax.dot_general(
        a, b, (((0,), (0,)), ((), ())), precision=precision, preferred_element_type=F32
    )


def place():
    row = lax.axis_index("row")
    col = lax.axis_index("col")
    return row // 4, row % 4, col // 2, col % 2


def remote(src, dst, send, recv, x, y, z, core):
    return pltpu.make_async_remote_copy(
        src_ref=src,
        dst_ref=dst,
        send_sem=send,
        recv_sem=recv,
        device_id=(x * 4 + y, z * 2 + core),
        device_id_type=MESH,
    )


def greet(devices):
    barrier = pltpu.get_barrier_semaphore()
    for x, y, z, core in devices:
        pl.semaphore_signal(
            barrier, inc=1, device_id=(x * 4 + y, z * 2 + core), device_id_type=MESH
        )
    pl.semaphore_wait(barrier, len(devices))


def plane_and_peer(x, y, z, core):
    out = []
    for dx in range(4):
        for dy in range(4):
            if dx or dy:
                out.append(((x + dx) % 4, (y + dy) % 4, z, core))
    return out + [(x, y, z, 1 - core)]


def spread_kernel(
    own, cot, strips, d6, d7, half, scat_s, scat_r, ag_s, ag_r, ex_s, ex_r, loc
):
    x, y, z, core = place()
    greet(plane_and_peer(x, y, z, core))
    half_copy = remote(
        cot.at[pl.ds(256 * (1 - core), 256)], half, ex_s.at[0], ex_r.at[0], x, y, z, 1 - core
    )
    half_copy.start()

    for p in range(NP):
        is_root = (x == 0) & (y == p)

        @pl.when(is_root)
        def _():
            here = pltpu.make_async_copy(
                own.at[pl.ds(x, 1), pl.ds(y, 1)],
                strips.at[p, pl.ds(x, 1), pl.ds(y, 1)],
                loc.at[0],
            )
            here.start()
            copies = []
            for d in range(1, 16):
                tx, ty = (x + d // 4) % 4, (y + d % 4) % 4
                copy = remote(
                    own.at[pl.ds(tx, 1), pl.ds(ty, 1)],
                    strips.at[p, pl.ds(tx, 1), pl.ds(ty, 1)],
                    scat_s.at[d],
                    scat_r.at[p],
                    tx, ty, z, core,
                )
                copy.start()
                copies.append(copy)
            here.wait()
            for copy in copies:
                copy.wait_send()

        @pl.when(jnp.logical_not(is_root))
        def _():
            remote(
                own.at[pl.ds(x, 1), pl.ds(y, 1)],
                strips.at[p, pl.ds(x, 1), pl.ds(y, 1)],
                scat_s.at[0],
                scat_r.at[p],
                x, y, z, 1 - core,
            ).wait_recv()

    left, right = pl.ds(0, NB), pl.ds(NB, NB)
    first = []
    for d in range(1, 4):
        tx, ty = (x + d) % 4, (y + d) % 4
        block = strips.at[:, pl.ds(x, 1), pl.ds(y, 1), :, left]
        first.append(remote(block, block, ag_s.at[0, d], ag_r.at[0, d], tx, y, z, core))
        block = strips.at[:, pl.ds(x, 1), pl.ds(y, 1), :, right]
        first.append(remote(block, block, ag_s.at[1, d], ag_r.at[1, d], x, ty, z, core))
    for copy in first:
        copy.start()
    for copy in first:
        copy.wait_recv()
    second = []
    for d in range(1, 4):
        tx, ty = (x + d) % 4, (y + d) % 4
        block = strips.at[:, :, pl.ds(y, 1), :, left]
        second.append(remote(block, block, ag_s.at[2, d], ag_r.at[2, d], x, ty, z, core))
        block = strips.at[:, pl.ds(x, 1), :, :, right]
        second.append(remote(block, block, ag_s.at[3, d], ag_r.at[3, d], tx, y, z, core))
    for copy in second:
        copy.start()
    for copy in second:
        copy.wait_recv()

    low = strips.at[:, :, :, :, right]
    high = strips
    send_low = remote(low, d6, ex_s.at[1], ex_r.at[1], x, y, z, 1 - core)
    send_high = remote(high, d7, ex_s.at[2], ex_r.at[2], x, y, z, 1 - core)

    @pl.when(core == 0)
    def _():
        send_low.start()
        here = pltpu.make_async_copy(low, d6, loc.at[1])
        here.start()
        here.wait()
        send_high.wait_recv()
        send_low.wait_send()

    @pl.when(core == 1)
    def _():
        send_high.start()
        here = pltpu.make_async_copy(high, d7, loc.at[1])
        here.start()
        here.wait()
        send_low.wait_recv()
        send_high.wait_send()

    for copy in first + second:
        copy.wait_send()
    half_copy.wait()


def spread(factor, cot):
    own = factor.reshape(4, 4, 32, 1024)
    vm = pl.BlockSpec(memory_space=pltpu.VMEM)
    dma = pltpu.SemaphoreType.DMA
    return pl.pallas_call(
        spread_kernel,
        out_shape=(
            jax.ShapeDtypeStruct((3, 4, 4, 32, 1024), F32),
            jax.ShapeDtypeStruct((3, 4, 4, 32, 512), F32),
            jax.ShapeDtypeStruct((3, 4, 4, 32, 1024), F32),
            jax.ShapeDtypeStruct((256, 1024), F32),
        ),
        in_specs=[vm, pl.BlockSpec(memory_space=pl.ANY)],
        out_specs=(vm, vm, vm, vm),
        scratch_shapes=[
            dma((16,)), dma((3,)), dma((4, 4)), dma((4, 4)), dma((3,)), dma((3,)), dma((2,)),
        ],
        compiler_params=pltpu.CompilerParams(
            collective_id=0, has_side_effects=True, vmem_limit_bytes=48 << 20
        ),
    )(own, cot)


CH = 4
CR = 128 // CH


def along_kernel(src, out, ring_s, ring_r, peer_s, peer_r):
    x, y, z, core = place()
    up, down = (z + 1) % 4, (z + 3) % 4
    greet([(x, y, up, core), (x, y, down, core), (x, y, z, 1 - core)])
    positions = (up, 3 - z)
    targets = (up, down)

    @pl.when(z == 3)
    def _():
        out[pl.ds(core, 1)] = src[...]

    def chunk(owner, way, step):
        return out.at[pl.ds(owner, 1), way, step]

    for step in range(CH):
        for way in range(2):
            pos, target = positions[way], targets[way]
            mine = chunk(core, way, step)
            send = remote(
                mine, mine, ring_s.at[way, step], ring_r.at[way, step], x, y, target, core
            )

            @pl.when(pos > 0)
            def _():
                send.wait_recv()

            @pl.when((z == 3) & (pos < 3))
            def _():
                remote(
                    src.at[:, way, step], mine,
                    ring_s.at[way, step], ring_r.at[way, step], x, y, target, core,
                ).start()

            @pl.when((z != 3) & (pos < 3))
            def _():
                send.start()

            @pl.when(z == 3)
            def _():
                remote(
                    src.at[:, way, step], mine,
                    peer_s.at[way, step], peer_r.at[way, step], x, y, z, 1 - core,
                ).start()

            @pl.when(z != 3)
            def _():
                remote(
                    mine, mine,
                    peer_s.at[way, step], peer_r.at[way, step], x, y, z, 1 - core,
                ).start()

    for step in range(CH):
        for way in range(2):
            pos, target = positions[way], targets[way]
            mine, other = chunk(core, way, step), chunk(1 - core, way, step)
            remote(
                mine, other, peer_s.at[way, step], peer_r.at[way, step], x, y, z, 1 - core
            ).wait()

            @pl.when(pos < 3)
            def _():
                remote(
                    mine, mine, ring_s.at[way, step], ring_r.at[way, step], x, y, target, core
                ).wait_send()


def along(half, collective_id):
    vm = pl.BlockSpec(memory_space=pltpu.VMEM)
    dma = pltpu.SemaphoreType.DMA
    out = pl.pallas_call(
        along_kernel,
        out_shape=jax.ShapeDtypeStruct((2, 2, CH, CR, 1536), F32),
        in_specs=[vm],
        out_specs=vm,
        scratch_shapes=[dma((2, CH)), dma((2, CH)), dma((2, CH)), dma((2, CH))],
        compiler_params=pltpu.CompilerParams(
            collective_id=collective_id, has_side_effects=True, vmem_limit_bytes=16 << 20
        ),
    )(half.reshape(1, 2, CH, CR, 1536))
    return out.reshape(512, 1536)


def gather_kernel(
    part, total, t6, t7, r1a, r1b, a1a, a1b, r2, a2,
    one_s, one_r, two_s, two_r, g_s, g_r, ex_s, ex_r, loc,
):
    x, y, z, core = place()
    greet(plane_and_peer(x, y, z, core))
    left, right = pl.ds(0, NB), pl.ds(NB, NB)
    cols = (left, right)
    one, two = [], []
    for d in range(1, 4):
        tx, ty = (x + d) % 4, (y + d) % 4
        one.append((
            remote(
                part.at[:, pl.ds(tx, 1), :, :, left], r1a.at[d - 1],
                one_s.at[0, d], one_r.at[0, d], tx, y, z, core,
            ),
            remote(
                part.at[:, :, pl.ds(ty, 1), :, right], r1b.at[d - 1],
                one_s.at[1, d], one_r.at[1, d], x, ty, z, core,
            ),
        ))
        two.append((
            remote(
                a1a.at[:, :, pl.ds(ty, 1)], r2.at[0, d - 1],
                two_s.at[0, d], two_r.at[0, d], x, ty, z, core,
            ),
            remote(
                a1b.at[:, pl.ds(tx, 1)], r2.at[1, d - 1],
                two_s.at[1, d], two_r.at[1, d], tx, y, z, core,
            ),
        ))
    for pair in one:
        for copy in pair:
            copy.start()
    for pair in one:
        pair[0].wait_recv()
    a1a[...] = (part[:, pl.ds(x, 1), :, :, left] + r1a[0]) + (r1a[1] + r1a[2])
    for pair in two:
        pair[0].start()
    for pair in one:
        pair[1].wait_recv()
    a1b[...] = (part[:, :, pl.ds(y, 1), :, right] + r1b[0]) + (r1b[1] + r1b[2])
    for pair in two:
        pair[1].start()
    for pair in two:
        pair[0].wait_recv()
    a2[0] = (a1a[:, :, pl.ds(y, 1)] + r2[0, 0]) + (r2[0, 1] + r2[0, 2])
    for pair in two:
        pair[1].wait_recv()
    a2[1] = (a1b[:, pl.ds(x, 1)] + r2[1, 0]) + (r2[1, 1] + r2[1, 2])

    def wanted(q, root, half):
        if q == root:
            return None
        if half == 0:
            if q == 0:
                return False
            return (z == 3) & (core == 1)
        if q == 2:
            return z == 3
        return (z == 3) & (core == 0)

    def under(flag, other, body):
        if flag is None:
            pl.when(other)(body)
        else:
            pl.when(flag & other)(body)

    for root in range(NP):
        at_root = (x == 0) & (y == root)
        for q in range(NP):
            for h in range(2):
                flag = wanted(q, root, h)
                if flag is False:
                    continue
                slot = total.at[q, pl.ds(x, 1), pl.ds(y, 1), :, cols[h]]

                def send():
                    remote(
                        a2.at[h, q], slot, g_s.at[root, q, h], g_r.at[q, h, x * 4 + y],
                        0, root, z, core,
                    ).start()

                def keep():
                    pltpu.make_async_copy(a2.at[h, q], slot, g_s.at[root, q, h]).start()

                under(flag, jnp.logical_not(at_root), send)
                under(flag, at_root, keep)
    for root in range(NP):
        at_root = (x == 0) & (y == root)
        for q in range(NP):
            for h in range(2):
                flag = wanted(q, root, h)
                if flag is False:
                    continue

                def sent():
                    slot = total.at[q, pl.ds(x, 1), pl.ds(y, 1), :, cols[h]]
                    remote(
                        a2.at[h, q], slot, g_s.at[root, q, h], g_r.at[q, h, x * 4 + y],
                        0, root, z, core,
                    ).wait_send()

                def kept():
                    slot = total.at[q, pl.ds(x, 1), pl.ds(y, 1), :, cols[h]]
                    pltpu.make_async_copy(a2.at[h, q], slot, g_s.at[root, q, h]).wait()
                    for d in range(1, 16):
                        sx, sy = (x + d // 4) % 4, (y + d % 4) % 4
                        slot = total.at[q, pl.ds(sx, 1), pl.ds(sy, 1), :, cols[h]]
                        remote(
                            a2.at[h, q], slot, g_s.at[root, q, h], g_r.at[q, h, sx * 4 + sy],
                            0, root, z, 1 - core,
                        ).wait_recv()

                under(flag, jnp.logical_not(at_root), sent)
                under(flag, at_root, kept)

    top = (x == 0) & (y < NP) & (z == 3)
    low = total.at[:, :, :, :, right]
    high = total.at[pl.ds(1, 2)]
    send_low = remote(low, t6, ex_s.at[0], ex_r.at[0], x, y, z, 1 - core)
    send_high = remote(high, t7, ex_s.at[1], ex_r.at[1], x, y, z, 1 - core)

    @pl.when(top & (core == 0))
    def _():
        send_low.start()
        here = pltpu.make_async_copy(low, t6, loc.at[0])
        here.start()
        here.wait()
        send_high.wait_recv()
        send_low.wait_send()

    @pl.when(top & (core == 1))
    def _():
        send_high.start()
        here = pltpu.make_async_copy(high, t7, loc.at[0])
        here.start()
        here.wait()
        send_low.wait_recv()
        send_high.wait_send()

    for pair in one + two:
        for copy in pair:
            copy.wait_send()


def gather(part):
    vm = pl.BlockSpec(memory_space=pltpu.VMEM)
    dma = pltpu.SemaphoreType.DMA
    return pl.pallas_call(
        gather_kernel,
        out_shape=(
            jax.ShapeDtypeStruct((3, 4, 4, 32, 1024), F32),
            jax.ShapeDtypeStruct((3, 4, 4, 32, 512), F32),
            jax.ShapeDtypeStruct((2, 4, 4, 32, 1024), F32),
        ),
        in_specs=[vm],
        out_specs=(vm, vm, vm),
        scratch_shapes=[
            pltpu.VMEM((3, 3, 1, 4, 32, 512), F32),
            pltpu.VMEM((3, 3, 4, 1, 32, 512), F32),
            pltpu.VMEM((3, 1, 4, 32, 512), F32),
            pltpu.VMEM((3, 4, 1, 32, 512), F32),
            pltpu.VMEM((2, 3, 3, 1, 1, 32, 512), F32),
            pltpu.VMEM((2, 3, 1, 1, 32, 512), F32),
            dma((2, 4)), dma((2, 4)), dma((2, 4)), dma((2, 4)),
            dma((3, 3, 2)), dma((3, 2, 16)), dma((2,)), dma((2,)), dma((1,)),
        ],
        compiler_params=pltpu.CompilerParams(
            collective_id=2, has_side_effects=True, vmem_limit_bytes=48 << 20
        ),
    )(part.reshape(3, 4, 4, 32, 1024))


BS = 128


def invert_kernel(d_ref, o_ref):
    rows = lax.broadcasted_iota(jnp.int32, (BS, BS), 0)
    cols = lax.broadcasted_iota(jnp.int32, (BS, BS), 1)
    diag = rows == cols
    for block in range(NP * (NB // BS)):
        which, at = block // (NB // BS), pl.ds(block % (NB // BS) * BS, BS)
        base = d_ref[which, at, at]
        scale = jnp.sum(jnp.where(diag, base, 0.0), axis=1, keepdims=True)
        o_ref[which, at, at] = jnp.where(diag, 1.0 / scale, 0.0)
    size = 1
    while size < BS:
        pick = (rows // (2 * size) == cols // (2 * size)) & (
            (rows // size) % 2 > (cols // size) % 2
        )
        for block in range(NP * (NB // BS)):
            which, at = block // (NB // BS), pl.ds(block % (NB // BS) * BS, BS)
            have = o_ref[which, at, at]
            below = jnp.where(pick, d_ref[which, at, at], 0.0)
            o_ref[which, at, at] = have - dot(dot(have, below, HI), have, HI)
        size *= 2
    while size < NB:
        for which in range(NP):
            for base in range(0, NB, 2 * size):
                up, down = pl.ds(base, size), pl.ds(base + size, size)
                corner = dot(
                    dot(o_ref[which, down, down], d_ref[which, down, up], HI),
                    o_ref[which, up, up], HI,
                )
                o_ref[which, down, up] = -corner
                o_ref[which, up, down] = jnp.zeros((size, size), F32)
        size *= 2


def invert(blocks):
    vm = pl.BlockSpec(memory_space=pltpu.VMEM)
    return pl.pallas_call(
        invert_kernel,
        out_shape=jax.ShapeDtypeStruct((NP, NB, NB), F32),
        in_specs=[vm],
        out_specs=vm,
        compiler_params=pltpu.CompilerParams(vmem_limit_bytes=16 << 20),
    )(blocks)


def lower_half(matrix):
    rows = lax.broadcasted_iota(jnp.int32, (NB, NB), 0)
    cols = lax.broadcasted_iota(jnp.int32, (NB, NB), 1)
    return jnp.where(rows > cols, matrix, jnp.where(rows == cols, 0.5 * matrix, 0.0))


def adjoint_of(factor, inverse, cot):
    inner = lower_half(dot_t(factor, jnp.tril(cot)))
    return lower_half(dot(dot_t(inverse, inner), inverse))


def chain(l, inv, t):
    a2 = adjoint_of(l[22], inv[2], t[22])
    y2 = a2 + a2.T
    t21 = t[21] - dot(y2, l[21])
    t20 = t[20] - dot(y2, l[20])
    s21 = dot(t21, inv[1])
    t11 = t[11] - dot_t(s21, l[21])
    t10 = t[10] - dot_t(s21, l[20])
    a1 = adjoint_of(l[11], inv[1], t11)
    y1 = a1 + a1.T
    t10 = t10 - dot(y1, l[10])
    t20 = t20 - dot(s21, l[10])
    s20 = dot(t20, inv[0])
    s10 = dot(t10, inv[0])
    t00 = t[0] - dot_t(s20, l[20]) - dot_t(s10, l[10])
    a0 = adjoint_of(l[0], inv[0], t00)
    y0 = a0 + a0.T
    return (a0, a1, a2), (y0, y1, y2), s10, s20, s21


def shards(factor, cot):
    row = lax.axis_index("row")
    col = lax.axis_index("col")
    core = col % 2
    strips, d6, d7, other_half = spread(factor, cot)
    d6 = d6.reshape(3, NB, NB)
    d7 = d7.reshape(3, NB, 1024)
    l = {
        0: d6[0], 10: d6[1], 20: d6[2],
        11: d7[1, :, :NB], 21: d7[2, :, :NB], 22: d7[2, :, NB:],
    }
    inv = invert(jnp.stack([l[0], l[11], l[22]]))
    my_half = lax.dynamic_slice(cot, (core * 256, 0), (256, 1024))
    g6 = jnp.where(core == 0, my_half, other_half)
    g7 = jnp.where(core == 0, other_half, my_half)
    s2 = dot(g7[:, NB:], inv[2])
    s1 = dot(g7[:, :NB] - dot(s2, l[21]), inv[1])
    s0 = dot(g6[:, NB:] - dot(s2, l[20]) - dot(s1, l[10]), inv[0])
    solved = along(jnp.concatenate([s0, s1, s2], axis=1), 1)
    lower_rows = row >= NP
    strips = strips.reshape(3 * NB, 1024)
    part = jnp.where(lower_rows, -dot_t(solved, factor), 0.0).reshape(3, NB, 1024)
    which = lax.broadcasted_iota(jnp.int32, (3, 1, 1), 0)
    part = jnp.where(which == row, cot[None], part)
    total, t6, t7 = gather(part)
    total = total.reshape(3, NB, 1024)
    t6 = t6.reshape(3, NB, NB)
    t7 = t7.reshape(2, NB, 1024)
    t = {
        0: t6[0], 10: t6[1], 20: t6[2],
        11: t7[0, :, :NB], 21: t7[1, :, :NB], 22: t7[1, :, NB:],
    }
    a, sym, s10, s20, s21 = chain(l, inv, t)
    pick = row
    rows0 = jnp.concatenate([sym[0], s10.T, s20.T], axis=1)
    rows1 = jnp.concatenate([s10, sym[1], s21.T], axis=1)
    rows2 = jnp.concatenate([s20, s21, sym[2]], axis=1)
    mixed = jnp.where(pick == 0, rows0, jnp.where(pick == 1, rows1, rows2))
    mixed_half = lax.dynamic_slice(mixed, (core * 256, 0), (256, 1536))
    mixed = along(mixed_half, 3)
    factor_rows = jnp.where(lower_rows, solved, mixed)
    own_total = lax.dynamic_index_in_dim(total, jnp.minimum(row, 2), 0, keepdims=False)
    start = jnp.where(lower_rows, cot, own_total)
    out = start - dot(factor_rows, strips)
    cut = cot[:, :NB], cot[:, NB:]
    last6 = jnp.where(
        lower_rows, solved[:, :NB],
        jnp.where(pick == 0, a[0], jnp.where(pick == 1, s10, s20)),
    )
    left7 = jnp.where(
        lower_rows, solved[:, NB:1024],
        jnp.where(pick == 0, cut[0], jnp.where(pick == 1, a[1], s21)),
    )
    right7 = jnp.where(
        lower_rows, solved[:, 1024:],
        jnp.where(pick == 2, a[2], cut[1]),
    )
    left = jnp.where(col == 7, left7, out[:, :NB])
    right = jnp.where(col == 7, right7, jnp.where(col == 6, last6, out[:, NB:]))
    return jnp.concatenate([left, right], axis=1)


def solution(mesh):
    placed = (P("row", "col"), P("row", "col"))
    return jax.shard_map(
        shards, mesh=mesh, in_specs=placed, out_specs=P("row", "col"), check_vma=False
    )
```

```python
import jax
import jax.numpy as jnp
from jax import lax
from jax.experimental import pallas as pl
from jax.experimental.pallas import tpu as pltpu
from jax.sharding import PartitionSpec as P

NB = 512
NP = 3
MESH = pl.DeviceIdType.MESH
HI = lax.Precision.HIGHEST
MID = lax.Precision.HIGH
F32 = jnp.float32


def dot(a, b, precision=MID):
    return jnp.dot(a, b, precision=precision, preferred_element_type=F32)


def dot_t(a, b, precision=MID):
    return lax.dot_general(
        a, b, (((0,), (0,)), ((), ())), precision=precision, preferred_element_type=F32
    )


def place():
    row = lax.axis_index("row")
    col = lax.axis_index("col")
    return row // 4, row % 4, col // 2, col % 2


def remote(src, dst, send, recv, x, y, z, core):
    return pltpu.make_async_remote_copy(
        src_ref=src,
        dst_ref=dst,
        send_sem=send,
        recv_sem=recv,
        device_id=(x * 4 + y, z * 2 + core),
        device_id_type=MESH,
    )


def greet(devices):
    barrier = pltpu.get_barrier_semaphore()
    for x, y, z, core in devices:
        pl.semaphore_signal(
            barrier, inc=1, device_id=(x * 4 + y, z * 2 + core), device_id_type=MESH
        )
    pl.semaphore_wait(barrier, len(devices))


def plane_and_peer(x, y, z, core):
    out = []
    for dx in range(4):
        for dy in range(4):
            if dx or dy:
                out.append(((x + dx) % 4, (y + dy) % 4, z, core))
    return out + [(x, y, z, 1 - core)]


def spread_kernel(
    own, cot, strips, d6, d7, half, scat_s, scat_r, ag_s, ag_r, ex_s, ex_r, loc
):
    x, y, z, core = place()
    greet(plane_and_peer(x, y, z, core))
    half_copy = remote(
        cot.at[pl.ds(256 * (1 - core), 256)], half, ex_s.at[0], ex_r.at[0], x, y, z, 1 - core
    )
    half_copy.start()

    for p in range(NP):
        is_root = (x == 0) & (y == p)

        @pl.when(is_root)
        def _():
            here = pltpu.make_async_copy(
                own.at[pl.ds(x, 1), pl.ds(y, 1)],
                strips.at[p, pl.ds(x, 1), pl.ds(y, 1)],
                loc.at[0],
            )
            here.start()
            copies = []
            for d in range(1, 16):
                tx, ty = (x + d // 4) % 4, (y + d % 4) % 4
                copy = remote(
                    own.at[pl.ds(tx, 1), pl.ds(ty, 1)],
                    strips.at[p, pl.ds(tx, 1), pl.ds(ty, 1)],
                    scat_s.at[d],
                    scat_r.at[p],
                    tx, ty, z, core,
                )
                copy.start()
                copies.append(copy)
            here.wait()
            for copy in copies:
                copy.wait_send()

        @pl.when(jnp.logical_not(is_root))
        def _():
            remote(
                own.at[pl.ds(x, 1), pl.ds(y, 1)],
                strips.at[p, pl.ds(x, 1), pl.ds(y, 1)],
                scat_s.at[0],
                scat_r.at[p],
                x, y, z, 1 - core,
            ).wait_recv()

    left, right = pl.ds(0, NB), pl.ds(NB, NB)
    first = []
    for d in range(1, 4):
        tx, ty = (x + d) % 4, (y + d) % 4
        block = strips.at[:, pl.ds(x, 1), pl.ds(y, 1), :, left]
        first.append(remote(block, block, ag_s.at[0, d], ag_r.at[0, d], tx, y, z, core))
        block = strips.at[:, pl.ds(x, 1), pl.ds(y, 1), :, right]
        first.append(remote(block, block, ag_s.at[1, d], ag_r.at[1, d], x, ty, z, core))
    for copy in first:
        copy.start()
    for copy in first:
        copy.wait_recv()
    second = []
    for d in range(1, 4):
        tx, ty = (x + d) % 4, (y + d) % 4
        block = strips.at[:, :, pl.ds(y, 1), :, left]
        second.append(remote(block, block, ag_s.at[2, d], ag_r.at[2, d], x, ty, z, core))
        block = strips.at[:, pl.ds(x, 1), :, :, right]
        second.append(remote(block, block, ag_s.at[3, d], ag_r.at[3, d], tx, y, z, core))
    for copy in second:
        copy.start()
    for copy in second:
        copy.wait_recv()

    low = strips.at[:, :, :, :, right]
    high = strips
    send_low = remote(low, d6, ex_s.at[1], ex_r.at[1], x, y, z, 1 - core)
    send_high = remote(high, d7, ex_s.at[2], ex_r.at[2], x, y, z, 1 - core)

    @pl.when(core == 0)
    def _():
        send_low.start()
        here = pltpu.make_async_copy(low, d6, loc.at[1])
        here.start()
        here.wait()
        send_high.wait_recv()
        send_low.wait_send()

    @pl.when(core == 1)
    def _():
        send_high.start()
        here = pltpu.make_async_copy(high, d7, loc.at[1])
        here.start()
        here.wait()
        send_low.wait_recv()
        send_high.wait_send()

    for copy in first + second:
        copy.wait_send()
    half_copy.wait()


def spread(factor, cot):
    own = factor.reshape(4, 4, 32, 1024)
    vm = pl.BlockSpec(memory_space=pltpu.VMEM)
    dma = pltpu.SemaphoreType.DMA
    return pl.pallas_call(
        spread_kernel,
        out_shape=(
            jax.ShapeDtypeStruct((3, 4, 4, 32, 1024), F32),
            jax.ShapeDtypeStruct((3, 4, 4, 32, 512), F32),
            jax.ShapeDtypeStruct((3, 4, 4, 32, 1024), F32),
            jax.ShapeDtypeStruct((256, 1024), F32),
        ),
        in_specs=[vm, pl.BlockSpec(memory_space=pl.ANY)],
        out_specs=(vm, vm, vm, vm),
        scratch_shapes=[
            dma((16,)), dma((3,)), dma((4, 4)), dma((4, 4)), dma((3,)), dma((3,)), dma((2,)),
        ],
        compiler_params=pltpu.CompilerParams(
            collective_id=0, has_side_effects=True, vmem_limit_bytes=48 << 20
        ),
    )(own, cot)


CH = 8
CR = 128 // CH


def along_kernel(src, out, ring_s, ring_r, peer_s, peer_r):
    x, y, z, core = place()
    up, down = (z + 1) % 4, (z + 3) % 4
    greet([(x, y, up, core), (x, y, down, core), (x, y, z, 1 - core)])
    positions = (up, 3 - z)
    targets = (up, down)

    @pl.when(z == 3)
    def _():
        out[pl.ds(core, 1)] = src[...]

    def chunk(owner, way, step):
        return out.at[pl.ds(owner, 1), way, step]

    def ring(way, step, block):
        mine = chunk(core, way, step)
        return remote(
            block, mine, ring_s.at[way, step], ring_r.at[way, step], x, y, targets[way], core
        )

    def across(way, step, block):
        mine = chunk(core, way, step)
        return remote(
            block, mine, peer_s.at[way, step], peer_r.at[way, step], x, y, z, 1 - core
        )

    @pl.when(z == 3)
    def _():
        for step in range(CH):
            for way in range(2):
                ring(way, step, src.at[:, way, step]).start()
        for step in range(CH):
            for way in range(2):
                across(way, step, src.at[:, way, step]).start()

    for tick in range(CH + 2):
        for way in range(2):
            for pos in range(1, 4):
                step = tick - (pos - 1)
                if not 0 <= step < CH:
                    continue

                @pl.when(positions[way] == pos)
                def _():
                    mine = chunk(core, way, step)
                    ring(way, step, mine).wait_recv()
                    if pos < 3:
                        ring(way, step, mine).start()
                    across(way, step, mine).start()

    for step in range(CH):
        for way in range(2):
            pos, target = positions[way], targets[way]
            mine, other = chunk(core, way, step), chunk(1 - core, way, step)
            remote(
                mine, other, peer_s.at[way, step], peer_r.at[way, step], x, y, z, 1 - core
            ).wait()

            @pl.when(pos < 3)
            def _():
                remote(
                    mine, mine, ring_s.at[way, step], ring_r.at[way, step], x, y, target, core
                ).wait_send()


def along(half, collective_id):
    vm = pl.BlockSpec(memory_space=pltpu.VMEM)
    dma = pltpu.SemaphoreType.DMA
    out = pl.pallas_call(
        along_kernel,
        out_shape=jax.ShapeDtypeStruct((2, 2, CH, CR, 1536), F32),
        in_specs=[vm],
        out_specs=vm,
        scratch_shapes=[dma((2, CH)), dma((2, CH)), dma((2, CH)), dma((2, CH))],
        compiler_params=pltpu.CompilerParams(
            collective_id=collective_id, has_side_effects=True, vmem_limit_bytes=16 << 20
        ),
    )(half.reshape(1, 2, CH, CR, 1536))
    return out.reshape(512, 1536)


def gather_kernel(
    part, total, t6, t7, r1a, r1b, a1a, a1b, r2, a2,
    one_s, one_r, two_s, two_r, g_s, g_r, ex_s, ex_r, loc,
):
    x, y, z, core = place()
    greet(plane_and_peer(x, y, z, core))
    left, right = pl.ds(0, NB), pl.ds(NB, NB)
    cols = (left, right)
    one, two = [], []
    for d in range(1, 4):
        tx, ty = (x + d) % 4, (y + d) % 4
        one.append((
            remote(
                part.at[:, pl.ds(tx, 1), :, :, left], r1a.at[d - 1],
                one_s.at[0, d], one_r.at[0, d], tx, y, z, core,
            ),
            remote(
                part.at[:, :, pl.ds(ty, 1), :, right], r1b.at[d - 1],
                one_s.at[1, d], one_r.at[1, d], x, ty, z, core,
            ),
        ))
        two.append((
            remote(
                a1a.at[:, :, pl.ds(ty, 1)], r2.at[0, d - 1],
                two_s.at[0, d], two_r.at[0, d], x, ty, z, core,
            ),
            remote(
                a1b.at[:, pl.ds(tx, 1)], r2.at[1, d - 1],
                two_s.at[1, d], two_r.at[1, d], tx, y, z, core,
            ),
        ))
    for pair in one:
        for copy in pair:
            copy.start()
    for pair in one:
        pair[0].wait_recv()
    a1a[...] = (part[:, pl.ds(x, 1), :, :, left] + r1a[0]) + (r1a[1] + r1a[2])
    for pair in two:
        pair[0].start()
    for pair in one:
        pair[1].wait_recv()
    a1b[...] = (part[:, :, pl.ds(y, 1), :, right] + r1b[0]) + (r1b[1] + r1b[2])
    for pair in two:
        pair[1].start()
    for pair in two:
        pair[0].wait_recv()
    a2[0] = (a1a[:, :, pl.ds(y, 1)] + r2[0, 0]) + (r2[0, 1] + r2[0, 2])
    for pair in two:
        pair[1].wait_recv()
    a2[1] = (a1b[:, pl.ds(x, 1)] + r2[1, 0]) + (r2[1, 1] + r2[1, 2])

    def wanted(q, root, half):
        if q == root:
            return None
        if half == 0:
            if q == 0:
                return False
            return (z == 3) & (core == 1)
        if q == 2:
            return z == 3
        return (z == 3) & (core == 0)

    def under(flag, other, body):
        if flag is None:
            pl.when(other)(body)
        else:
            pl.when(flag & other)(body)

    for root in range(NP):
        at_root = (x == 0) & (y == root)
        for q in range(NP):
            for h in range(2):
                flag = wanted(q, root, h)
                if flag is False:
                    continue
                slot = total.at[q, pl.ds(x, 1), pl.ds(y, 1), :, cols[h]]

                def send():
                    remote(
                        a2.at[h, q], slot, g_s.at[root, q, h], g_r.at[q, h, x * 4 + y],
                        0, root, z, core,
                    ).start()

                def keep():
                    pltpu.make_async_copy(a2.at[h, q], slot, g_s.at[root, q, h]).start()

                under(flag, jnp.logical_not(at_root), send)
                under(flag, at_root, keep)
    for root in range(NP):
        at_root = (x == 0) & (y == root)
        for q in range(NP):
            for h in range(2):
                flag = wanted(q, root, h)
                if flag is False:
                    continue

                def sent():
                    slot = total.at[q, pl.ds(x, 1), pl.ds(y, 1), :, cols[h]]
                    remote(
                        a2.at[h, q], slot, g_s.at[root, q, h], g_r.at[q, h, x * 4 + y],
                        0, root, z, core,
                    ).wait_send()

                def kept():
                    slot = total.at[q, pl.ds(x, 1), pl.ds(y, 1), :, cols[h]]
                    pltpu.make_async_copy(a2.at[h, q], slot, g_s.at[root, q, h]).wait()
                    for d in range(1, 16):
                        sx, sy = (x + d // 4) % 4, (y + d % 4) % 4
                        slot = total.at[q, pl.ds(sx, 1), pl.ds(sy, 1), :, cols[h]]
                        remote(
                            a2.at[h, q], slot, g_s.at[root, q, h], g_r.at[q, h, sx * 4 + sy],
                            0, root, z, 1 - core,
                        ).wait_recv()

                under(flag, jnp.logical_not(at_root), sent)
                under(flag, at_root, kept)

    top = (x == 0) & (y < NP) & (z == 3)
    low = total.at[:, :, :, :, right]
    high = total.at[pl.ds(1, 2)]
    send_low = remote(low, t6, ex_s.at[0], ex_r.at[0], x, y, z, 1 - core)
    send_high = remote(high, t7, ex_s.at[1], ex_r.at[1], x, y, z, 1 - core)

    @pl.when(top & (core == 0))
    def _():
        send_low.start()
        here = pltpu.make_async_copy(low, t6, loc.at[0])
        here.start()
        here.wait()
        send_high.wait_recv()
        send_low.wait_send()

    @pl.when(top & (core == 1))
    def _():
        send_high.start()
        here = pltpu.make_async_copy(high, t7, loc.at[0])
        here.start()
        here.wait()
        send_low.wait_recv()
        send_high.wait_send()

    for pair in one + two:
        for copy in pair:
            copy.wait_send()


def gather(part):
    vm = pl.BlockSpec(memory_space=pltpu.VMEM)
    dma = pltpu.SemaphoreType.DMA
    return pl.pallas_call(
        gather_kernel,
        out_shape=(
            jax.ShapeDtypeStruct((3, 4, 4, 32, 1024), F32),
            jax.ShapeDtypeStruct((3, 4, 4, 32, 512), F32),
            jax.ShapeDtypeStruct((2, 4, 4, 32, 1024), F32),
        ),
        in_specs=[vm],
        out_specs=(vm, vm, vm),
        scratch_shapes=[
            pltpu.VMEM((3, 3, 1, 4, 32, 512), F32),
            pltpu.VMEM((3, 3, 4, 1, 32, 512), F32),
            pltpu.VMEM((3, 1, 4, 32, 512), F32),
            pltpu.VMEM((3, 4, 1, 32, 512), F32),
            pltpu.VMEM((2, 3, 3, 1, 1, 32, 512), F32),
            pltpu.VMEM((2, 3, 1, 1, 32, 512), F32),
            dma((2, 4)), dma((2, 4)), dma((2, 4)), dma((2, 4)),
            dma((3, 3, 2)), dma((3, 2, 16)), dma((2,)), dma((2,)), dma((1,)),
        ],
        compiler_params=pltpu.CompilerParams(
            collective_id=2, has_side_effects=True, vmem_limit_bytes=48 << 20
        ),
    )(part.reshape(3, 4, 4, 32, 1024))


BS = 128


def invert_kernel(d_ref, o_ref):
    rows = lax.broadcasted_iota(jnp.int32, (BS, BS), 0)
    cols = lax.broadcasted_iota(jnp.int32, (BS, BS), 1)
    diag = rows == cols
    for block in range(NP * (NB // BS)):
        which, at = block // (NB // BS), pl.ds(block % (NB // BS) * BS, BS)
        base = d_ref[which, at, at]
        scale = jnp.sum(jnp.where(diag, base, 0.0), axis=1, keepdims=True)
        o_ref[which, at, at] = jnp.where(diag, 1.0 / scale, 0.0)
    size = 1
    while size < BS:
        pick = (rows // (2 * size) == cols // (2 * size)) & (
            (rows // size) % 2 > (cols // size) % 2
        )
        for block in range(NP * (NB // BS)):
            which, at = block // (NB // BS), pl.ds(block % (NB // BS) * BS, BS)
            have = o_ref[which, at, at]
            below = jnp.where(pick, d_ref[which, at, at], 0.0)
            o_ref[which, at, at] = have - dot(dot(have, below, HI), have, HI)
        size *= 2
    while size < NB:
        for which in range(NP):
            for base in range(0, NB, 2 * size):
                up, down = pl.ds(base, size), pl.ds(base + size, size)
                corner = dot(
                    dot(o_ref[which, down, down], d_ref[which, down, up], HI),
                    o_ref[which, up, up], HI,
                )
                o_ref[which, down, up] = -corner
                o_ref[which, up, down] = jnp.zeros((size, size), F32)
        size *= 2


def invert(blocks):
    vm = pl.BlockSpec(memory_space=pltpu.VMEM)
    return pl.pallas_call(
        invert_kernel,
        out_shape=jax.ShapeDtypeStruct((NP, NB, NB), F32),
        in_specs=[vm],
        out_specs=vm,
        compiler_params=pltpu.CompilerParams(vmem_limit_bytes=16 << 20),
    )(blocks)


def lower_half(matrix):
    rows = lax.broadcasted_iota(jnp.int32, (NB, NB), 0)
    cols = lax.broadcasted_iota(jnp.int32, (NB, NB), 1)
    return jnp.where(rows > cols, matrix, jnp.where(rows == cols, 0.5 * matrix, 0.0))


def adjoint_of(factor, inverse, cot):
    inner = lower_half(dot_t(factor, jnp.tril(cot)))
    return lower_half(dot(dot_t(inverse, inner), inverse))


def chain(l, inv, t):
    a2 = adjoint_of(l[22], inv[2], t[22])
    y2 = a2 + a2.T
    t21 = t[21] - dot(y2, l[21])
    t20 = t[20] - dot(y2, l[20])
    s21 = dot(t21, inv[1])
    t11 = t[11] - dot_t(s21, l[21])
    t10 = t[10] - dot_t(s21, l[20])
    a1 = adjoint_of(l[11], inv[1], t11)
    y1 = a1 + a1.T
    t10 = t10 - dot(y1, l[10])
    t20 = t20 - dot(s21, l[10])
    s20 = dot(t20, inv[0])
    s10 = dot(t10, inv[0])
    t00 = t[0] - dot_t(s20, l[20]) - dot_t(s10, l[10])
    a0 = adjoint_of(l[0], inv[0], t00)
    y0 = a0 + a0.T
    return (a0, a1, a2), (y0, y1, y2), s10, s20, s21


def shards(factor, cot):
    row = lax.axis_index("row")
    col = lax.axis_index("col")
    core = col % 2
    strips, d6, d7, other_half = spread(factor, cot)
    d6 = d6.reshape(3, NB, NB)
    d7 = d7.reshape(3, NB, 1024)
    l = {
        0: d6[0], 10: d6[1], 20: d6[2],
        11: d7[1, :, :NB], 21: d7[2, :, :NB], 22: d7[2, :, NB:],
    }
    inv = invert(jnp.stack([l[0], l[11], l[22]]))
    my_half = lax.dynamic_slice(cot, (core * 256, 0), (256, 1024))
    g6 = jnp.where(core == 0, my_half, other_half)
    g7 = jnp.where(core == 0, other_half, my_half)
    s2 = dot(g7[:, NB:], inv[2])
    s1 = dot(g7[:, :NB] - dot(s2, l[21]), inv[1])
    s0 = dot(g6[:, NB:] - dot(s2, l[20]) - dot(s1, l[10]), inv[0])
    solved = along(jnp.concatenate([s0, s1, s2], axis=1), 1)
    lower_rows = row >= NP
    strips = strips.reshape(3 * NB, 1024)
    part = jnp.where(lower_rows, -dot_t(solved, factor), 0.0).reshape(3, NB, 1024)
    which = lax.broadcasted_iota(jnp.int32, (3, 1, 1), 0)
    part = jnp.where(which == row, cot[None], part)
    total, t6, t7 = gather(part)
    total = total.reshape(3, NB, 1024)
    t6 = t6.reshape(3, NB, NB)
    t7 = t7.reshape(2, NB, 1024)
    t = {
        0: t6[0], 10: t6[1], 20: t6[2],
        11: t7[0, :, :NB], 21: t7[1, :, :NB], 22: t7[1, :, NB:],
    }
    a, sym, s10, s20, s21 = chain(l, inv, t)
    pick = row
    rows0 = jnp.concatenate([sym[0], s10.T, s20.T], axis=1)
    rows1 = jnp.concatenate([s10, sym[1], s21.T], axis=1)
    rows2 = jnp.concatenate([s20, s21, sym[2]], axis=1)
    mixed = jnp.where(pick == 0, rows0, jnp.where(pick == 1, rows1, rows2))
    mixed_half = lax.dynamic_slice(mixed, (core * 256, 0), (256, 1536))
    mixed = along(mixed_half, 3)
    factor_rows = jnp.where(lower_rows, solved, mixed)
    own_total = lax.dynamic_index_in_dim(total, jnp.minimum(row, 2), 0, keepdims=False)
    start = jnp.where(lower_rows, cot, own_total)
    out = start - dot(factor_rows, strips)
    cut = cot[:, :NB], cot[:, NB:]
    last6 = jnp.where(
        lower_rows, solved[:, :NB],
        jnp.where(pick == 0, a[0], jnp.where(pick == 1, s10, s20)),
    )
    left7 = jnp.where(
        lower_rows, solved[:, NB:1024],
        jnp.where(pick == 0, cut[0], jnp.where(pick == 1, a[1], s21)),
    )
    right7 = jnp.where(
        lower_rows, solved[:, 1024:],
        jnp.where(pick == 2, a[2], cut[1]),
    )
    left = jnp.where(col == 7, left7, out[:, :NB])
    right = jnp.where(col == 7, right7, jnp.where(col == 6, last6, out[:, NB:]))
    return jnp.concatenate([left, right], axis=1)


def solution(mesh):
    placed = (P("row", "col"), P("row", "col"))
    return jax.shard_map(
        shards, mesh=mesh, in_specs=placed, out_specs=P("row", "col"), check_vma=False
    )
```

```python
import jax
import jax.numpy as jnp
from jax import lax
from jax.experimental import pallas as pl
from jax.experimental.pallas import tpu as pltpu
from jax.sharding import PartitionSpec as P

NB = 512
NP = 3
MESH = pl.DeviceIdType.MESH
HI = lax.Precision.HIGHEST
MID = lax.Precision.HIGH
F32 = jnp.float32


def dot(a, b, precision=MID):
    return jnp.dot(a, b, precision=precision, preferred_element_type=F32)


def dot_t(a, b, precision=MID):
    return lax.dot_general(
        a, b, (((0,), (0,)), ((), ())), precision=precision, preferred_element_type=F32
    )


def place():
    row = lax.axis_index("row")
    col = lax.axis_index("col")
    return row // 4, row % 4, col // 2, col % 2


def remote(src, dst, send, recv, x, y, z, core):
    return pltpu.make_async_remote_copy(
        src_ref=src,
        dst_ref=dst,
        send_sem=send,
        recv_sem=recv,
        device_id=(x * 4 + y, z * 2 + core),
        device_id_type=MESH,
    )


def greet(devices):
    barrier = pltpu.get_barrier_semaphore()
    for x, y, z, core in devices:
        pl.semaphore_signal(
            barrier, inc=1, device_id=(x * 4 + y, z * 2 + core), device_id_type=MESH
        )
    pl.semaphore_wait(barrier, len(devices))


def plane_and_peer(x, y, z, core):
    out = []
    for dx in range(4):
        for dy in range(4):
            if dx or dy:
                out.append(((x + dx) % 4, (y + dy) % 4, z, core))
    return out + [(x, y, z, 1 - core)]


CH = 8
CR = 128 // CH
LEFT, RIGHT = pl.ds(0, NB), pl.ds(NB, NB)
ROWS = (pl.ds(0, 16), pl.ds(16, 16))
PAIR = (pl.ds(0, 2), pl.ds(2, 2))


def unit(part, u, core):
    if part == 0:
        p = u + core if u < 2 else 2
        off = NB * (1 - core) if u < 2 else NB
    else:
        p = u - core if u >= 1 else 0
        off = NB * core if u >= 1 else 0
    if isinstance(off, int):
        return p, pl.ds(off, NB)
    return p, pl.ds(pl.multiple_of(off, NB), NB)


def line(order, x, y, d):
    return ((x + d) % 4, y) if order == 0 else (x, (y + d) % 4)


def spread_steps(part, own, strips, sems):
    scat_s, scat_r, one_s, one_r, two_s, two_r, loc = sems
    x, y, z, core = place()
    units = [unit(part, u, core) for u in range(NP)]

    def piece(ref, u, px, py):
        p, cols = units[u]
        if ref is own:
            return own.at[px, py, :, cols]
        return strips.at[p, px, py, :, cols]

    def scatter(u, d):
        tx, ty = (x + d // 4) % 4, (y + d % 4) % 4
        return remote(
            piece(own, u, tx, ty), piece(strips, u, tx, ty),
            scat_s.at[u, d], scat_r.at[u], tx, ty, z, core,
        )

    def keep(u):
        return pltpu.make_async_copy(piece(own, u, x, y), piece(strips, u, x, y), loc.at[u])

    roots = [(x == 0) & (y == units[u][0]) for u in range(NP)]
    for u in range(NP):

        @pl.when(roots[u])
        def _():
            keep(u).start()
            for d in range(15, 0, -1):
                scatter(u, d).start()

    yield

    for u in range(NP):

        @pl.when(roots[u])
        def _():
            keep(u).wait()

        @pl.when(jnp.logical_not(roots[u]))
        def _():
            here = piece(strips, u, x, y)
            remote(here, here, scat_s.at[u, 0], scat_r.at[u], x, y, z, 1 - core).wait_recv()

    first = []
    for u in range(NP):
        p, cols = units[u]
        for order in range(2):
            for d in range(1, 4):
                here = strips.at[p, x, y, ROWS[order], cols]
                tx, ty = line(order, x, y, d)
                first.append(
                    remote(
                        here, here, one_s.at[order, u, d], one_r.at[order, u, d],
                        tx, ty, z, core,
                    )
                )
    for copy in first:
        copy.start()
    yield

    for copy in first:
        copy.wait_recv()

    def block(order, u, at, pick):
        p, cols = units[u]
        if order == 0:
            return strips.at[p, pick, (y + at) % 4, ROWS[0], cols]
        return strips.at[p, (x + at) % 4, pick, ROWS[1], cols]

    def second(order, u, kind):
        whole = pl.ds(0, 4)
        at, pick, d = (
            (0, whole, 1), (0, whole, 3), (3, PAIR[0], 1), (1, PAIR[1], 3)
        )[kind]
        ref = block(order, u, at, pick)
        tx, ty = line(1 - order, x, y, d)
        return remote(
            ref, ref, two_s.at[order, u, kind], two_r.at[order, u, kind], tx, ty, z, core
        )

    def arrival(order, u, kind):
        whole = pl.ds(0, 4)
        at, pick = ((3, whole), (1, whole), (2, PAIR[0]), (2, PAIR[1]))[kind]
        ref = block(order, u, at, pick)
        return remote(
            ref, ref, two_s.at[order, u, kind], two_r.at[order, u, kind], x, y, z, 1 - core
        )

    every = [(order, u) for u in range(NP) for order in range(2)]
    for order, u in every:
        for kind in (0, 1):
            second(order, u, kind).start()
    yield

    for order, u in every:
        for kind in (0, 1):
            arrival(order, u, kind).wait_recv()
            second(order, u, kind + 2).start()
    yield

    for order, u in every:
        for kind in (2, 3):
            arrival(order, u, kind).wait_recv()
    yield

    for u in range(NP):

        @pl.when(roots[u])
        def _():
            for d in range(1, 16):
                scatter(u, d).wait_send()

    for copy in first:
        copy.wait_send()
    for order, u in every:
        for kind in range(4):
            second(order, u, kind).wait_send()
    yield


def along_steps(src, out, sems):
    ring_s, ring_r, peer_s, peer_r = sems
    x, y, z, core = place()
    up, down = (z + 1) % 4, (z + 3) % 4
    positions = (up, 3 - z)
    targets = (up, down)

    def chunk(owner, way, step):
        return out.at[pl.ds(owner, 1), way, step]

    def ring(way, step, block):
        mine = chunk(core, way, step)
        return remote(
            block, mine, ring_s.at[way, step], ring_r.at[way, step], x, y, targets[way], core
        )

    def across(way, step, block):
        mine = chunk(core, way, step)
        return remote(
            block, mine, peer_s.at[way, step], peer_r.at[way, step], x, y, z, 1 - core
        )

    @pl.when(z == 3)
    def _():
        for step in range(CH):
            for way in range(2):
                ring(way, step, src.at[:, way, step]).start()
        for step in range(CH):
            for way in range(2):
                across(way, step, src.at[:, way, step]).start()
        out[pl.ds(core, 1)] = src[...]

    yield
    for tick in range(CH + 2):
        for way in range(2):
            for pos in range(1, 4):
                step = tick - (pos - 1)
                if not 0 <= step < CH:
                    continue

                @pl.when(positions[way] == pos)
                def _():
                    mine = chunk(core, way, step)
                    ring(way, step, mine).wait_recv()
                    if pos < 3:
                        ring(way, step, mine).start()
                    across(way, step, mine).start()

        yield

    for step in range(CH):
        for way in range(2):
            mine, other = chunk(core, way, step), chunk(1 - core, way, step)
            remote(
                mine, other, peer_s.at[way, step], peer_r.at[way, step], x, y, z, 1 - core
            ).wait()

            @pl.when(positions[way] < 3)
            def _():
                ring(way, step, mine).wait_send()

    yield


def reduce_steps(part, wide, src, out, bufs, sems):
    got, acc, tot, got2, fin = bufs
    one_s, one_r, two_s, two_r, g_s, g_r, loc = sems
    x, y, z, core = place()
    units = [unit(part, u, core) for u in range(NP)]
    every = [(order, u) for u in range(NP) for order in range(2)]

    def share(order, u, at, pick):
        p, cols = units[u]
        if order == 0:
            return p, (x + at) % 4, pick, ROWS[0], cols
        return p, pick, (y + at) % 4, ROWS[1], cols

    def one(order, u, kind, way):
        step = 1 if way == 0 else 3
        if kind == 0:
            ref = src.at[share(order, u, 2, PAIR[way])]
        elif kind == 1:
            ref = src.at[share(order, u, step, PAIR[1 - way])]
        else:
            ref = acc.at[order, u, way]
        tx, ty = line(order, x, y, step)
        return remote(
            ref, got.at[order, u, kind, way],
            one_s.at[order, u, kind * 2 + way], one_r.at[order, u, kind * 2 + way],
            tx, ty, z, core,
        )

    for kind in (0, 1):
        for order, u in every:
            for way in range(2):
                one(order, u, kind, way).start()
    yield

    for order, u in every:
        for way in range(2):
            one(order, u, 0, way).wait_recv()
            step = 1 if way == 0 else 3
            acc[order, u, way] = (
                src[share(order, u, step, PAIR[way])] + got[order, u, 0, way]
            )
            one(order, u, 2, way).start()
    yield

    def two(order, u, d):
        tx, ty = line(1 - order, x, y, d)
        index = ty if order == 0 else tx
        return remote(
            tot.at[order, u, index], got2.at[order, u, d - 1],
            two_s.at[order, u, d], two_r.at[order, u, d], tx, ty, z, core,
        )

    for order, u in every:
        for kind in (1, 2):
            for way in range(2):
                one(order, u, kind, way).wait_recv()
        for half in range(2):
            base = src[share(order, u, 0, PAIR[half])]
            tot[order, u, PAIR[half]] = base + (
                got[order, u, 2, half] + got[order, u, 1, 1 - half]
            )
        for d in range(1, 4):
            two(order, u, d).start()
    yield

    for order, u in every:
        for d in range(1, 4):
            two(order, u, d).wait_recv()
        here = y if order == 0 else x
        fin[u, ROWS[order]] = (tot[order, u, here] + got2[order, u, 0]) + (
            got2[order, u, 1] + got2[order, u, 2]
        )

    def slot(u, px, py):
        return out.at[core, u, px, py] if wide else out.at[u, px, py]

    def send(root, u):
        return remote(
            fin.at[u], slot(u, x, y), g_s.at[root, u], g_r.at[u, x * 4 + y], 0, root, z, core
        )

    def keep(u):
        return pltpu.make_async_copy(fin.at[u], slot(u, x, y), loc.at[u])

    def cases():
        for root in range(NP):
            at_root = (x == 0) & (y == root)
            for u in range(NP):
                flag = units[u][0] == root
                if wide:
                    flag = flag | (z == 3)
                yield root, u, flag & at_root, flag & jnp.logical_not(at_root)

    for root, u, local, away in cases():

        @pl.when(away)
        def _():
            send(root, u).start()

        @pl.when(local)
        def _():
            keep(u).start()

    yield

    for root, u, local, away in cases():

        @pl.when(away)
        def _():
            send(root, u).wait_send()

        @pl.when(local)
        def _():
            keep(u).wait()
            for d in range(1, 16):
                sx, sy = (x + d // 4) % 4, (y + d % 4) % 4
                remote(
                    fin.at[u], slot(u, sx, sy), g_s.at[root, u], g_r.at[u, sx * 4 + sy],
                    x, y, z, 1 - core,
                ).wait_recv()

    for order, u in every:
        for kind in range(3):
            for way in range(2):
                one(order, u, kind, way).wait_send()
        for d in range(1, 4):
            two(order, u, d).wait_send()
    yield


DMA = pltpu.SemaphoreType.DMA
SPREAD_SEMS = [
    DMA((3, 16)), DMA((3,)), DMA((2, 3, 4)), DMA((2, 3, 4)), DMA((2, 3, 4)), DMA((2, 3, 4)),
    DMA((3,)),
]
ALONG_SEMS = [DMA((2, CH))] * 4
REDUCE_BUFS = [
    pltpu.VMEM((2, 3, 3, 2, 2, 16, NB), F32),
    pltpu.VMEM((2, 3, 2, 2, 16, NB), F32),
    pltpu.VMEM((2, 3, 4, 16, NB), F32),
    pltpu.VMEM((2, 3, 3, 16, NB), F32),
    pltpu.VMEM((3, 32, NB), F32),
]
REDUCE_SEMS = [
    DMA((2, 3, 6)), DMA((2, 3, 6)), DMA((2, 3, 4)), DMA((2, 3, 4)), DMA((3, 3)), DMA((3, 16)),
    DMA((3,)),
]
VM = pl.BlockSpec(memory_space=pltpu.VMEM)
ANY = pl.BlockSpec(memory_space=pl.ANY)


def drive(*plan):
    for steps, count in plan:
        for _ in range(count):
            next(steps)


def spread_kernel(own, cot, strips, blocks, half, *sems):
    x, y, z, core = place()
    greet(plane_and_peer(x, y, z, core))
    ex_s, ex_r, loc = sems[-3:]
    half_copy = remote(
        cot.at[pl.ds(256 * (1 - core), 256)], half, ex_s.at[3], ex_r.at[3], x, y, z, 1 - core
    )
    half_copy.start()
    steps = spread_steps(0, own, strips, sems[:7])
    drive((steps, 5))
    for u in range(NP):
        p, cols = unit(0, u, core)
        ref = strips.at[p, :, :, :, cols]
        remote(
            ref, blocks.at[core, u], ex_s.at[u], ex_r.at[u], x, y, z, 1 - core
        ).start()
        pltpu.make_async_copy(ref, blocks.at[core, u], loc.at[u]).start()
    drive((steps, 1))
    for u in range(NP):
        p, cols = unit(0, u, core)
        ref = strips.at[p, :, :, :, cols]
        pltpu.make_async_copy(ref, blocks.at[core, u], loc.at[u]).wait()
        remote(
            ref, blocks.at[1 - core, u], ex_s.at[u], ex_r.at[u], x, y, z, 1 - core
        ).wait()
    half_copy.wait()


def comm(collective_id, mib):
    return pltpu.CompilerParams(
        collective_id=collective_id, has_side_effects=True, vmem_limit_bytes=mib << 20
    )


def spread(factor, cot):
    return pl.pallas_call(
        spread_kernel,
        out_shape=(
            jax.ShapeDtypeStruct((3, 4, 4, 32, 1024), F32),
            jax.ShapeDtypeStruct((2, 3, 4, 4, 32, NB), F32),
            jax.ShapeDtypeStruct((256, 1024), F32),
        ),
        in_specs=[ANY, ANY],
        out_specs=(ANY, VM, VM),
        scratch_shapes=SPREAD_SEMS + [DMA((4,)), DMA((4,)), DMA((3,))],
        compiler_params=comm(0, 32),
    )(factor.reshape(4, 4, 32, 1024), cot)


def with_z(x, y, z, core):
    return plane_and_peer(x, y, z, core) + [
        (x, y, (z + 1) % 4, core), (x, y, (z + 3) % 4, core)
    ]


def along_spread_kernel(src, own, _, out, strips, *sems):
    greet(with_z(*place()))
    a = along_steps(src, out, sems[7:])
    s = spread_steps(1, own, strips, sems[:7])
    drive((a, 1), (s, 1), (a, 4), (s, 1), (a, 2), (s, 1), (a, 4), (s, 1), (a, 1), (s, 2))


def along_spread(half, factor, strips):
    out, strips = pl.pallas_call(
        along_spread_kernel,
        out_shape=(
            jax.ShapeDtypeStruct((2, 2, CH, CR, 1536), F32),
            jax.ShapeDtypeStruct((3, 4, 4, 32, 1024), F32),
        ),
        in_specs=[VM, ANY, ANY],
        out_specs=(VM, ANY),
        scratch_shapes=SPREAD_SEMS + ALONG_SEMS,
        input_output_aliases={2: 1},
        compiler_params=comm(1, 16),
    )(half.reshape(1, 2, CH, CR, 1536), factor.reshape(4, 4, 32, 1024), strips)
    return out.reshape(512, 1536), strips.reshape(1536, 1024)


def reduce_kernel(src, out, *rest):
    x, y, z, core = place()
    greet(plane_and_peer(x, y, z, core))
    bufs, sems = rest[:5], rest[5:]
    ex_s, ex_r = sems[-2:]
    steps = reduce_steps(0, True, src, out, bufs, sems[:7])
    drive((steps, 5))

    @pl.when((x == 0) & (y < NP) & (z == 3))
    def _():
        remote(
            out.at[core], out.at[core], ex_s.at[0], ex_r.at[0], x, y, z, 1 - core
        ).start()
        remote(
            out.at[core], out.at[1 - core], ex_s.at[0], ex_r.at[0], x, y, z, 1 - core
        ).wait()


def reduce_rows(part):
    return pl.pallas_call(
        reduce_kernel,
        out_shape=jax.ShapeDtypeStruct((2, 3, 4, 4, 32, NB), F32),
        in_specs=[VM],
        out_specs=VM,
        scratch_shapes=REDUCE_BUFS + REDUCE_SEMS + [DMA((1,)), DMA((1,))],
        compiler_params=comm(2, 32),
    )(part.reshape(3, 4, 4, 32, 1024))


def along_reduce_kernel(src, part, out, rest_out, *rest):
    greet(with_z(*place()))
    bufs, sems = rest[:5], rest[5:]
    a = along_steps(src, out, sems[7:])
    r = reduce_steps(1, False, part, rest_out, bufs, sems[:7])
    drive((a, 1), (r, 1), (a, 3), (r, 1), (a, 4), (r, 1), (a, 3), (r, 1), (a, 1), (r, 1))


def along_reduce(half, part):
    out, rest_out = pl.pallas_call(
        along_reduce_kernel,
        out_shape=(
            jax.ShapeDtypeStruct((2, 2, CH, CR, 1536), F32),
            jax.ShapeDtypeStruct((3, 4, 4, 32, NB), F32),
        ),
        in_specs=[VM, VM],
        out_specs=(VM, VM),
        scratch_shapes=REDUCE_BUFS + REDUCE_SEMS + ALONG_SEMS,
        compiler_params=comm(3, 40),
    )(half.reshape(1, 2, CH, CR, 1536), part.reshape(3, 4, 4, 32, 1024))
    return out.reshape(512, 1536), rest_out.reshape(3, NB, NB)


BS = 128


def invert_kernel(d_ref, o_ref):
    rows = lax.broadcasted_iota(jnp.int32, (BS, BS), 0)
    cols = lax.broadcasted_iota(jnp.int32, (BS, BS), 1)
    diag = rows == cols
    for block in range(NP * (NB // BS)):
        which, at = block // (NB // BS), pl.ds(block % (NB // BS) * BS, BS)
        base = d_ref[which, at, at]
        scale = jnp.sum(jnp.where(diag, base, 0.0), axis=1, keepdims=True)
        o_ref[which, at, at] = jnp.where(diag, 1.0 / scale, 0.0)
    size = 1
    while size < BS:
        pick = (rows // (2 * size) == cols // (2 * size)) & (
            (rows // size) % 2 > (cols // size) % 2
        )
        for block in range(NP * (NB // BS)):
            which, at = block // (NB // BS), pl.ds(block % (NB // BS) * BS, BS)
            have = o_ref[which, at, at]
            below = jnp.where(pick, d_ref[which, at, at], 0.0)
            o_ref[which, at, at] = have - dot(dot(have, below, HI), have, HI)
        size *= 2
    while size < NB:
        for which in range(NP):
            for base in range(0, NB, 2 * size):
                up, down = pl.ds(base, size), pl.ds(base + size, size)
                corner = dot(
                    dot(o_ref[which, down, down], d_ref[which, down, up], HI),
                    o_ref[which, up, up], HI,
                )
                o_ref[which, down, up] = -corner
                o_ref[which, up, down] = jnp.zeros((size, size), F32)
        size *= 2


def invert(blocks):
    vm = pl.BlockSpec(memory_space=pltpu.VMEM)
    return pl.pallas_call(
        invert_kernel,
        out_shape=jax.ShapeDtypeStruct((NP, NB, NB), F32),
        in_specs=[vm],
        out_specs=vm,
        compiler_params=pltpu.CompilerParams(vmem_limit_bytes=16 << 20),
    )(blocks)


def lower_half(matrix):
    rows = lax.broadcasted_iota(jnp.int32, (NB, NB), 0)
    cols = lax.broadcasted_iota(jnp.int32, (NB, NB), 1)
    return jnp.where(rows > cols, matrix, jnp.where(rows == cols, 0.5 * matrix, 0.0))


def adjoint_of(factor, inverse, cot):
    inner = lower_half(dot_t(factor, jnp.tril(cot)))
    return lower_half(dot(dot_t(inverse, inner), inverse))


def chain(l, inv, t):
    a2 = adjoint_of(l[22], inv[2], t[22])
    y2 = a2 + a2.T
    t21 = t[21] - dot(y2, l[21])
    t20 = t[20] - dot(y2, l[20])
    s21 = dot(t21, inv[1])
    t11 = t[11] - dot_t(s21, l[21])
    t10 = t[10] - dot_t(s21, l[20])
    a1 = adjoint_of(l[11], inv[1], t11)
    y1 = a1 + a1.T
    t10 = t10 - dot(y1, l[10])
    t20 = t20 - dot(s21, l[10])
    s20 = dot(t20, inv[0])
    s10 = dot(t10, inv[0])
    t00 = t[0] - dot_t(s20, l[20]) - dot_t(s10, l[10])
    a0 = adjoint_of(l[0], inv[0], t00)
    y0 = a0 + a0.T
    return (a0, a1, a2), (y0, y1, y2), s10, s20, s21


def shards(factor, cot):
    row = lax.axis_index("row")
    col = lax.axis_index("col")
    core = col % 2
    strips, blocks, other_half = spread(factor, cot)
    blocks = blocks.reshape(2, 3, NB, NB)
    l = {
        0: blocks[0, 0], 10: blocks[0, 1], 20: blocks[0, 2],
        11: blocks[1, 0], 21: blocks[1, 1], 22: blocks[1, 2],
    }
    inv = invert(jnp.stack([l[0], l[11], l[22]]))
    my_half = lax.dynamic_slice(cot, (core * 256, 0), (256, 1024))
    g6 = jnp.where(core == 0, my_half, other_half)
    g7 = jnp.where(core == 0, other_half, my_half)
    s2 = dot(g7[:, NB:], inv[2])
    s1 = dot(g7[:, :NB] - dot(s2, l[21]), inv[1])
    s0 = dot(g6[:, NB:] - dot(s2, l[20]) - dot(s1, l[10]), inv[0])
    solved, strips = along_spread(jnp.concatenate([s0, s1, s2], axis=1), factor, strips)
    lower_rows = row >= NP
    part = jnp.where(lower_rows, -dot_t(solved, factor), 0.0).reshape(3, NB, 1024)
    which = lax.broadcasted_iota(jnp.int32, (3, 1, 1), 0)
    part = jnp.where(which == row, cot[None], part)
    near = reduce_rows(part).reshape(2, 3, NB, NB)
    t = {
        0: near[0, 0], 10: near[0, 1], 20: near[0, 2],
        11: near[1, 0], 21: near[1, 1], 22: near[1, 2],
    }
    a, sym, s10, s20, s21 = chain(l, inv, t)
    pick = row
    rows0 = jnp.concatenate([sym[0], s10.T, s20.T], axis=1)
    rows1 = jnp.concatenate([s10, sym[1], s21.T], axis=1)
    rows2 = jnp.concatenate([s20, s21, sym[2]], axis=1)
    mixed = jnp.where(pick == 0, rows0, jnp.where(pick == 1, rows1, rows2))
    mixed_half = lax.dynamic_slice(mixed, (core * 256, 0), (256, 1536))
    mixed, far = along_reduce(mixed_half, part)
    factor_rows = jnp.where(lower_rows, solved, mixed)
    even = core == 0

    def by_row(zero, one, two):
        return jnp.where(row == 0, zero, jnp.where(row == 1, one, two))

    total_left = by_row(
        far[0], jnp.where(even, far[1], near[1, 0]), jnp.where(even, far[2], near[1, 1])
    )
    total_right = by_row(
        jnp.where(even, near[0, 0], far[1]),
        jnp.where(even, near[0, 1], far[2]),
        jnp.where(even, near[0, 2], near[1, 2]),
    )
    start = jnp.where(
        lower_rows, cot, jnp.concatenate([total_left, total_right], axis=1)
    )
    out = start - dot(factor_rows, strips)
    cut = cot[:, :NB], cot[:, NB:]
    last6 = jnp.where(
        lower_rows, solved[:, :NB],
        jnp.where(pick == 0, a[0], jnp.where(pick == 1, s10, s20)),
    )
    left7 = jnp.where(
        lower_rows, solved[:, NB:1024],
        jnp.where(pick == 0, cut[0], jnp.where(pick == 1, a[1], s21)),
    )
    right7 = jnp.where(
        lower_rows, solved[:, 1024:],
        jnp.where(pick == 2, a[2], cut[1]),
    )
    left = jnp.where(col == 7, left7, out[:, :NB])
    right = jnp.where(col == 7, right7, jnp.where(col == 6, last6, out[:, NB:]))
    return jnp.concatenate([left, right], axis=1)


def solution(mesh):
    placed = (P("row", "col"), P("row", "col"))
    return jax.shard_map(
        shards, mesh=mesh, in_specs=placed, out_specs=P("row", "col"), check_vma=False
    )
```

```python
import jax
import jax.numpy as jnp
from jax import lax
from jax.experimental import pallas as pl
from jax.experimental.pallas import tpu as pltpu
from jax.sharding import PartitionSpec as P

NB = 512
NP = 3
MESH = pl.DeviceIdType.MESH
HI = lax.Precision.HIGHEST
MID = lax.Precision.HIGH
F32 = jnp.float32


def dot(a, b, precision=MID):
    return jnp.dot(a, b, precision=precision, preferred_element_type=F32)


def dot_t(a, b, precision=MID):
    return lax.dot_general(
        a, b, (((0,), (0,)), ((), ())), precision=precision, preferred_element_type=F32
    )


def place():
    row = lax.axis_index("row")
    col = lax.axis_index("col")
    return row // 4, row % 4, col // 2, col % 2


def remote(src, dst, send, recv, x, y, z, core):
    return pltpu.make_async_remote_copy(
        src_ref=src,
        dst_ref=dst,
        send_sem=send,
        recv_sem=recv,
        device_id=(x * 4 + y, z * 2 + core),
        device_id_type=MESH,
    )


def greet(devices):
    barrier = pltpu.get_barrier_semaphore()
    for x, y, z, core in devices:
        pl.semaphore_signal(
            barrier, inc=1, device_id=(x * 4 + y, z * 2 + core), device_id_type=MESH
        )
    pl.semaphore_wait(barrier, len(devices))


def plane_and_peer(x, y, z, core):
    out = []
    for dx in range(4):
        for dy in range(4):
            if dx or dy:
                out.append(((x + dx) % 4, (y + dy) % 4, z, core))
    return out + [(x, y, z, 1 - core)]


CH = 8
CR = 128 // CH
LEFT, RIGHT = pl.ds(0, NB), pl.ds(NB, NB)
ROWS = (pl.ds(0, 16), pl.ds(16, 16))
PAIR = (pl.ds(0, 2), pl.ds(2, 2))


def unit(part, u, core):
    if part == 0:
        p = u + core if u < 2 else 2
        off = NB * (1 - core) if u < 2 else NB
    else:
        p = u - core if u >= 1 else 0
        off = NB * core if u >= 1 else 0
    if isinstance(off, int):
        return p, pl.ds(off, NB)
    return p, pl.ds(pl.multiple_of(off, NB), NB)


def line(order, x, y, d):
    return ((x + d) % 4, y) if order == 0 else (x, (y + d) % 4)


def spread_steps(part, own, strips, sems):
    scat_s, scat_r, one_s, one_r, two_s, two_r, loc = sems
    x, y, z, core = place()
    units = [unit(part, u, core) for u in range(NP)]

    def piece(ref, u, px, py):
        p, cols = units[u]
        if ref is own:
            return own.at[px, py, :, cols]
        return strips.at[p, px, py, :, cols]

    def scatter(u, d):
        tx, ty = (x + d // 4) % 4, (y + d % 4) % 4
        return remote(
            piece(own, u, tx, ty), piece(strips, u, tx, ty),
            scat_s.at[u, d], scat_r.at[u], tx, ty, z, core,
        )

    def keep(u):
        return pltpu.make_async_copy(piece(own, u, x, y), piece(strips, u, x, y), loc.at[u])

    roots = [(x == 0) & (y == units[u][0]) for u in range(NP)]
    for u in range(NP):

        @pl.when(roots[u])
        def _():
            keep(u).start()
            for d in range(15, 0, -1):
                scatter(u, d).start()

    yield

    for u in range(NP):

        @pl.when(roots[u])
        def _():
            keep(u).wait()

        @pl.when(jnp.logical_not(roots[u]))
        def _():
            here = piece(strips, u, x, y)
            remote(here, here, scat_s.at[u, 0], scat_r.at[u], x, y, z, 1 - core).wait_recv()

    first = []
    for u in range(NP):
        p, cols = units[u]
        for order in range(2):
            for d in range(1, 4):
                here = strips.at[p, x, y, ROWS[order], cols]
                tx, ty = line(order, x, y, d)
                first.append(
                    remote(
                        here, here, one_s.at[order, u, d], one_r.at[order, u, d],
                        tx, ty, z, core,
                    )
                )
    for copy in first:
        copy.start()
    yield

    for copy in first:
        copy.wait_recv()

    def block(order, u, at, pick):
        p, cols = units[u]
        if order == 0:
            return strips.at[p, pick, (y + at) % 4, ROWS[0], cols]
        return strips.at[p, (x + at) % 4, pick, ROWS[1], cols]

    def second(order, u, kind):
        whole = pl.ds(0, 4)
        at, pick, d = (
            (0, whole, 1), (0, whole, 3), (3, PAIR[0], 1), (1, PAIR[1], 3)
        )[kind]
        ref = block(order, u, at, pick)
        tx, ty = line(1 - order, x, y, d)
        return remote(
            ref, ref, two_s.at[order, u, kind], two_r.at[order, u, kind], tx, ty, z, core
        )

    def arrival(order, u, kind):
        whole = pl.ds(0, 4)
        at, pick = ((3, whole), (1, whole), (2, PAIR[0]), (2, PAIR[1]))[kind]
        ref = block(order, u, at, pick)
        return remote(
            ref, ref, two_s.at[order, u, kind], two_r.at[order, u, kind], x, y, z, 1 - core
        )

    every = [(order, u) for u in range(NP) for order in range(2)]
    for order, u in every:
        for kind in (0, 1):
            second(order, u, kind).start()
    yield

    for order, u in every:
        for kind in (0, 1):
            arrival(order, u, kind).wait_recv()
            second(order, u, kind + 2).start()
    yield

    for order, u in every:
        for kind in (2, 3):
            arrival(order, u, kind).wait_recv()
    yield

    for u in range(NP):

        @pl.when(roots[u])
        def _():
            for d in range(1, 16):
                scatter(u, d).wait_send()

    for copy in first:
        copy.wait_send()
    for order, u in every:
        for kind in range(4):
            second(order, u, kind).wait_send()
    yield


def along_steps(src, out, sems):
    ring_s, ring_r, peer_s, peer_r = sems
    x, y, z, core = place()
    up, down = (z + 1) % 4, (z + 3) % 4
    positions = (up, 3 - z)
    targets = (up, down)

    def chunk(owner, way, step):
        return out.at[pl.ds(owner, 1), way, step]

    def ring(way, step, block):
        mine = chunk(core, way, step)
        return remote(
            block, mine, ring_s.at[way, step], ring_r.at[way, step], x, y, targets[way], core
        )

    def across(way, step, block):
        mine = chunk(core, way, step)
        return remote(
            block, mine, peer_s.at[way, step], peer_r.at[way, step], x, y, z, 1 - core
        )

    @pl.when(z == 3)
    def _():
        for step in range(CH):
            for way in range(2):
                ring(way, step, src.at[:, way, step]).start()
        for step in range(CH):
            for way in range(2):
                across(way, step, src.at[:, way, step]).start()
        out[pl.ds(core, 1)] = src[...]

    yield
    for tick in range(CH + 2):
        for way in range(2):
            for pos in range(1, 4):
                step = tick - (pos - 1)
                if not 0 <= step < CH:
                    continue

                @pl.when(positions[way] == pos)
                def _():
                    mine = chunk(core, way, step)
                    ring(way, step, mine).wait_recv()
                    if pos < 3:
                        ring(way, step, mine).start()
                    across(way, step, mine).start()

        yield

    for step in range(CH):
        for way in range(2):
            mine, other = chunk(core, way, step), chunk(1 - core, way, step)
            remote(
                mine, other, peer_s.at[way, step], peer_r.at[way, step], x, y, z, 1 - core
            ).wait()

            @pl.when(positions[way] < 3)
            def _():
                ring(way, step, mine).wait_send()

    yield


def reduce_steps(part, wide, src, out, bufs, sems):
    got, acc, tot, got2, fin = bufs
    one_s, one_r, two_s, two_r, g_s, g_r, loc = sems
    x, y, z, core = place()
    units = [unit(part, u, core) for u in range(NP)]
    every = [(order, u) for u in range(NP) for order in range(2)]

    def share(order, u, at, pick):
        p, cols = units[u]
        if order == 0:
            return p, (x + at) % 4, pick, ROWS[0], cols
        return p, pick, (y + at) % 4, ROWS[1], cols

    def one(order, u, kind, way):
        step = 1 if way == 0 else 3
        if kind == 0:
            ref = src.at[share(order, u, 2, PAIR[way])]
        elif kind == 1:
            ref = src.at[share(order, u, step, PAIR[1 - way])]
        else:
            ref = acc.at[order, u, way]
        tx, ty = line(order, x, y, step)
        return remote(
            ref, got.at[order, u, kind, way],
            one_s.at[order, u, kind * 2 + way], one_r.at[order, u, kind * 2 + way],
            tx, ty, z, core,
        )

    for kind in (0, 1):
        for order, u in every:
            for way in range(2):
                one(order, u, kind, way).start()
    yield

    for order, u in every:
        for way in range(2):
            one(order, u, 0, way).wait_recv()
            step = 1 if way == 0 else 3
            acc[order, u, way] = (
                src[share(order, u, step, PAIR[way])] + got[order, u, 0, way]
            )
            one(order, u, 2, way).start()
    yield

    def two(order, u, d):
        tx, ty = line(1 - order, x, y, d)
        index = ty if order == 0 else tx
        return remote(
            tot.at[order, u, index], got2.at[order, u, d - 1],
            two_s.at[order, u, d], two_r.at[order, u, d], tx, ty, z, core,
        )

    for order, u in every:
        for kind in (1, 2):
            for way in range(2):
                one(order, u, kind, way).wait_recv()
        for half in range(2):
            base = src[share(order, u, 0, PAIR[half])]
            tot[order, u, PAIR[half]] = base + (
                got[order, u, 2, half] + got[order, u, 1, 1 - half]
            )
        for d in range(1, 4):
            two(order, u, d).start()
    yield

    for order, u in every:
        for d in range(1, 4):
            two(order, u, d).wait_recv()
        here = y if order == 0 else x
        fin[u, ROWS[order]] = (tot[order, u, here] + got2[order, u, 0]) + (
            got2[order, u, 1] + got2[order, u, 2]
        )

    def slot(u, px, py):
        return out.at[core, u, px, py] if wide else out.at[u, px, py]

    def send(root, u):
        return remote(
            fin.at[u], slot(u, x, y), g_s.at[root, u], g_r.at[u, x * 4 + y], 0, root, z, core
        )

    def keep(u):
        return pltpu.make_async_copy(fin.at[u], slot(u, x, y), loc.at[u])

    def cases():
        for root in range(NP):
            at_root = (x == 0) & (y == root)
            for u in range(NP):
                flag = units[u][0] == root
                if wide:
                    flag = flag | (z == 3)
                yield root, u, flag & at_root, flag & jnp.logical_not(at_root)

    for root, u, local, away in cases():

        @pl.when(away)
        def _():
            send(root, u).start()

        @pl.when(local)
        def _():
            keep(u).start()

    yield

    for root, u, local, away in cases():

        @pl.when(away)
        def _():
            send(root, u).wait_send()

        @pl.when(local)
        def _():
            keep(u).wait()
            for d in range(1, 16):
                sx, sy = (x + d // 4) % 4, (y + d % 4) % 4
                remote(
                    fin.at[u], slot(u, sx, sy), g_s.at[root, u], g_r.at[u, sx * 4 + sy],
                    x, y, z, 1 - core,
                ).wait_recv()

    for order, u in every:
        for kind in range(3):
            for way in range(2):
                one(order, u, kind, way).wait_send()
        for d in range(1, 4):
            two(order, u, d).wait_send()
    yield


DMA = pltpu.SemaphoreType.DMA
SPREAD_SEMS = [
    DMA((3, 16)), DMA((3,)), DMA((2, 3, 4)), DMA((2, 3, 4)), DMA((2, 3, 4)), DMA((2, 3, 4)),
    DMA((3,)),
]
ALONG_SEMS = [DMA((2, CH))] * 4
REDUCE_BUFS = [
    pltpu.VMEM((2, 3, 3, 2, 2, 16, NB), F32),
    pltpu.VMEM((2, 3, 2, 2, 16, NB), F32),
    pltpu.VMEM((2, 3, 4, 16, NB), F32),
    pltpu.VMEM((2, 3, 3, 16, NB), F32),
    pltpu.VMEM((3, 32, NB), F32),
]
REDUCE_SEMS = [
    DMA((2, 3, 6)), DMA((2, 3, 6)), DMA((2, 3, 4)), DMA((2, 3, 4)), DMA((3, 3)), DMA((3, 16)),
    DMA((3,)),
]
VM = pl.BlockSpec(memory_space=pltpu.VMEM)
ANY = pl.BlockSpec(memory_space=pl.ANY)


def drive(*plan):
    for steps, count in plan:
        for _ in range(count):
            next(steps)


def spread_kernel(own, cot, strips, blocks, half, *sems):
    x, y, z, core = place()
    greet(plane_and_peer(x, y, z, core))
    ex_s, ex_r, loc = sems[-3:]
    half_copy = remote(
        cot.at[pl.ds(256 * (1 - core), 256)], half, ex_s.at[3], ex_r.at[3], x, y, z, 1 - core
    )
    half_copy.start()
    steps = spread_steps(0, own, strips, sems[:7])
    drive((steps, 5))
    for u in range(NP):
        p, cols = unit(0, u, core)
        ref = strips.at[p, :, :, :, cols]
        remote(
            ref, blocks.at[core, u], ex_s.at[u], ex_r.at[u], x, y, z, 1 - core
        ).start()
        pltpu.make_async_copy(ref, blocks.at[core, u], loc.at[u]).start()
    drive((steps, 1))
    for u in range(NP):
        p, cols = unit(0, u, core)
        ref = strips.at[p, :, :, :, cols]
        pltpu.make_async_copy(ref, blocks.at[core, u], loc.at[u]).wait()
        remote(
            ref, blocks.at[1 - core, u], ex_s.at[u], ex_r.at[u], x, y, z, 1 - core
        ).wait()
    half_copy.wait()


def comm(collective_id, mib):
    return pltpu.CompilerParams(
        collective_id=collective_id, has_side_effects=True, vmem_limit_bytes=mib << 20
    )


def spread(factor, cot):
    return pl.pallas_call(
        spread_kernel,
        out_shape=(
            jax.ShapeDtypeStruct((3, 4, 4, 32, 1024), F32),
            jax.ShapeDtypeStruct((2, 3, 4, 4, 32, NB), F32),
            jax.ShapeDtypeStruct((256, 1024), F32),
        ),
        in_specs=[ANY, ANY],
        out_specs=(ANY, VM, VM),
        scratch_shapes=SPREAD_SEMS + [DMA((4,)), DMA((4,)), DMA((3,))],
        compiler_params=comm(0, 32),
    )(factor.reshape(4, 4, 32, 1024), cot)


def with_z(x, y, z, core):
    return plane_and_peer(x, y, z, core) + [
        (x, y, (z + 1) % 4, core), (x, y, (z + 3) % 4, core)
    ]


def along_spread_kernel(src, own, _, out, strips, *sems):
    greet(with_z(*place()))
    a = along_steps(src, out, sems[7:])
    s = spread_steps(1, own, strips, sems[:7])
    drive((a, 1), (s, 1), (a, 2), (s, 1), (a, 2), (s, 1), (a, 4), (s, 1), (a, 2), (a, 1), (s, 2))


def along_spread(half, factor, strips):
    out, strips = pl.pallas_call(
        along_spread_kernel,
        out_shape=(
            jax.ShapeDtypeStruct((2, 2, CH, CR, 1536), F32),
            jax.ShapeDtypeStruct((3, 4, 4, 32, 1024), F32),
        ),
        in_specs=[VM, ANY, ANY],
        out_specs=(VM, ANY),
        scratch_shapes=SPREAD_SEMS + ALONG_SEMS,
        input_output_aliases={2: 1},
        compiler_params=comm(1, 16),
    )(half.reshape(1, 2, CH, CR, 1536), factor.reshape(4, 4, 32, 1024), strips)
    return out.reshape(512, 1536), strips.reshape(1536, 1024)


def reduce_kernel(src, out, *rest):
    x, y, z, core = place()
    greet(plane_and_peer(x, y, z, core))
    bufs, sems = rest[:5], rest[5:]
    ex_s, ex_r = sems[-2:]
    steps = reduce_steps(0, True, src, out, bufs, sems[:7])
    drive((steps, 5))

    @pl.when((x == 0) & (y < NP) & (z == 3))
    def _():
        remote(
            out.at[core], out.at[core], ex_s.at[0], ex_r.at[0], x, y, z, 1 - core
        ).start()
        remote(
            out.at[core], out.at[1 - core], ex_s.at[0], ex_r.at[0], x, y, z, 1 - core
        ).wait()


def reduce_rows(part):
    return pl.pallas_call(
        reduce_kernel,
        out_shape=jax.ShapeDtypeStruct((2, 3, 4, 4, 32, NB), F32),
        in_specs=[VM],
        out_specs=VM,
        scratch_shapes=REDUCE_BUFS + REDUCE_SEMS + [DMA((1,)), DMA((1,))],
        compiler_params=comm(2, 32),
    )(part.reshape(3, 4, 4, 32, 1024))


def along_reduce_kernel(src, part, out, rest_out, *rest):
    greet(with_z(*place()))
    bufs, sems = rest[:5], rest[5:]
    a = along_steps(src, out, sems[7:])
    r = reduce_steps(1, False, part, rest_out, bufs, sems[:7])
    drive((a, 1), (r, 1), (a, 2), (r, 1), (a, 3), (r, 1), (a, 1), (r, 1), (a, 4), (a, 1), (r, 1))


def along_reduce(half, part):
    out, rest_out = pl.pallas_call(
        along_reduce_kernel,
        out_shape=(
            jax.ShapeDtypeStruct((2, 2, CH, CR, 1536), F32),
            jax.ShapeDtypeStruct((3, 4, 4, 32, NB), F32),
        ),
        in_specs=[VM, VM],
        out_specs=(VM, VM),
        scratch_shapes=REDUCE_BUFS + REDUCE_SEMS + ALONG_SEMS,
        compiler_params=comm(3, 40),
    )(half.reshape(1, 2, CH, CR, 1536), part.reshape(3, 4, 4, 32, 1024))
    return out.reshape(512, 1536), rest_out.reshape(3, NB, NB)


BS = 128


def invert_kernel(d_ref, o_ref):
    rows = lax.broadcasted_iota(jnp.int32, (BS, BS), 0)
    cols = lax.broadcasted_iota(jnp.int32, (BS, BS), 1)
    diag = rows == cols
    for block in range(NP * (NB // BS)):
        which, at = block // (NB // BS), pl.ds(block % (NB // BS) * BS, BS)
        base = d_ref[which, at, at]
        scale = jnp.sum(jnp.where(diag, base, 0.0), axis=1, keepdims=True)
        o_ref[which, at, at] = jnp.where(diag, 1.0 / scale, 0.0)

    def level(step, carry):
        pick = ((rows >> (step + 1)) == (cols >> (step + 1))) & (
            ((rows >> step) & 1) > ((cols >> step) & 1)
        )
        for block in range(NP * (NB // BS)):
            which, at = block // (NB // BS), pl.ds(block % (NB // BS) * BS, BS)
            have = o_ref[which, at, at]
            below = jnp.where(pick, d_ref[which, at, at], 0.0)
            o_ref[which, at, at] = have - dot(dot(have, below, HI), have, HI)
        return carry

    lax.fori_loop(0, 7, level, 0)
    size = BS
    while size < NB:
        for which in range(NP):
            for base in range(0, NB, 2 * size):
                up, down = pl.ds(base, size), pl.ds(base + size, size)
                corner = dot(
                    dot(o_ref[which, down, down], d_ref[which, down, up], HI),
                    o_ref[which, up, up], HI,
                )
                o_ref[which, down, up] = -corner
                o_ref[which, up, down] = jnp.zeros((size, size), F32)
        size *= 2


def invert(blocks):
    vm = pl.BlockSpec(memory_space=pltpu.VMEM)
    return pl.pallas_call(
        invert_kernel,
        out_shape=jax.ShapeDtypeStruct((NP, NB, NB), F32),
        in_specs=[vm],
        out_specs=vm,
        compiler_params=pltpu.CompilerParams(vmem_limit_bytes=16 << 20),
    )(blocks)


def plan():
    rows = []
    l00, l10, l20, l11, l21, l22, t00, t10, t20, t11, t21, t22, i0, i1, i2 = range(15)
    w, p, q, a2, y2, s21, s21t, a1, y1, s20, s10, s20t, s10t, a0, y0 = range(15, 30)

    def mm(a, b, to, tril=0, half=0):
        rows.append((0, a, b, to, to, tril, 0, 1, half))

    def take(a, b, to):
        rows.append((0, a, b, to, to, 0, 1, -1, 0))

    def turn(a, to, add=0):
        rows.append((1, a, a, a, to, 0, add, 1, 0))

    def adjoint(l, i, t, a, y):
        turn(l, w)
        mm(w, t, p, tril=1, half=1)
        turn(i, w)
        mm(w, p, q)
        mm(q, i, a, half=1)
        turn(a, y, add=1)

    adjoint(l22, i2, t22, a2, y2)
    take(y2, l21, t21)
    take(y2, l20, t20)
    mm(t21, i1, s21)
    turn(s21, s21t)
    take(s21t, l21, t11)
    take(s21t, l20, t10)
    adjoint(l11, i1, t11, a1, y1)
    take(y1, l10, t10)
    take(s21, l10, t20)
    mm(t20, i0, s20)
    mm(t10, i0, s10)
    turn(s20, s20t)
    turn(s10, s10t)
    take(s20t, l20, t00)
    take(s10t, l10, t00)
    adjoint(l00, i0, t00, a0, y0)
    coupling = ((y0, s10t, s20t), (s10, y1, s21t), (s20, s21, y2))
    result = ((a0, a0, a0), (s10, a1, a1), (s20, s21, a2))
    return rows, [x + y for x, y in zip(coupling, result)]


PLAN, PICKS = plan()
BLK = 256


def chain_kernel(plan_ref, pick_ref, l_ref, t_ref, i_ref, q_ref, z_ref, m, high, low):
    row, col = lax.axis_index("row"), lax.axis_index("col")
    for n in range(6):
        m[n] = l_ref[n]
        m[6 + n] = t_ref[n]
    for n in range(3):
        m[12 + n] = i_ref[n]

    def op(n, carry):
        kind, a, b, c = (plan_ref[n, j] for j in range(4))
        to, tril, keep, sign, half = (plan_ref[n, j] for j in range(4, 9))

        @pl.when(kind == 0)
        def _():
            def split(i, carry):
                at = pl.ds(pl.multiple_of(i * 128, 128), 128)
                rows = lax.broadcasted_iota(jnp.int32, (128, NB), 0) + i * 128
                cols = lax.broadcasted_iota(jnp.int32, (128, NB), 1)
                value = jnp.where((cols - rows) * tril > 0, 0.0, m[b, at])
                top = value.astype(jnp.bfloat16)
                high[at] = top
                low[at] = (value - top.astype(F32)).astype(jnp.bfloat16)
                return carry

            lax.fori_loop(0, 4, split, 0)

            def product(i, carry):
                at = pl.ds(pl.multiple_of(i * BLK, BLK), BLK)
                value = m[a, at]
                top = value.astype(jnp.bfloat16)
                rest = (value - top.astype(F32)).astype(jnp.bfloat16)
                right = high[...]
                total = jnp.dot(rest, right, preferred_element_type=F32)
                total += jnp.dot(top, low[...], preferred_element_type=F32)
                total += jnp.dot(top, right, preferred_element_type=F32)
                rows = lax.broadcasted_iota(jnp.int32, (BLK, NB), 0) + i * BLK
                cols = lax.broadcasted_iota(jnp.int32, (BLK, NB), 1)
                total = total * sign.astype(F32)
                halved = jnp.where(rows > cols, total, jnp.where(rows == cols, 0.5 * total, 0.0))
                total = jnp.where(half > 0, halved, total)
                m[to, at] = jnp.where(keep > 0, m[c, at], 0.0) + total
                return carry

            lax.fori_loop(0, NB // BLK, product, 0)

        @pl.when(kind == 1)
        def _():
            def turn(i, carry):
                at = pl.ds(pl.multiple_of(i * 128, 128), 128)
                m[to, :, at] = m[a, at].T + jnp.where(keep > 0, m[a, :, at], 0.0)
                return carry

            lax.fori_loop(0, 4, turn, 0)

        return carry

    lax.fori_loop(0, len(PLAN), op, 0)
    p = jnp.minimum(row, 2)
    half = pl.ds(pl.multiple_of(col % 2 * 256, 256), 256)
    for j in range(3):
        q_ref[:, j * NB : (j + 1) * NB] = m[pick_ref[p, j], half]
        z_ref[j] = m[pick_ref[p, 3 + j]]


def chain(blocks, near, inv):
    smem = pl.BlockSpec(memory_space=pltpu.SMEM)
    return pl.pallas_call(
        chain_kernel,
        out_shape=(
            jax.ShapeDtypeStruct((256, 3 * NB), F32),
            jax.ShapeDtypeStruct((3, NB, NB), F32),
        ),
        in_specs=[smem, smem, VM, VM, VM],
        out_specs=(VM, VM),
        scratch_shapes=[
            pltpu.VMEM((30, NB, NB), F32),
            pltpu.VMEM((NB, NB), jnp.bfloat16),
            pltpu.VMEM((NB, NB), jnp.bfloat16),
        ],
        compiler_params=pltpu.CompilerParams(vmem_limit_bytes=56 << 20),
    )(jnp.array(PLAN, jnp.int32), jnp.array(PICKS, jnp.int32), blocks, near, inv)


def shards(factor, cot):
    row = lax.axis_index("row")
    col = lax.axis_index("col")
    core = col % 2
    strips, blocks, other_half = spread(factor, cot)
    blocks = blocks.reshape(2, 3, NB, NB)
    l = {
        0: blocks[0, 0], 10: blocks[0, 1], 20: blocks[0, 2],
        11: blocks[1, 0], 21: blocks[1, 1], 22: blocks[1, 2],
    }
    inv = invert(jnp.stack([l[0], l[11], l[22]]))
    my_half = lax.dynamic_slice(cot, (core * 256, 0), (256, 1024))
    g6 = jnp.where(core == 0, my_half, other_half)
    g7 = jnp.where(core == 0, other_half, my_half)
    s2 = dot(g7[:, NB:], inv[2])
    s1 = dot(g7[:, :NB] - dot(s2, l[21]), inv[1])
    s0 = dot(g6[:, NB:] - dot(s2, l[20]) - dot(s1, l[10]), inv[0])
    solved, strips = along_spread(jnp.concatenate([s0, s1, s2], axis=1), factor, strips)
    lower_rows = row >= NP
    part = jnp.where(lower_rows, -dot_t(solved, factor), 0.0).reshape(3, NB, 1024)
    which = lax.broadcasted_iota(jnp.int32, (3, 1, 1), 0)
    part = jnp.where(which == row, cot[None], part)
    near = reduce_rows(part).reshape(2, 3, NB, NB)
    mixed_half, z = chain(blocks.reshape(6, NB, NB), near.reshape(6, NB, NB), inv)
    mixed, far = along_reduce(mixed_half, part)
    factor_rows = jnp.where(lower_rows, solved, mixed)
    even = core == 0

    def by_row(zero, one, two):
        return jnp.where(row == 0, zero, jnp.where(row == 1, one, two))

    total_left = by_row(
        far[0], jnp.where(even, far[1], near[1, 0]), jnp.where(even, far[2], near[1, 1])
    )
    total_right = by_row(
        jnp.where(even, near[0, 0], far[1]),
        jnp.where(even, near[0, 1], far[2]),
        jnp.where(even, near[0, 2], near[1, 2]),
    )
    start = jnp.where(
        lower_rows, cot, jnp.concatenate([total_left, total_right], axis=1)
    )
    out = start - dot(factor_rows, strips)
    last6 = jnp.where(lower_rows, solved[:, :NB], z[0])
    left7 = jnp.where(
        lower_rows, solved[:, NB:1024], jnp.where(row == 0, cot[:, :NB], z[1])
    )
    right7 = jnp.where(
        lower_rows, solved[:, 1024:], jnp.where(row == 2, z[2], cot[:, NB:])
    )
    left = jnp.where(col == 7, left7, out[:, :NB])
    right = jnp.where(col == 7, right7, jnp.where(col == 6, last6, out[:, NB:]))
    return jnp.concatenate([left, right], axis=1)


def solution(mesh):
    placed = (P("row", "col"), P("row", "col"))
    return jax.shard_map(
        shards, mesh=mesh, in_specs=placed, out_specs=P("row", "col"), check_vma=False
    )
```

```python
import jax
import jax.numpy as jnp
from jax import lax
from jax.experimental import pallas as pl
from jax.experimental.pallas import tpu as pltpu
from jax.sharding import PartitionSpec as P

NB = 512
NP = 3
MESH = pl.DeviceIdType.MESH
HI = lax.Precision.HIGHEST
MID = lax.Precision.HIGH
F32 = jnp.float32


def dot(a, b, precision=MID):
    return jnp.dot(a, b, precision=precision, preferred_element_type=F32)


def dot_t(a, b, precision=MID):
    return lax.dot_general(
        a, b, (((0,), (0,)), ((), ())), precision=precision, preferred_element_type=F32
    )


def place():
    row = lax.axis_index("row")
    col = lax.axis_index("col")
    return row // 4, row % 4, col // 2, col % 2


def remote(src, dst, send, recv, x, y, z, core):
    return pltpu.make_async_remote_copy(
        src_ref=src,
        dst_ref=dst,
        send_sem=send,
        recv_sem=recv,
        device_id=(x * 4 + y, z * 2 + core),
        device_id_type=MESH,
    )


def greet(devices):
    barrier = pltpu.get_barrier_semaphore()
    for x, y, z, core in devices:
        pl.semaphore_signal(
            barrier, inc=1, device_id=(x * 4 + y, z * 2 + core), device_id_type=MESH
        )
    pl.semaphore_wait(barrier, len(devices))


def plane_and_peer(x, y, z, core):
    out = []
    for dx in range(4):
        for dy in range(4):
            if dx or dy:
                out.append(((x + dx) % 4, (y + dy) % 4, z, core))
    return out + [(x, y, z, 1 - core)]


CH = 8
CR = 128 // CH
LEFT, RIGHT = pl.ds(0, NB), pl.ds(NB, NB)
ROWS = (pl.ds(0, 16), pl.ds(16, 16))
PAIR = (pl.ds(0, 2), pl.ds(2, 2))


def unit(part, u, core):
    if part == 0:
        p = u + core if u < 2 else 2
        off = NB * (1 - core) if u < 2 else NB
    else:
        p = u - core if u >= 1 else 0
        off = NB * core if u >= 1 else 0
    if isinstance(off, int):
        return p, pl.ds(off, NB)
    return p, pl.ds(pl.multiple_of(off, NB), NB)


def line(order, x, y, d):
    return ((x + d) % 4, y) if order == 0 else (x, (y + d) % 4)


def spread_steps(part, own, strips, sems):
    scat_s, scat_r, one_s, one_r, two_s, two_r, loc = sems
    x, y, z, core = place()
    units = [unit(part, u, core) for u in range(NP)]

    def piece(ref, u, px, py):
        p, cols = units[u]
        if ref is own:
            return own.at[px, py, :, cols]
        return strips.at[p, px, py, :, cols]

    def scatter(u, d):
        tx, ty = (x + d // 4) % 4, (y + d % 4) % 4
        return remote(
            piece(own, u, tx, ty), piece(strips, u, tx, ty),
            scat_s.at[u, d], scat_r.at[u], tx, ty, z, core,
        )

    def keep(u):
        return pltpu.make_async_copy(piece(own, u, x, y), piece(strips, u, x, y), loc.at[u])

    roots = [(x == 0) & (y == units[u][0]) for u in range(NP)]
    for u in range(NP):

        @pl.when(roots[u])
        def _():
            keep(u).start()
            for d in range(15, 0, -1):
                scatter(u, d).start()

    yield

    for u in range(NP):

        @pl.when(roots[u])
        def _():
            keep(u).wait()

        @pl.when(jnp.logical_not(roots[u]))
        def _():
            here = piece(strips, u, x, y)
            remote(here, here, scat_s.at[u, 0], scat_r.at[u], x, y, z, 1 - core).wait_recv()

    first = []
    for u in range(NP):
        p, cols = units[u]
        for order in range(2):
            for d in range(1, 4):
                here = strips.at[p, x, y, ROWS[order], cols]
                tx, ty = line(order, x, y, d)
                first.append(
                    remote(
                        here, here, one_s.at[order, u, d], one_r.at[order, u, d],
                        tx, ty, z, core,
                    )
                )
    for copy in first:
        copy.start()
    yield

    for copy in first:
        copy.wait_recv()

    def block(order, u, at, pick):
        p, cols = units[u]
        if order == 0:
            return strips.at[p, pick, (y + at) % 4, ROWS[0], cols]
        return strips.at[p, (x + at) % 4, pick, ROWS[1], cols]

    def second(order, u, kind):
        whole = pl.ds(0, 4)
        at, pick, d = (
            (0, whole, 1), (0, whole, 3), (3, PAIR[0], 1), (1, PAIR[1], 3)
        )[kind]
        ref = block(order, u, at, pick)
        tx, ty = line(1 - order, x, y, d)
        return remote(
            ref, ref, two_s.at[order, u, kind], two_r.at[order, u, kind], tx, ty, z, core
        )

    def arrival(order, u, kind):
        whole = pl.ds(0, 4)
        at, pick = ((3, whole), (1, whole), (2, PAIR[0]), (2, PAIR[1]))[kind]
        ref = block(order, u, at, pick)
        return remote(
            ref, ref, two_s.at[order, u, kind], two_r.at[order, u, kind], x, y, z, 1 - core
        )

    every = [(order, u) for u in range(NP) for order in range(2)]
    for order, u in every:
        for kind in (0, 1):
            second(order, u, kind).start()
    yield

    for order, u in every:
        for kind in (0, 1):
            arrival(order, u, kind).wait_recv()
            second(order, u, kind + 2).start()
    yield

    for order, u in every:
        for kind in (2, 3):
            arrival(order, u, kind).wait_recv()
    yield

    for u in range(NP):

        @pl.when(roots[u])
        def _():
            for d in range(1, 16):
                scatter(u, d).wait_send()

    for copy in first:
        copy.wait_send()
    for order, u in every:
        for kind in range(4):
            second(order, u, kind).wait_send()
    yield


AHEAD = 3


def along_steps(src, out, sems, used):
    ring_s, ring_r, peer_s, peer_r = sems
    x, y, z, core = place()
    up, down = (z + 1) % 4, (z + 3) % 4
    positions = (up, 3 - z)
    targets = (up, down)
    source = used & (z == 3)

    def chunk(owner, way, step):
        return out.at[pl.ds(owner, 1), way, step]

    def ring(way, step, block):
        mine = chunk(core, way, step)
        return remote(
            block, mine, ring_s.at[way, step], ring_r.at[way, step], x, y, targets[way], core
        )

    def across(way, step, block):
        mine = chunk(core, way, step)
        return remote(
            block, mine, peer_s.at[way, step], peer_r.at[way, step], x, y, z, 1 - core
        )

    def issue(step):
        for way in range(2):
            ring(way, step, src.at[:, way, step]).start()
        for way in range(2):
            across(way, step, src.at[:, way, step]).start()

    @pl.when(source)
    def _():
        for step in range(AHEAD):
            issue(step)
        out[pl.ds(core, 1)] = src[...]

    yield
    for tick in range(CH + 2):
        if tick + AHEAD < CH:

            @pl.when(source)
            def _():
                for way in range(2):
                    ring(way, tick, src.at[:, way, tick]).wait_send()
                issue(tick + AHEAD)

        for way in range(2):
            for pos in range(1, 4):
                step = tick - (pos - 1)
                if not 0 <= step < CH:
                    continue

                @pl.when(used & (positions[way] == pos))
                def _():
                    mine = chunk(core, way, step)
                    ring(way, step, mine).wait_recv()
                    if pos < 3:
                        ring(way, step, mine).start()
                    across(way, step, mine).start()

        yield

    @pl.when(used)
    def _():
        for step in range(CH):
            for way in range(2):
                mine, other = chunk(core, way, step), chunk(1 - core, way, step)
                remote(
                    mine, other, peer_s.at[way, step], peer_r.at[way, step],
                    x, y, z, 1 - core,
                ).wait()
                left = positions[way] < 3
                if step + AHEAD < CH:
                    left = left & (z != 3)

                @pl.when(left)
                def _():
                    ring(way, step, mine).wait_send()

    yield


def reduce_steps(part, wide, src, out, bufs, sems):
    got, acc, tot, got2, fin = bufs
    one_s, one_r, two_s, two_r, g_s, g_r, loc = sems
    x, y, z, core = place()
    units = [unit(part, u, core) for u in range(NP)]
    every = [(order, u) for u in range(NP) for order in range(2)]

    def share(order, u, at, pick):
        p, cols = units[u]
        if order == 0:
            return p, (x + at) % 4, pick, ROWS[0], cols
        return p, pick, (y + at) % 4, ROWS[1], cols

    def one(order, u, kind, way):
        step = 1 if way == 0 else 3
        if kind == 0:
            ref = src.at[share(order, u, 2, PAIR[way])]
        elif kind == 1:
            ref = src.at[share(order, u, step, PAIR[1 - way])]
        else:
            ref = acc.at[order, u, way]
        tx, ty = line(order, x, y, step)
        return remote(
            ref, got.at[order, u, kind, way],
            one_s.at[order, u, kind * 2 + way], one_r.at[order, u, kind * 2 + way],
            tx, ty, z, core,
        )

    for kind in (0, 1):
        for order, u in every:
            for way in range(2):
                one(order, u, kind, way).start()
    yield

    for order, u in every:
        for way in range(2):
            one(order, u, 0, way).wait_recv()
            step = 1 if way == 0 else 3
            acc[order, u, way] = (
                src[share(order, u, step, PAIR[way])] + got[order, u, 0, way]
            )
            one(order, u, 2, way).start()
    yield

    def two(order, u, d):
        tx, ty = line(1 - order, x, y, d)
        index = ty if order == 0 else tx
        return remote(
            tot.at[order, u, index], got2.at[order, u, d - 1],
            two_s.at[order, u, d], two_r.at[order, u, d], tx, ty, z, core,
        )

    for order, u in every:
        for kind in (1, 2):
            for way in range(2):
                one(order, u, kind, way).wait_recv()
        for half in range(2):
            base = src[share(order, u, 0, PAIR[half])]
            tot[order, u, PAIR[half]] = base + (
                got[order, u, 2, half] + got[order, u, 1, 1 - half]
            )
        for d in range(1, 4):
            two(order, u, d).start()
    yield

    for order, u in every:
        for d in range(1, 4):
            two(order, u, d).wait_recv()
        here = y if order == 0 else x
        fin[u, ROWS[order]] = (tot[order, u, here] + got2[order, u, 0]) + (
            got2[order, u, 1] + got2[order, u, 2]
        )

    def slot(u, px, py):
        return out.at[core, u, px, py] if wide else out.at[u, px, py]

    def send(root, u):
        return remote(
            fin.at[u], slot(u, x, y), g_s.at[root, u], g_r.at[u, x * 4 + y], 0, root, z, core
        )

    def keep(u):
        return pltpu.make_async_copy(fin.at[u], slot(u, x, y), loc.at[u])

    def cases():
        for root in range(NP):
            at_root = (x == 0) & (y == root)
            for u in range(NP):
                flag = units[u][0] == root
                if wide:
                    flag = flag | (z == 3)
                yield root, u, flag & at_root, flag & jnp.logical_not(at_root)

    for root, u, local, away in cases():

        @pl.when(away)
        def _():
            send(root, u).start()

        @pl.when(local)
        def _():
            keep(u).start()

    yield

    for root, u, local, away in cases():

        @pl.when(away)
        def _():
            send(root, u).wait_send()

        @pl.when(local)
        def _():
            keep(u).wait()
            for d in range(1, 16):
                sx, sy = (x + d // 4) % 4, (y + d % 4) % 4
                remote(
                    fin.at[u], slot(u, sx, sy), g_s.at[root, u], g_r.at[u, sx * 4 + sy],
                    x, y, z, 1 - core,
                ).wait_recv()

    for order, u in every:
        for kind in range(3):
            for way in range(2):
                one(order, u, kind, way).wait_send()
        for d in range(1, 4):
            two(order, u, d).wait_send()
    yield


DMA = pltpu.SemaphoreType.DMA
SPREAD_SEMS = [
    DMA((3, 16)), DMA((3,)), DMA((2, 3, 4)), DMA((2, 3, 4)), DMA((2, 3, 4)), DMA((2, 3, 4)),
    DMA((3,)),
]
ALONG_SEMS = [DMA((2, CH))] * 4
REDUCE_BUFS = [
    pltpu.VMEM((2, 3, 3, 2, 2, 16, NB), F32),
    pltpu.VMEM((2, 3, 2, 2, 16, NB), F32),
    pltpu.VMEM((2, 3, 4, 16, NB), F32),
    pltpu.VMEM((2, 3, 3, 16, NB), F32),
    pltpu.VMEM((3, 32, NB), F32),
]
REDUCE_SEMS = [
    DMA((2, 3, 6)), DMA((2, 3, 6)), DMA((2, 3, 4)), DMA((2, 3, 4)), DMA((3, 3)), DMA((3, 16)),
    DMA((3,)),
]
VM = pl.BlockSpec(memory_space=pltpu.VMEM)
ANY = pl.BlockSpec(memory_space=pl.ANY)


def drive(*plan):
    for steps, count in plan:
        for _ in range(count):
            next(steps)


def spread_kernel(own, cot, strips, blocks, half, *sems):
    x, y, z, core = place()
    greet(plane_and_peer(x, y, z, core))
    ex_s, ex_r, loc = sems[-3:]
    half_copy = remote(
        cot.at[pl.ds(256 * (1 - core), 256)], half, ex_s.at[3], ex_r.at[3], x, y, z, 1 - core
    )
    half_copy.start()
    steps = spread_steps(0, own, strips, sems[:7])
    drive((steps, 5))
    for u in range(NP):
        p, cols = unit(0, u, core)
        ref = strips.at[p, :, :, :, cols]
        remote(
            ref, blocks.at[core, u], ex_s.at[u], ex_r.at[u], x, y, z, 1 - core
        ).start()
        pltpu.make_async_copy(ref, blocks.at[core, u], loc.at[u]).start()
    drive((steps, 1))
    for u in range(NP):
        p, cols = unit(0, u, core)
        ref = strips.at[p, :, :, :, cols]
        pltpu.make_async_copy(ref, blocks.at[core, u], loc.at[u]).wait()
        remote(
            ref, blocks.at[1 - core, u], ex_s.at[u], ex_r.at[u], x, y, z, 1 - core
        ).wait()
    half_copy.wait()


def comm(collective_id, mib):
    return pltpu.CompilerParams(
        collective_id=collective_id, has_side_effects=True, vmem_limit_bytes=mib << 20
    )


def spread(factor, cot):
    return pl.pallas_call(
        spread_kernel,
        out_shape=(
            jax.ShapeDtypeStruct((3, 4, 4, 32, 1024), F32),
            jax.ShapeDtypeStruct((2, 3, 4, 4, 32, NB), F32),
            jax.ShapeDtypeStruct((256, 1024), F32),
        ),
        in_specs=[ANY, ANY],
        out_specs=(ANY, VM, VM),
        scratch_shapes=SPREAD_SEMS + [DMA((4,)), DMA((4,)), DMA((3,))],
        compiler_params=comm(0, 32),
    )(factor.reshape(4, 4, 32, 1024), cot)


def with_z(x, y, z, core):
    return plane_and_peer(x, y, z, core) + [
        (x, y, (z + 1) % 4, core), (x, y, (z + 3) % 4, core)
    ]


def along_spread_kernel(src, own, _, out, strips, *sems):
    greet(with_z(*place()))
    a = along_steps(src, out, sems[7:], lax.axis_index("row") >= NP)
    s = spread_steps(1, own, strips, sems[:7])
    drive((s, 1), (a, 1), (a, 2), (s, 1), (a, 2), (s, 1), (a, 4), (s, 1), (a, 2), (a, 1), (s, 2))


def along_spread(half, factor, strips):
    out, strips = pl.pallas_call(
        along_spread_kernel,
        out_shape=(
            jax.ShapeDtypeStruct((2, 2, CH, CR, 1536), F32),
            jax.ShapeDtypeStruct((3, 4, 4, 32, 1024), F32),
        ),
        in_specs=[VM, ANY, ANY],
        out_specs=(VM, ANY),
        scratch_shapes=SPREAD_SEMS + ALONG_SEMS,
        input_output_aliases={2: 1},
        compiler_params=comm(1, 16),
    )(half.reshape(1, 2, CH, CR, 1536), factor.reshape(4, 4, 32, 1024), strips)
    return out.reshape(512, 1536), strips.reshape(1536, 1024)


def reduce_kernel(src, out, *rest):
    x, y, z, core = place()
    greet(plane_and_peer(x, y, z, core))
    bufs, sems = rest[:5], rest[5:]
    ex_s, ex_r = sems[-2:]
    steps = reduce_steps(0, True, src, out, bufs, sems[:7])
    drive((steps, 5))

    @pl.when((x == 0) & (y < NP) & (z == 3))
    def _():
        remote(
            out.at[core], out.at[core], ex_s.at[0], ex_r.at[0], x, y, z, 1 - core
        ).start()
        remote(
            out.at[core], out.at[1 - core], ex_s.at[0], ex_r.at[0], x, y, z, 1 - core
        ).wait()


def reduce_rows(part):
    return pl.pallas_call(
        reduce_kernel,
        out_shape=jax.ShapeDtypeStruct((2, 3, 4, 4, 32, NB), F32),
        in_specs=[VM],
        out_specs=VM,
        scratch_shapes=REDUCE_BUFS + REDUCE_SEMS + [DMA((1,)), DMA((1,))],
        compiler_params=comm(2, 32),
    )(part.reshape(3, 4, 4, 32, 1024))


def along_reduce_kernel(src, part, out, rest_out, *rest):
    greet(with_z(*place()))
    bufs, sems = rest[:5], rest[5:]
    a = along_steps(src, out, sems[7:], lax.axis_index("row") < NP)
    r = reduce_steps(1, False, part, rest_out, bufs, sems[:7])
    drive((a, 1), (r, 1), (a, 3), (r, 1), (a, 3), (r, 1), (a, 1), (r, 1), (a, 3), (a, 1), (r, 1))


def along_reduce(half, part):
    out, rest_out = pl.pallas_call(
        along_reduce_kernel,
        out_shape=(
            jax.ShapeDtypeStruct((2, 2, CH, CR, 1536), F32),
            jax.ShapeDtypeStruct((3, 4, 4, 32, NB), F32),
        ),
        in_specs=[VM, VM],
        out_specs=(VM, VM),
        scratch_shapes=REDUCE_BUFS + REDUCE_SEMS + ALONG_SEMS,
        compiler_params=comm(3, 40),
    )(half.reshape(1, 2, CH, CR, 1536), part.reshape(3, 4, 4, 32, 1024))
    return out.reshape(512, 1536), rest_out.reshape(3, NB, NB)


BS = 128


def invert_kernel(d_ref, o_ref):
    rows = lax.broadcasted_iota(jnp.int32, (BS, BS), 0)
    cols = lax.broadcasted_iota(jnp.int32, (BS, BS), 1)
    diag = rows == cols
    for block in range(NP * (NB // BS)):
        which, at = block // (NB // BS), pl.ds(block % (NB // BS) * BS, BS)
        base = d_ref[which, at, at]
        scale = jnp.sum(jnp.where(diag, base, 0.0), axis=1, keepdims=True)
        o_ref[which, at, at] = jnp.where(diag, 1.0 / scale, 0.0)

    def level(step, carry):
        pick = ((rows >> (step + 1)) == (cols >> (step + 1))) & (
            ((rows >> step) & 1) > ((cols >> step) & 1)
        )
        for block in range(NP * (NB // BS)):
            which, at = block // (NB // BS), pl.ds(block % (NB // BS) * BS, BS)
            have = o_ref[which, at, at]
            below = jnp.where(pick, d_ref[which, at, at], 0.0)
            o_ref[which, at, at] = have - dot(dot(have, below, HI), have, HI)
        return carry

    lax.fori_loop(0, 7, level, 0)
    size = BS
    while size < NB:
        for which in range(NP):
            for base in range(0, NB, 2 * size):
                up, down = pl.ds(base, size), pl.ds(base + size, size)
                corner = dot(
                    dot(o_ref[which, down, down], d_ref[which, down, up], HI),
                    o_ref[which, up, up], HI,
                )
                o_ref[which, down, up] = -corner
                o_ref[which, up, down] = jnp.zeros((size, size), F32)
        size *= 2


def invert(blocks):
    vm = pl.BlockSpec(memory_space=pltpu.VMEM)
    return pl.pallas_call(
        invert_kernel,
        out_shape=jax.ShapeDtypeStruct((NP, NB, NB), F32),
        in_specs=[vm],
        out_specs=vm,
        compiler_params=pltpu.CompilerParams(vmem_limit_bytes=16 << 20),
    )(blocks)


def plan():
    rows = []
    l00, l10, l20, l11, l21, l22, t00, t10, t20, t11, t21, t22, i0, i1, i2 = range(15)
    w, p, q, a2, y2, s21, s21t, a1, y1, s20, s10, s20t, s10t, a0, y0 = range(15, 30)

    def mm(a, b, to, tril=0, half=0):
        rows.append((0, a, b, to, to, tril, 0, 1, half))

    def take(a, b, to):
        rows.append((0, a, b, to, to, 0, 1, -1, 0))

    def turn(a, to, add=0):
        rows.append((1, a, a, a, to, 0, add, 1, 0))

    def adjoint(l, i, t, a, y):
        turn(l, w)
        mm(w, t, p, tril=1, half=1)
        turn(i, w)
        mm(w, p, q)
        mm(q, i, a, half=1)
        turn(a, y, add=1)

    adjoint(l22, i2, t22, a2, y2)
    take(y2, l21, t21)
    take(y2, l20, t20)
    mm(t21, i1, s21)
    turn(s21, s21t)
    take(s21t, l21, t11)
    take(s21t, l20, t10)
    adjoint(l11, i1, t11, a1, y1)
    take(y1, l10, t10)
    take(s21, l10, t20)
    mm(t20, i0, s20)
    mm(t10, i0, s10)
    turn(s20, s20t)
    turn(s10, s10t)
    take(s20t, l20, t00)
    take(s10t, l10, t00)
    adjoint(l00, i0, t00, a0, y0)
    coupling = ((y0, s10t, s20t), (s10, y1, s21t), (s20, s21, y2))
    result = ((a0, a0, a0), (s10, a1, a1), (s20, s21, a2))
    return rows, [x + y for x, y in zip(coupling, result)]


PLAN, PICKS = plan()
BLK = 256


def chain_kernel(plan_ref, pick_ref, l_ref, t_ref, i_ref, q_ref, z_ref, m, high, low):
    row, col = lax.axis_index("row"), lax.axis_index("col")
    for n in range(6):
        m[n] = l_ref[n]
        m[6 + n] = t_ref[n]
    for n in range(3):
        m[12 + n] = i_ref[n]

    def op(n, carry):
        kind, a, b, c = (plan_ref[n, j] for j in range(4))
        to, tril, keep, sign, half = (plan_ref[n, j] for j in range(4, 9))

        @pl.when(kind == 0)
        def _():
            def split(i, carry):
                at = pl.ds(pl.multiple_of(i * 128, 128), 128)
                rows = lax.broadcasted_iota(jnp.int32, (128, NB), 0) + i * 128
                cols = lax.broadcasted_iota(jnp.int32, (128, NB), 1)
                value = jnp.where((cols - rows) * tril > 0, 0.0, m[b, at])
                top = value.astype(jnp.bfloat16)
                high[at] = top
                low[at] = (value - top.astype(F32)).astype(jnp.bfloat16)
                return carry

            lax.fori_loop(0, 4, split, 0)

            def product(i, carry):
                at = pl.ds(pl.multiple_of(i * BLK, BLK), BLK)
                value = m[a, at]
                top = value.astype(jnp.bfloat16)
                rest = (value - top.astype(F32)).astype(jnp.bfloat16)
                right = high[...]
                total = jnp.dot(rest, right, preferred_element_type=F32)
                total += jnp.dot(top, low[...], preferred_element_type=F32)
                total += jnp.dot(top, right, preferred_element_type=F32)
                rows = lax.broadcasted_iota(jnp.int32, (BLK, NB), 0) + i * BLK
                cols = lax.broadcasted_iota(jnp.int32, (BLK, NB), 1)
                total = total * sign.astype(F32)
                halved = jnp.where(rows > cols, total, jnp.where(rows == cols, 0.5 * total, 0.0))
                total = jnp.where(half > 0, halved, total)
                m[to, at] = jnp.where(keep > 0, m[c, at], 0.0) + total
                return carry

            lax.fori_loop(0, NB // BLK, product, 0)

        @pl.when(kind == 1)
        def _():
            def turn(i, carry):
                at = pl.ds(pl.multiple_of(i * 128, 128), 128)
                m[to, :, at] = m[a, at].T + jnp.where(keep > 0, m[a, :, at], 0.0)
                return carry

            lax.fori_loop(0, 4, turn, 0)

        return carry

    lax.fori_loop(0, len(PLAN), op, 0)
    p = jnp.minimum(row, 2)
    half = pl.ds(pl.multiple_of(col % 2 * 256, 256), 256)
    for j in range(3):
        q_ref[:, j * NB : (j + 1) * NB] = m[pick_ref[p, j], half]
        z_ref[j] = m[pick_ref[p, 3 + j]]


def chain(blocks, near, inv):
    smem = pl.BlockSpec(memory_space=pltpu.SMEM)
    return pl.pallas_call(
        chain_kernel,
        out_shape=(
            jax.ShapeDtypeStruct((256, 3 * NB), F32),
            jax.ShapeDtypeStruct((3, NB, NB), F32),
        ),
        in_specs=[smem, smem, VM, VM, VM],
        out_specs=(VM, VM),
        scratch_shapes=[
            pltpu.VMEM((30, NB, NB), F32),
            pltpu.VMEM((NB, NB), jnp.bfloat16),
            pltpu.VMEM((NB, NB), jnp.bfloat16),
        ],
        compiler_params=pltpu.CompilerParams(vmem_limit_bytes=56 << 20),
    )(jnp.array(PLAN, jnp.int32), jnp.array(PICKS, jnp.int32), blocks, near, inv)


def finish_kernel(cot, solved, mixed, strips, far, near, z, out, high, low, f_high, f_low):
    row, col = lax.axis_index("row"), lax.axis_index("col")
    core = col % 2
    r = jnp.minimum(row, 2)
    lower_rows = row >= NP

    @pl.when(col < 7)
    def _():
        def split(i, carry):
            at = pl.ds(pl.multiple_of(i * 128, 128), 128)
            value = jnp.where(lower_rows, solved[at], mixed[at])
            top = value.astype(jnp.bfloat16)
            f_high[at] = top
            f_low[at] = (value - top.astype(F32)).astype(jnp.bfloat16)
            return carry

        lax.fori_loop(0, 4, split, 0)

    for h in range(2):
        cols = pl.ds(h * NB, NB)
        if h == 0:
            use_far = (core == 0) | (row == 0)
            at_far = r * (1 - core)
            at_near = jnp.maximum(r - core, 0)
            plain = col < 7
        else:
            use_far = (core == 1) & (row < 2)
            at_far = jnp.minimum(r + 1, 2)
            at_near = r * (1 - core) + 2 * core
            plain = col < 6

        @pl.when(plain)
        def _():
            def begin(i, carry):
                at = pl.ds(pl.multiple_of(i * 128, 128), 128)
                total = jnp.where(use_far, far[at_far, at], near[core, at_near, at])
                out[at, cols] = jnp.where(lower_rows, cot[at, cols], total)
                return carry

            lax.fori_loop(0, 4, begin, 0)

            def deep(k, carry):
                def split(i, carry):
                    at = pl.ds(pl.multiple_of(i * 128, 128), 128)
                    from_at = pl.ds(pl.multiple_of(k * NB + i * 128, 128), 128)
                    value = strips[from_at, cols]
                    top = value.astype(jnp.bfloat16)
                    high[at] = top
                    low[at] = (value - top.astype(F32)).astype(jnp.bfloat16)
                    return carry

                lax.fori_loop(0, 4, split, 0)
                inner = pl.ds(pl.multiple_of(k * NB, NB), NB)

                def product(i, carry):
                    at = pl.ds(pl.multiple_of(i * BLK, BLK), BLK)
                    top, rest, right = f_high[at, inner], f_low[at, inner], high[...]
                    total = jnp.dot(rest, right, preferred_element_type=F32)
                    total += jnp.dot(top, low[...], preferred_element_type=F32)
                    total += jnp.dot(top, right, preferred_element_type=F32)
                    out[at, cols] = out[at, cols] - total
                    return carry

                lax.fori_loop(0, NB // BLK, product, 0)
                return carry

            lax.fori_loop(0, NP, deep, 0)

        @pl.when(jnp.logical_not(plain))
        def _():
            def move(i, carry):
                at = pl.ds(pl.multiple_of(i * 128, 128), 128)
                if h == 0:
                    upper = jnp.where(row == 0, cot[at, cols], z[1, at])
                    out[at, cols] = jnp.where(lower_rows, solved[at, NB : 2 * NB], upper)
                else:
                    upper = jnp.where(row == 2, z[2, at], cot[at, cols])
                    last = jnp.where(lower_rows, solved[at, 2 * NB :], upper)
                    first = jnp.where(lower_rows, solved[at, :NB], z[0, at])
                    out[at, cols] = jnp.where(col == 7, last, first)
                return carry

            lax.fori_loop(0, 4, move, 0)


def finish(cot, solved, mixed, strips, far, near, z):
    return pl.pallas_call(
        finish_kernel,
        out_shape=jax.ShapeDtypeStruct((NB, 2 * NB), F32),
        in_specs=[VM] * 7,
        out_specs=VM,
        scratch_shapes=[
            pltpu.VMEM((NB, NB), jnp.bfloat16),
            pltpu.VMEM((NB, NB), jnp.bfloat16),
            pltpu.VMEM((NB, 3 * NB), jnp.bfloat16),
            pltpu.VMEM((NB, 3 * NB), jnp.bfloat16),
        ],
        compiler_params=pltpu.CompilerParams(vmem_limit_bytes=40 << 20),
    )(cot, solved, mixed, strips, far, near, z)


def shards(factor, cot):
    row = lax.axis_index("row")
    col = lax.axis_index("col")
    core = col % 2
    strips, blocks, other_half = spread(factor, cot)
    blocks = blocks.reshape(2, 3, NB, NB)
    l = {
        0: blocks[0, 0], 10: blocks[0, 1], 20: blocks[0, 2],
        11: blocks[1, 0], 21: blocks[1, 1], 22: blocks[1, 2],
    }
    inv = invert(jnp.stack([l[0], l[11], l[22]]))
    my_half = lax.dynamic_slice(cot, (core * 256, 0), (256, 1024))
    g6 = jnp.where(core == 0, my_half, other_half)
    g7 = jnp.where(core == 0, other_half, my_half)
    s2 = dot(g7[:, NB:], inv[2])
    s1 = dot(g7[:, :NB] - dot(s2, l[21]), inv[1])
    s0 = dot(g6[:, NB:] - dot(s2, l[20]) - dot(s1, l[10]), inv[0])
    solved, strips = along_spread(jnp.concatenate([s0, s1, s2], axis=1), factor, strips)
    lower_rows = row >= NP
    part = jnp.where(lower_rows, -dot_t(solved, factor), 0.0).reshape(3, NB, 1024)
    which = lax.broadcasted_iota(jnp.int32, (3, 1, 1), 0)
    part = jnp.where(which == row, cot[None], part)
    near = reduce_rows(part).reshape(2, 3, NB, NB)
    mixed_half, z = chain(blocks.reshape(6, NB, NB), near.reshape(6, NB, NB), inv)
    mixed, far = along_reduce(mixed_half, part)
    return finish(cot, solved, mixed, strips, far, near, z)


def solution(mesh):
    placed = (P("row", "col"), P("row", "col"))
    return jax.shard_map(
        shards, mesh=mesh, in_specs=placed, out_specs=P("row", "col"), check_vma=False
    )
```

```python
import jax
import jax.numpy as jnp
from jax import lax
from jax.experimental import pallas as pl
from jax.experimental.pallas import tpu as pltpu
from jax.sharding import PartitionSpec as P

NB = 512
NP = 3
MESH = pl.DeviceIdType.MESH
HI = lax.Precision.HIGHEST
MID = lax.Precision.HIGH
F32 = jnp.float32


def dot(a, b, precision=MID):
    return jnp.dot(a, b, precision=precision, preferred_element_type=F32)


def dot_t(a, b, precision=MID):
    return lax.dot_general(
        a, b, (((0,), (0,)), ((), ())), precision=precision, preferred_element_type=F32
    )


def place():
    row = lax.axis_index("row")
    col = lax.axis_index("col")
    return row // 4, row % 4, col // 2, col % 2


def remote(src, dst, send, recv, x, y, z, core):
    return pltpu.make_async_remote_copy(
        src_ref=src,
        dst_ref=dst,
        send_sem=send,
        recv_sem=recv,
        device_id=(x * 4 + y, z * 2 + core),
        device_id_type=MESH,
    )


def greet(devices):
    barrier = pltpu.get_barrier_semaphore()
    for x, y, z, core in devices:
        pl.semaphore_signal(
            barrier, inc=1, device_id=(x * 4 + y, z * 2 + core), device_id_type=MESH
        )
    pl.semaphore_wait(barrier, len(devices))


def plane_and_peer(x, y, z, core):
    out = []
    for dx in range(4):
        for dy in range(4):
            if dx or dy:
                out.append(((x + dx) % 4, (y + dy) % 4, z, core))
    return out + [(x, y, z, 1 - core)]


CH = 8
CR = 128 // CH
LEFT, RIGHT = pl.ds(0, NB), pl.ds(NB, NB)
ROWS = (pl.ds(0, 16), pl.ds(16, 16))
PAIR = (pl.ds(0, 2), pl.ds(2, 2))


def unit(part, u, core):
    if part == 0:
        p = u + core if u < 2 else 2
        off = NB * (1 - core) if u < 2 else NB
    else:
        p = u - core if u >= 1 else 0
        off = NB * core if u >= 1 else 0
    if isinstance(off, int):
        return p, pl.ds(off, NB)
    return p, pl.ds(pl.multiple_of(off, NB), NB)


def line(order, x, y, d):
    return ((x + d) % 4, y) if order == 0 else (x, (y + d) % 4)


def spread_steps(part, own, strips, sems):
    scat_s, scat_r, one_s, one_r, two_s, two_r, loc = sems
    x, y, z, core = place()
    units = [unit(part, u, core) for u in range(NP)]

    def piece(ref, u, px, py):
        p, cols = units[u]
        if ref is own:
            return own.at[px, py, :, cols]
        return strips.at[p, px, py, :, cols]

    def scatter(u, d):
        tx, ty = (x + d // 4) % 4, (y + d % 4) % 4
        return remote(
            piece(own, u, tx, ty), piece(strips, u, tx, ty),
            scat_s.at[u, d], scat_r.at[u], tx, ty, z, core,
        )

    def keep(u):
        return pltpu.make_async_copy(piece(own, u, x, y), piece(strips, u, x, y), loc.at[u])

    roots = [(x == 0) & (y == units[u][0]) for u in range(NP)]
    for u in range(NP):

        @pl.when(roots[u])
        def _():
            keep(u).start()
            for d in range(15, 0, -1):
                scatter(u, d).start()

    yield

    for u in range(NP):

        @pl.when(roots[u])
        def _():
            keep(u).wait()

        @pl.when(jnp.logical_not(roots[u]))
        def _():
            here = piece(strips, u, x, y)
            remote(here, here, scat_s.at[u, 0], scat_r.at[u], x, y, z, 1 - core).wait_recv()

    def at(u, px, py, rows):
        p, cols = units[u]
        return strips.at[p, px, py, rows, cols]

    for _ in share_steps(at, one_s, one_r, two_s, two_r):
        yield

    for u in range(NP):

        @pl.when(roots[u])
        def _():
            for d in range(1, 16):
                scatter(u, d).wait_send()

    yield


def share_steps(ref_at, one_s, one_r, two_s, two_r):
    x, y, z, core = place()
    every = [(order, u) for u in range(NP) for order in range(2)]
    first = []
    for order, u in every:
        for d in range(1, 4):
            here = ref_at(u, x, y, ROWS[order])
            tx, ty = line(order, x, y, d)
            first.append(
                remote(
                    here, here, one_s.at[order, u, d], one_r.at[order, u, d], tx, ty, z, core
                )
            )
    for copy in first:
        copy.start()
    yield

    for copy in first:
        copy.wait_recv()

    def block(order, u, at, pick):
        if order == 0:
            return ref_at(u, pick, (y + at) % 4, ROWS[0])
        return ref_at(u, (x + at) % 4, pick, ROWS[1])

    def second(order, u, kind):
        whole = pl.ds(0, 4)
        at, pick, d = (
            (0, whole, 1), (0, whole, 3), (3, PAIR[0], 1), (1, PAIR[1], 3)
        )[kind]
        ref = block(order, u, at, pick)
        tx, ty = line(1 - order, x, y, d)
        return remote(
            ref, ref, two_s.at[order, u, kind], two_r.at[order, u, kind], tx, ty, z, core
        )

    def arrival(order, u, kind):
        whole = pl.ds(0, 4)
        at, pick = ((3, whole), (1, whole), (2, PAIR[0]), (2, PAIR[1]))[kind]
        ref = block(order, u, at, pick)
        return remote(
            ref, ref, two_s.at[order, u, kind], two_r.at[order, u, kind], x, y, z, 1 - core
        )

    for order, u in every:
        for kind in (0, 1):
            second(order, u, kind).start()
    yield

    for order, u in every:
        for kind in (0, 1):
            arrival(order, u, kind).wait_recv()
            second(order, u, kind + 2).start()
    yield

    for order, u in every:
        for kind in (2, 3):
            arrival(order, u, kind).wait_recv()
    yield

    for copy in first:
        copy.wait_send()
    for order, u in every:
        for kind in range(4):
            second(order, u, kind).wait_send()
    yield


AHEAD = 3


def along_steps(src, out, sems, used):
    ring_s, ring_r, peer_s, peer_r = sems
    x, y, z, core = place()
    up, down = (z + 1) % 4, (z + 3) % 4
    positions = (up, 3 - z)
    targets = (up, down)
    source = used & (z == 3)

    def chunk(owner, way, step):
        return out.at[pl.ds(owner, 1), way, step]

    def ring(way, step, block):
        mine = chunk(core, way, step)
        return remote(
            block, mine, ring_s.at[way, step], ring_r.at[way, step], x, y, targets[way], core
        )

    def across(way, step, block):
        mine = chunk(core, way, step)
        return remote(
            block, mine, peer_s.at[way, step], peer_r.at[way, step], x, y, z, 1 - core
        )

    def issue(step):
        for way in range(2):
            ring(way, step, src.at[:, way, step]).start()
        for way in range(2):
            across(way, step, src.at[:, way, step]).start()

    @pl.when(source)
    def _():
        for step in range(AHEAD):
            issue(step)
        out[pl.ds(core, 1)] = src[...]

    yield
    for tick in range(CH + 2):
        if tick + AHEAD < CH:

            @pl.when(source)
            def _():
                for way in range(2):
                    ring(way, tick, src.at[:, way, tick]).wait_send()
                issue(tick + AHEAD)

        for way in range(2):
            for pos in range(1, 4):
                step = tick - (pos - 1)
                if not 0 <= step < CH:
                    continue

                @pl.when(used & (positions[way] == pos))
                def _():
                    mine = chunk(core, way, step)
                    ring(way, step, mine).wait_recv()
                    if pos < 3:
                        ring(way, step, mine).start()
                    across(way, step, mine).start()

        yield

    @pl.when(used)
    def _():
        for step in range(CH):
            for way in range(2):
                mine, other = chunk(core, way, step), chunk(1 - core, way, step)
                remote(
                    mine, other, peer_s.at[way, step], peer_r.at[way, step],
                    x, y, z, 1 - core,
                ).wait()
                left = positions[way] < 3
                if step + AHEAD < CH:
                    left = left & (z != 3)

                @pl.when(left)
                def _():
                    ring(way, step, mine).wait_send()

    yield


def reduce_steps(part, wide, src, out, bufs, sems):
    got, acc, tot, got2, fin = bufs
    one_s, one_r, two_s, two_r, g_s, g_r, loc = sems
    x, y, z, core = place()
    units = [unit(part, u, core) for u in range(NP)]
    every = [(order, u) for u in range(NP) for order in range(2)]

    def share(order, u, at, pick):
        p, cols = units[u]
        if order == 0:
            return p, (x + at) % 4, pick, ROWS[0], cols
        return p, pick, (y + at) % 4, ROWS[1], cols

    def one(order, u, kind, way):
        step = 1 if way == 0 else 3
        if kind == 0:
            ref = src.at[share(order, u, 2, PAIR[way])]
        elif kind == 1:
            ref = src.at[share(order, u, step, PAIR[1 - way])]
        else:
            ref = acc.at[order, u, way]
        tx, ty = line(order, x, y, step)
        return remote(
            ref, got.at[order, u, kind, way],
            one_s.at[order, u, kind * 2 + way], one_r.at[order, u, kind * 2 + way],
            tx, ty, z, core,
        )

    for kind in (0, 1):
        for order, u in every:
            for way in range(2):
                one(order, u, kind, way).start()
    yield

    for order, u in every:
        for way in range(2):
            one(order, u, 0, way).wait_recv()
            step = 1 if way == 0 else 3
            acc[order, u, way] = (
                src[share(order, u, step, PAIR[way])] + got[order, u, 0, way]
            )
            one(order, u, 2, way).start()
    yield

    def two(order, u, d):
        tx, ty = line(1 - order, x, y, d)
        index = ty if order == 0 else tx
        return remote(
            tot.at[order, u, index], got2.at[order, u, d - 1],
            two_s.at[order, u, d], two_r.at[order, u, d], tx, ty, z, core,
        )

    for order, u in every:
        for kind in (1, 2):
            for way in range(2):
                one(order, u, kind, way).wait_recv()
        for half in range(2):
            base = src[share(order, u, 0, PAIR[half])]
            tot[order, u, PAIR[half]] = base + (
                got[order, u, 2, half] + got[order, u, 1, 1 - half]
            )
        for d in range(1, 4):
            two(order, u, d).start()
    yield

    for order, u in every:
        for d in range(1, 4):
            two(order, u, d).wait_recv()
        here = y if order == 0 else x
        total = (tot[order, u, here] + got2[order, u, 0]) + (
            got2[order, u, 1] + got2[order, u, 2]
        )
        if wide:
            out[core, u, x, y, ROWS[order]] = total
        else:
            fin[u, ROWS[order]] = total

    def sends():
        for order, u in every:
            for kind in range(3):
                for way in range(2):
                    one(order, u, kind, way).wait_send()
            for d in range(1, 4):
                two(order, u, d).wait_send()

    if wide:

        def at(u, px, py, rows):
            return out.at[core, u, px, py, rows]

        for _ in share_steps(at, *wide):
            yield
        sends()
        yield
        return

    def slot(u, px, py):
        return out.at[u, px, py]

    def send(root, u):
        return remote(
            fin.at[u], slot(u, x, y), g_s.at[root, u], g_r.at[u, x * 4 + y], 0, root, z, core
        )

    def keep(u):
        return pltpu.make_async_copy(fin.at[u], slot(u, x, y), loc.at[u])

    def cases():
        for root in range(NP):
            at_root = (x == 0) & (y == root)
            for u in range(NP):
                flag = units[u][0] == root
                yield root, u, flag & at_root, flag & jnp.logical_not(at_root)

    for root, u, local, away in cases():

        @pl.when(away)
        def _():
            send(root, u).start()

        @pl.when(local)
        def _():
            keep(u).start()

    yield

    for root, u, local, away in cases():

        @pl.when(away)
        def _():
            send(root, u).wait_send()

        @pl.when(local)
        def _():
            keep(u).wait()
            for d in range(1, 16):
                sx, sy = (x + d // 4) % 4, (y + d % 4) % 4
                remote(
                    fin.at[u], slot(u, sx, sy), g_s.at[root, u], g_r.at[u, sx * 4 + sy],
                    x, y, z, 1 - core,
                ).wait_recv()

    sends()
    yield


DMA = pltpu.SemaphoreType.DMA
SPREAD_SEMS = [
    DMA((3, 16)), DMA((3,)), DMA((2, 3, 4)), DMA((2, 3, 4)), DMA((2, 3, 4)), DMA((2, 3, 4)),
    DMA((3,)),
]
ALONG_SEMS = [DMA((2, CH))] * 4
REDUCE_BUFS = [
    pltpu.VMEM((2, 3, 3, 2, 2, 16, NB), F32),
    pltpu.VMEM((2, 3, 2, 2, 16, NB), F32),
    pltpu.VMEM((2, 3, 4, 16, NB), F32),
    pltpu.VMEM((2, 3, 3, 16, NB), F32),
    pltpu.VMEM((3, 32, NB), F32),
]
REDUCE_SEMS = [
    DMA((2, 3, 6)), DMA((2, 3, 6)), DMA((2, 3, 4)), DMA((2, 3, 4)), DMA((3, 3)), DMA((3, 16)),
    DMA((3,)),
]
VM = pl.BlockSpec(memory_space=pltpu.VMEM)
ANY = pl.BlockSpec(memory_space=pl.ANY)


def drive(*plan):
    for steps, count in plan:
        for _ in range(count):
            next(steps)


def spread_kernel(own, cot, strips, blocks, half, *sems):
    x, y, z, core = place()
    greet(plane_and_peer(x, y, z, core))
    ex_s, ex_r, loc = sems[-3:]
    half_copy = remote(
        cot.at[pl.ds(256 * (1 - core), 256)], half, ex_s.at[3], ex_r.at[3], x, y, z, 1 - core
    )
    half_copy.start()
    steps = spread_steps(0, own, strips, sems[:7])
    drive((steps, 5))
    for u in range(NP):
        p, cols = unit(0, u, core)
        ref = strips.at[p, :, :, :, cols]
        remote(
            ref, blocks.at[core, u], ex_s.at[u], ex_r.at[u], x, y, z, 1 - core
        ).start()
        pltpu.make_async_copy(ref, blocks.at[core, u], loc.at[u]).start()
    drive((steps, 2))
    for u in range(NP):
        p, cols = unit(0, u, core)
        ref = strips.at[p, :, :, :, cols]
        pltpu.make_async_copy(ref, blocks.at[core, u], loc.at[u]).wait()
        remote(
            ref, blocks.at[1 - core, u], ex_s.at[u], ex_r.at[u], x, y, z, 1 - core
        ).wait()
    half_copy.wait()


def comm(collective_id, mib):
    return pltpu.CompilerParams(
        collective_id=collective_id, has_side_effects=True, vmem_limit_bytes=mib << 20
    )


def spread(factor, cot):
    return pl.pallas_call(
        spread_kernel,
        out_shape=(
            jax.ShapeDtypeStruct((3, 4, 4, 32, 1024), F32),
            jax.ShapeDtypeStruct((2, 3, 4, 4, 32, NB), F32),
            jax.ShapeDtypeStruct((256, 1024), F32),
        ),
        in_specs=[ANY, ANY],
        out_specs=(ANY, VM, VM),
        scratch_shapes=SPREAD_SEMS + [DMA((4,)), DMA((4,)), DMA((3,))],
        compiler_params=comm(0, 32),
    )(factor.reshape(4, 4, 32, 1024), cot)


def with_z(x, y, z, core):
    return plane_and_peer(x, y, z, core) + [
        (x, y, (z + 1) % 4, core), (x, y, (z + 3) % 4, core)
    ]


def along_spread_kernel(src, own, _, out, strips, *sems):
    greet(with_z(*place()))
    a = along_steps(src, out, sems[7:], lax.axis_index("row") >= NP)
    s = spread_steps(1, own, strips, sems[:7])
    drive((s, 1), (a, 1), (a, 2), (s, 1), (a, 2), (s, 1), (a, 4), (s, 1), (a, 2), (a, 1), (s, 3))


def along_spread(half, factor, strips):
    out, strips = pl.pallas_call(
        along_spread_kernel,
        out_shape=(
            jax.ShapeDtypeStruct((2, 2, CH, CR, 1536), F32),
            jax.ShapeDtypeStruct((3, 4, 4, 32, 1024), F32),
        ),
        in_specs=[VM, ANY, ANY],
        out_specs=(VM, ANY),
        scratch_shapes=SPREAD_SEMS + ALONG_SEMS,
        input_output_aliases={2: 1},
        compiler_params=comm(1, 16),
    )(half.reshape(1, 2, CH, CR, 1536), factor.reshape(4, 4, 32, 1024), strips)
    return out.reshape(512, 1536), strips.reshape(1536, 1024)


def reduce_kernel(src, out, *rest):
    x, y, z, core = place()
    greet(plane_and_peer(x, y, z, core))
    bufs, sems = rest[:5], rest[5:]
    ex_s, ex_r = sems[-2:]
    steps = reduce_steps(0, sems[7:11], src, out, bufs, sems[:7])
    drive((steps, 7))
    for u in range(NP):
        remote(
            out.at[core, u], out.at[core, u], ex_s.at[u], ex_r.at[u], x, y, z, 1 - core
        ).start()
    drive((steps, 2))
    for u in range(NP):
        remote(
            out.at[core, u], out.at[1 - core, u], ex_s.at[u], ex_r.at[u], x, y, z, 1 - core
        ).wait()


def reduce_rows(part):
    return pl.pallas_call(
        reduce_kernel,
        out_shape=jax.ShapeDtypeStruct((2, 3, 4, 4, 32, NB), F32),
        in_specs=[VM],
        out_specs=VM,
        scratch_shapes=REDUCE_BUFS + REDUCE_SEMS + [DMA((2, 3, 4))] * 4 + [DMA((3,)), DMA((3,))],
        compiler_params=comm(2, 32),
    )(part.reshape(3, 4, 4, 32, 1024))


def along_reduce_kernel(src, part, out, rest_out, *rest):
    greet(with_z(*place()))
    bufs, sems = rest[:5], rest[5:]
    a = along_steps(src, out, sems[7:], lax.axis_index("row") < NP)
    r = reduce_steps(1, None, part, rest_out, bufs, sems[:7])
    drive((a, 1), (r, 1), (a, 3), (r, 1), (a, 3), (r, 1), (a, 1), (r, 1), (a, 3), (a, 1), (r, 1))


def along_reduce(half, part):
    out, rest_out = pl.pallas_call(
        along_reduce_kernel,
        out_shape=(
            jax.ShapeDtypeStruct((2, 2, CH, CR, 1536), F32),
            jax.ShapeDtypeStruct((3, 4, 4, 32, NB), F32),
        ),
        in_specs=[VM, VM],
        out_specs=(VM, VM),
        scratch_shapes=REDUCE_BUFS + REDUCE_SEMS + ALONG_SEMS,
        compiler_params=comm(3, 40),
    )(half.reshape(1, 2, CH, CR, 1536), part.reshape(3, 4, 4, 32, 1024))
    return out.reshape(512, 1536), rest_out.reshape(3, NB, NB)


BS = 128


def invert_kernel(d_ref, o_ref):
    rows = lax.broadcasted_iota(jnp.int32, (BS, BS), 0)
    cols = lax.broadcasted_iota(jnp.int32, (BS, BS), 1)
    diag = rows == cols
    for block in range(NP * (NB // BS)):
        which, at = block // (NB // BS), pl.ds(block % (NB // BS) * BS, BS)
        base = d_ref[which, at, at]
        scale = jnp.sum(jnp.where(diag, base, 0.0), axis=1, keepdims=True)
        o_ref[which, at, at] = jnp.where(diag, 1.0 / scale, 0.0)

    def level(step, carry):
        pick = ((rows >> (step + 1)) == (cols >> (step + 1))) & (
            ((rows >> step) & 1) > ((cols >> step) & 1)
        )
        for block in range(NP * (NB // BS)):
            which, at = block // (NB // BS), pl.ds(block % (NB // BS) * BS, BS)
            have = o_ref[which, at, at]
            below = jnp.where(pick, d_ref[which, at, at], 0.0)
            o_ref[which, at, at] = have - dot(dot(have, below, HI), have, HI)
        return carry

    lax.fori_loop(0, 7, level, 0)
    size = BS
    while size < NB:
        for which in range(NP):
            for base in range(0, NB, 2 * size):
                up, down = pl.ds(base, size), pl.ds(base + size, size)
                corner = dot(
                    dot(o_ref[which, down, down], d_ref[which, down, up], HI),
                    o_ref[which, up, up], HI,
                )
                o_ref[which, down, up] = -corner
                o_ref[which, up, down] = jnp.zeros((size, size), F32)
        size *= 2


def invert(blocks):
    vm = pl.BlockSpec(memory_space=pltpu.VMEM)
    return pl.pallas_call(
        invert_kernel,
        out_shape=jax.ShapeDtypeStruct((NP, NB, NB), F32),
        in_specs=[vm],
        out_specs=vm,
        compiler_params=pltpu.CompilerParams(vmem_limit_bytes=16 << 20),
    )(blocks)


def plan():
    rows = []
    l00, l10, l20, l11, l21, l22, t00, t10, t20, t11, t21, t22, i0, i1, i2 = range(15)
    w, p, q, a2, y2, s21, s21t, a1, y1, s20, s10, s20t, s10t, a0, y0, none = range(15, 31)

    def mm(a, b, to):
        rows.append((0, a, b, none, to, 1))

    def take(a, b, to):
        rows.append((0, a, b, to, to, -1))

    def turn(a, to, add=0):
        rows.append((1, a, a, a, to, add))

    def lower(a, twice):
        rows.append((2, a, a, a, a, twice))

    def adjoint(l, i, t, a, y):
        turn(l, w)
        lower(t, 2)
        mm(w, t, p)
        lower(p, 1)
        turn(i, w)
        mm(w, p, q)
        mm(q, i, a)
        lower(a, 1)
        turn(a, y, add=1)

    adjoint(l22, i2, t22, a2, y2)
    take(y2, l21, t21)
    take(y2, l20, t20)
    mm(t21, i1, s21)
    turn(s21, s21t)
    take(s21t, l21, t11)
    take(s21t, l20, t10)
    adjoint(l11, i1, t11, a1, y1)
    take(y1, l10, t10)
    take(s21, l10, t20)
    mm(t20, i0, s20)
    mm(t10, i0, s10)
    turn(s20, s20t)
    turn(s10, s10t)
    take(s20t, l20, t00)
    take(s10t, l10, t00)
    adjoint(l00, i0, t00, a0, y0)
    coupling = ((y0, s10t, s20t), (s10, y1, s21t), (s20, s21, y2))
    result = ((a0, a0, a0), (s10, a1, a1), (s20, s21, a2))
    return rows, [x + y for x, y in zip(coupling, result)]


PLAN, PICKS = plan()
BLK = 512


def chain_kernel(plan_ref, pick_ref, l_ref, t_ref, i_ref, q_ref, z_ref, m, high, low):
    row, col = lax.axis_index("row"), lax.axis_index("col")
    for n in range(6):
        m[n] = l_ref[n]
        m[6 + n] = t_ref[n]
    for n in range(3):
        m[12 + n] = i_ref[n]
    m[30] = jnp.zeros((NB, NB), F32)

    def op(n, carry):
        kind, a, b, c, to, value = (plan_ref[n, j] for j in range(6))
        scale = value.astype(F32)

        @pl.when(kind == 0)
        def _():
            def split(i, carry):
                at = pl.ds(pl.multiple_of(i * 128, 128), 128)
                own = m[b, at]
                top = own.astype(jnp.bfloat16)
                high[0, at] = top
                high[1, at] = (own - top.astype(F32)).astype(jnp.bfloat16)
                high[2, at] = top
                own = m[a, at] * scale
                top = own.astype(jnp.bfloat16)
                low[at, :NB] = top
                low[at, NB : 2 * NB] = top
                low[at, 2 * NB :] = (own - top.astype(F32)).astype(jnp.bfloat16)
                return carry

            lax.fori_loop(0, 4, split, 0)
            right = high[...].reshape(3 * NB, NB)
            m[to] = m[c] + jnp.dot(low[...], right, preferred_element_type=F32)

        @pl.when(kind == 2)
        def _():
            def mask(i, carry):
                at = pl.ds(pl.multiple_of(i * 128, 128), 128)
                rows = lax.broadcasted_iota(jnp.int32, (128, NB), 0) + i * 128
                cols = lax.broadcasted_iota(jnp.int32, (128, NB), 1)
                own = m[a, at]
                diag = jnp.where(rows == cols, own * (0.5 * scale), 0.0)
                m[to, at] = jnp.where(rows > cols, own, diag)
                return carry

            lax.fori_loop(0, 4, mask, 0)

        @pl.when(kind == 1)
        def _():
            def turn(i, carry):
                at = pl.ds(pl.multiple_of(i * 128, 128), 128)
                m[to, :, at] = m[a, at].T + m[a, :, at] * scale
                return carry

            lax.fori_loop(0, 4, turn, 0)

        return carry

    lax.fori_loop(0, len(PLAN), op, 0)
    p = jnp.minimum(row, 2)
    half = pl.ds(pl.multiple_of(col % 2 * 256, 256), 256)
    for j in range(3):
        q_ref[:, j * NB : (j + 1) * NB] = m[pick_ref[p, j], half]
        z_ref[j] = m[pick_ref[p, 3 + j]]


def chain(blocks, near, inv):
    smem = pl.BlockSpec(memory_space=pltpu.SMEM)
    return pl.pallas_call(
        chain_kernel,
        out_shape=(
            jax.ShapeDtypeStruct((256, 3 * NB), F32),
            jax.ShapeDtypeStruct((3, NB, NB), F32),
        ),
        in_specs=[smem, smem, VM, VM, VM],
        out_specs=(VM, VM),
        scratch_shapes=[
            pltpu.VMEM((31, NB, NB), F32),
            pltpu.VMEM((3, NB, NB), jnp.bfloat16),
            pltpu.VMEM((NB, 3 * NB), jnp.bfloat16),
        ],
        compiler_params=pltpu.CompilerParams(vmem_limit_bytes=58 << 20),
    )(jnp.array(PLAN, jnp.int32), jnp.array(PICKS, jnp.int32), blocks, near, inv)


def finish_kernel(cot, solved, mixed, strips, far, near, z, out, high, low, f_high, f_low):
    row, col = lax.axis_index("row"), lax.axis_index("col")
    core = col % 2
    r = jnp.minimum(row, 2)
    lower_rows = row >= NP

    @pl.when(col < 7)
    def _():
        def split(i, carry):
            at = pl.ds(pl.multiple_of(i * 128, 128), 128)
            value = jnp.where(lower_rows, solved[at], mixed[at])
            top = value.astype(jnp.bfloat16)
            f_high[at] = top
            f_low[at] = (value - top.astype(F32)).astype(jnp.bfloat16)
            return carry

        lax.fori_loop(0, 4, split, 0)

    for h in range(2):
        cols = pl.ds(h * NB, NB)
        if h == 0:
            use_far = (core == 0) | (row == 0)
            at_far = r * (1 - core)
            at_near = jnp.maximum(r - core, 0)
            plain = col < 7
        else:
            use_far = (core == 1) & (row < 2)
            at_far = jnp.minimum(r + 1, 2)
            at_near = r * (1 - core) + 2 * core
            plain = col < 6

        @pl.when(plain)
        def _():
            def begin(i, carry):
                at = pl.ds(pl.multiple_of(i * 128, 128), 128)
                total = jnp.where(use_far, far[at_far, at], near[core, at_near, at])
                out[at, cols] = jnp.where(lower_rows, cot[at, cols], total)
                return carry

            lax.fori_loop(0, 4, begin, 0)

            def deep(k, carry):
                def split(i, carry):
                    at = pl.ds(pl.multiple_of(i * 128, 128), 128)
                    from_at = pl.ds(pl.multiple_of(k * NB + i * 128, 128), 128)
                    value = strips[from_at, cols]
                    top = value.astype(jnp.bfloat16)
                    high[at] = top
                    low[at] = (value - top.astype(F32)).astype(jnp.bfloat16)
                    return carry

                lax.fori_loop(0, 4, split, 0)
                inner = pl.ds(pl.multiple_of(k * NB, NB), NB)

                def product(i, carry):
                    at = pl.ds(pl.multiple_of(i * BLK, BLK), BLK)
                    top, rest, right = f_high[at, inner], f_low[at, inner], high[...]
                    total = jnp.dot(rest, right, preferred_element_type=F32)
                    total += jnp.dot(top, low[...], preferred_element_type=F32)
                    total += jnp.dot(top, right, preferred_element_type=F32)
                    out[at, cols] = out[at, cols] - total
                    return carry

                lax.fori_loop(0, NB // BLK, product, 0)
                return carry

            lax.fori_loop(0, NP, deep, 0)

        @pl.when(jnp.logical_not(plain))
        def _():
            def move(i, carry):
                at = pl.ds(pl.multiple_of(i * 128, 128), 128)
                if h == 0:
                    upper = jnp.where(row == 0, cot[at, cols], z[1, at])
                    out[at, cols] = jnp.where(lower_rows, solved[at, NB : 2 * NB], upper)
                else:
                    upper = jnp.where(row == 2, z[2, at], cot[at, cols])
                    last = jnp.where(lower_rows, solved[at, 2 * NB :], upper)
                    first = jnp.where(lower_rows, solved[at, :NB], z[0, at])
                    out[at, cols] = jnp.where(col == 7, last, first)
                return carry

            lax.fori_loop(0, 4, move, 0)


def finish(cot, solved, mixed, strips, far, near, z):
    return pl.pallas_call(
        finish_kernel,
        out_shape=jax.ShapeDtypeStruct((NB, 2 * NB), F32),
        in_specs=[VM] * 7,
        out_specs=VM,
        scratch_shapes=[
            pltpu.VMEM((NB, NB), jnp.bfloat16),
            pltpu.VMEM((NB, NB), jnp.bfloat16),
            pltpu.VMEM((NB, 3 * NB), jnp.bfloat16),
            pltpu.VMEM((NB, 3 * NB), jnp.bfloat16),
        ],
        compiler_params=pltpu.CompilerParams(vmem_limit_bytes=40 << 20),
    )(cot, solved, mixed, strips, far, near, z)


def shards(factor, cot):
    row = lax.axis_index("row")
    col = lax.axis_index("col")
    core = col % 2
    strips, blocks, other_half = spread(factor, cot)
    blocks = blocks.reshape(2, 3, NB, NB)
    l = {
        0: blocks[0, 0], 10: blocks[0, 1], 20: blocks[0, 2],
        11: blocks[1, 0], 21: blocks[1, 1], 22: blocks[1, 2],
    }
    inv = invert(jnp.stack([l[0], l[11], l[22]]))
    my_half = lax.dynamic_slice(cot, (core * 256, 0), (256, 1024))
    g6 = jnp.where(core == 0, my_half, other_half)
    g7 = jnp.where(core == 0, other_half, my_half)
    s2 = dot(g7[:, NB:], inv[2])
    s1 = dot(g7[:, :NB] - dot(s2, l[21]), inv[1])
    s0 = dot(g6[:, NB:] - dot(s2, l[20]) - dot(s1, l[10]), inv[0])
    solved, strips = along_spread(jnp.concatenate([s0, s1, s2], axis=1), factor, strips)
    lower_rows = row >= NP
    part = jnp.where(lower_rows, -dot_t(solved, factor), 0.0).reshape(3, NB, 1024)
    which = lax.broadcasted_iota(jnp.int32, (3, 1, 1), 0)
    part = jnp.where(which == row, cot[None], part)
    near = reduce_rows(part).reshape(2, 3, NB, NB)
    mixed_half, z = chain(blocks.reshape(6, NB, NB), near.reshape(6, NB, NB), inv)
    mixed, far = along_reduce(mixed_half, part)
    return finish(cot, solved, mixed, strips, far, near, z)


def solution(mesh):
    placed = (P("row", "col"), P("row", "col"))
    return jax.shard_map(
        shards, mesh=mesh, in_specs=placed, out_specs=P("row", "col"), check_vma=False
    )
```

```python
import jax
import jax.numpy as jnp
from jax import lax
from jax.experimental import pallas as pl
from jax.experimental.pallas import tpu as pltpu
from jax.sharding import PartitionSpec as P

NB = 512
NP = 3
MESH = pl.DeviceIdType.MESH
HI = lax.Precision.HIGHEST
MID = lax.Precision.HIGH
F32 = jnp.float32


def dot(a, b, precision=MID):
    return jnp.dot(a, b, precision=precision, preferred_element_type=F32)


def dot_t(a, b, precision=MID):
    return lax.dot_general(
        a, b, (((0,), (0,)), ((), ())), precision=precision, preferred_element_type=F32
    )


def place():
    row = lax.axis_index("row")
    col = lax.axis_index("col")
    return row // 4, row % 4, col // 2, col % 2


def remote(src, dst, send, recv, x, y, z, core):
    return pltpu.make_async_remote_copy(
        src_ref=src,
        dst_ref=dst,
        send_sem=send,
        recv_sem=recv,
        device_id=(x * 4 + y, z * 2 + core),
        device_id_type=MESH,
    )


def greet(devices):
    barrier = pltpu.get_barrier_semaphore()
    for x, y, z, core in devices:
        pl.semaphore_signal(
            barrier, inc=1, device_id=(x * 4 + y, z * 2 + core), device_id_type=MESH
        )
    pl.semaphore_wait(barrier, len(devices))


def plane_and_peer(x, y, z, core):
    out = []
    for dx in range(4):
        for dy in range(4):
            if dx or dy:
                out.append(((x + dx) % 4, (y + dy) % 4, z, core))
    return out + [(x, y, z, 1 - core)]


CH = 8
CR = 128 // CH
LEFT, RIGHT = pl.ds(0, NB), pl.ds(NB, NB)
ROWS = (pl.ds(0, 16), pl.ds(16, 16))
PAIR = (pl.ds(0, 2), pl.ds(2, 2))


def unit(part, u, core):
    if part == 0:
        p = u + core if u < 2 else 2
        off = NB * (1 - core) if u < 2 else NB
    else:
        p = u - core if u >= 1 else 0
        off = NB * core if u >= 1 else 0
    if isinstance(off, int):
        return p, pl.ds(off, NB)
    return p, pl.ds(pl.multiple_of(off, NB), NB)


def line(order, x, y, d):
    return ((x + d) % 4, y) if order == 0 else (x, (y + d) % 4)


def spread_steps(part, own, strips, sems, hand=None):
    scat_s, scat_r, one_s, one_r, two_s, two_r, loc = sems
    x, y, z, core = place()
    units = [unit(part, u, core) for u in range(NP)]

    def piece(ref, u, px, py):
        p, cols = units[u]
        if ref is own:
            return own.at[px, py, :, cols]
        return strips.at[p, px, py, :, cols]

    def scatter(u, d):
        tx, ty = (x + d // 4) % 4, (y + d % 4) % 4
        return remote(
            piece(own, u, tx, ty), piece(strips, u, tx, ty),
            scat_s.at[u, d], scat_r.at[u], tx, ty, z, core,
        )

    def keep(u):
        return pltpu.make_async_copy(piece(own, u, x, y), piece(strips, u, x, y), loc.at[u])

    roots = [(x == 0) & (y == units[u][0]) for u in range(NP)]
    for u in range(NP):

        @pl.when(roots[u])
        def _():
            keep(u).start()
            for d in range(15, 0, -1):
                scatter(u, d).start()

    yield

    for u in range(NP):

        @pl.when(roots[u])
        def _():
            keep(u).wait()

        @pl.when(jnp.logical_not(roots[u]))
        def _():
            here = piece(strips, u, x, y)
            remote(here, here, scat_s.at[u, 0], scat_r.at[u], x, y, z, 1 - core).wait_recv()

    def at(u, px, py, rows):
        p, cols = units[u]
        return strips.at[p, px, py, rows, cols]

    for _ in share_steps(at, one_s, one_r, two_s, two_r, hand):
        yield

    for u in range(NP):

        @pl.when(roots[u])
        def _():
            for d in range(1, 16):
                scatter(u, d).wait_send()

    yield


def piece_line(order, x, y, at):
    if order == 0:
        return pl.ds(0, 4), (y + at) % 4, ROWS[0]
    return (x + at) % 4, pl.ds(0, 4), ROWS[1]


ALL_LINES = [(order, u, at) for order in range(2) for u in range(NP) for at in range(4)]


def share_steps(ref_at, one_s, one_r, two_s, two_r, hand=None):
    x, y, z, core = place()
    every = [(order, u) for u in range(NP) for order in range(2)]
    first = []
    for order, u in every:
        for d in range(1, 4):
            here = ref_at(u, x, y, ROWS[order])
            tx, ty = line(order, x, y, d)
            first.append(
                remote(
                    here, here, one_s.at[order, u, d], one_r.at[order, u, d], tx, ty, z, core
                )
            )
    for copy in first:
        copy.start()
    yield

    for copy in first:
        copy.wait_recv()

    def block(order, u, at, pick):
        if order == 0:
            return ref_at(u, pick, (y + at) % 4, ROWS[0])
        return ref_at(u, (x + at) % 4, pick, ROWS[1])

    def second(order, u, kind):
        whole = pl.ds(0, 4)
        at, pick, d = (
            (0, whole, 1), (0, whole, 3), (3, PAIR[0], 1), (1, PAIR[1], 3)
        )[kind]
        ref = block(order, u, at, pick)
        tx, ty = line(1 - order, x, y, d)
        return remote(
            ref, ref, two_s.at[order, u, kind], two_r.at[order, u, kind], tx, ty, z, core
        )

    def arrival(order, u, kind):
        whole = pl.ds(0, 4)
        at, pick = ((3, whole), (1, whole), (2, PAIR[0]), (2, PAIR[1]))[kind]
        ref = block(order, u, at, pick)
        return remote(
            ref, ref, two_s.at[order, u, kind], two_r.at[order, u, kind], x, y, z, 1 - core
        )

    whole_line = pl.ds(0, 4)
    for order, u in every:
        for kind in (0, 1):
            second(order, u, kind).start()
    if hand:
        for order, u in every:
            hand(order, u, 0, block(order, u, 0, whole_line))
    yield

    for order, u in every:
        for kind in (0, 1):
            arrival(order, u, kind).wait_recv()
            second(order, u, kind + 2).start()
    if hand:
        for order, u in every:
            for at in (3, 1):
                hand(order, u, at, block(order, u, at, whole_line))
    yield

    for order, u in every:
        for kind in (2, 3):
            arrival(order, u, kind).wait_recv()
        if hand:
            hand(order, u, 2, block(order, u, 2, whole_line))
    yield

    for copy in first:
        copy.wait_send()
    for order, u in every:
        for kind in range(4):
            second(order, u, kind).wait_send()
    yield


AHEAD = 3


def along_steps(src, out, sems, used):
    ring_s, ring_r, peer_s, peer_r = sems
    x, y, z, core = place()
    up, down = (z + 1) % 4, (z + 3) % 4
    positions = (up, 3 - z)
    targets = (up, down)
    source = used & (z == 3)

    def chunk(owner, way, step):
        return out.at[pl.ds(owner, 1), way, step]

    def ring(way, step, block):
        mine = chunk(core, way, step)
        return remote(
            block, mine, ring_s.at[way, step], ring_r.at[way, step], x, y, targets[way], core
        )

    def across(way, step, block):
        mine = chunk(core, way, step)
        return remote(
            block, mine, peer_s.at[way, step], peer_r.at[way, step], x, y, z, 1 - core
        )

    def issue(step):
        for way in range(2):
            ring(way, step, src.at[:, way, step]).start()
        for way in range(2):
            across(way, step, src.at[:, way, step]).start()

    @pl.when(source)
    def _():
        for step in range(AHEAD):
            issue(step)
        out[pl.ds(core, 1)] = src[...]

    yield
    for tick in range(CH + 2):
        if tick + AHEAD < CH:

            @pl.when(source)
            def _():
                for way in range(2):
                    ring(way, tick, src.at[:, way, tick]).wait_send()
                issue(tick + AHEAD)

        for way in range(2):
            for pos in range(1, 4):
                step = tick - (pos - 1)
                if not 0 <= step < CH:
                    continue

                @pl.when(used & (positions[way] == pos))
                def _():
                    mine = chunk(core, way, step)
                    ring(way, step, mine).wait_recv()
                    if pos < 3:
                        ring(way, step, mine).start()
                    across(way, step, mine).start()

        yield

    @pl.when(used)
    def _():
        for step in range(CH):
            for way in range(2):
                mine, other = chunk(core, way, step), chunk(1 - core, way, step)
                remote(
                    mine, other, peer_s.at[way, step], peer_r.at[way, step],
                    x, y, z, 1 - core,
                ).wait()
                left = positions[way] < 3
                if step + AHEAD < CH:
                    left = left & (z != 3)

                @pl.when(left)
                def _():
                    ring(way, step, mine).wait_send()

    yield


def reduce_steps(part, wide, src, out, bufs, sems, hand=None):
    got, acc, tot, got2, fin = bufs
    one_s, one_r, two_s, two_r, g_s, g_r, loc = sems
    x, y, z, core = place()
    units = [unit(part, u, core) for u in range(NP)]
    every = [(order, u) for u in range(NP) for order in range(2)]

    def share(order, u, at, pick):
        p, cols = units[u]
        if order == 0:
            return p, (x + at) % 4, pick, ROWS[0], cols
        return p, pick, (y + at) % 4, ROWS[1], cols

    def one(order, u, kind, way):
        step = 1 if way == 0 else 3
        if kind == 0:
            ref = src.at[share(order, u, 2, PAIR[way])]
        elif kind == 1:
            ref = src.at[share(order, u, step, PAIR[1 - way])]
        else:
            ref = acc.at[order, u, way]
        tx, ty = line(order, x, y, step)
        return remote(
            ref, got.at[order, u, kind, way],
            one_s.at[order, u, kind * 2 + way], one_r.at[order, u, kind * 2 + way],
            tx, ty, z, core,
        )

    for kind in (0, 1):
        for order, u in every:
            for way in range(2):
                one(order, u, kind, way).start()
    yield

    for order, u in every:
        for way in range(2):
            one(order, u, 0, way).wait_recv()
            step = 1 if way == 0 else 3
            acc[order, u, way] = (
                src[share(order, u, step, PAIR[way])] + got[order, u, 0, way]
            )
            one(order, u, 2, way).start()
    yield

    def two(order, u, d):
        tx, ty = line(1 - order, x, y, d)
        index = ty if order == 0 else tx
        return remote(
            tot.at[order, u, index], got2.at[order, u, d - 1],
            two_s.at[order, u, d], two_r.at[order, u, d], tx, ty, z, core,
        )

    for order, u in every:
        for kind in (1, 2):
            for way in range(2):
                one(order, u, kind, way).wait_recv()
        for half in range(2):
            base = src[share(order, u, 0, PAIR[half])]
            tot[order, u, PAIR[half]] = base + (
                got[order, u, 2, half] + got[order, u, 1, 1 - half]
            )
        for d in range(1, 4):
            two(order, u, d).start()
    yield

    for order, u in every:
        for d in range(1, 4):
            two(order, u, d).wait_recv()
        here = y if order == 0 else x
        total = (tot[order, u, here] + got2[order, u, 0]) + (
            got2[order, u, 1] + got2[order, u, 2]
        )
        if wide:
            out[core, u, x, y, ROWS[order]] = total
        else:
            fin[u, ROWS[order]] = total

    def sends():
        for order, u in every:
            for kind in range(3):
                for way in range(2):
                    one(order, u, kind, way).wait_send()
            for d in range(1, 4):
                two(order, u, d).wait_send()

    if wide:

        def at(u, px, py, rows):
            return out.at[core, u, px, py, rows]

        for _ in share_steps(at, *wide, hand):
            yield
        sends()
        yield
        return

    def slot(u, px, py):
        return out.at[u, px, py]

    def send(root, u):
        return remote(
            fin.at[u], slot(u, x, y), g_s.at[root, u], g_r.at[u, x * 4 + y], 0, root, z, core
        )

    def keep(u):
        return pltpu.make_async_copy(fin.at[u], slot(u, x, y), loc.at[u])

    def cases():
        for root in range(NP):
            at_root = (x == 0) & (y == root)
            for u in range(NP):
                flag = units[u][0] == root
                yield root, u, flag & at_root, flag & jnp.logical_not(at_root)

    for root, u, local, away in cases():

        @pl.when(away)
        def _():
            send(root, u).start()

        @pl.when(local)
        def _():
            keep(u).start()

    yield

    for root, u, local, away in cases():

        @pl.when(away)
        def _():
            send(root, u).wait_send()

        @pl.when(local)
        def _():
            keep(u).wait()
            for d in range(1, 16):
                sx, sy = (x + d // 4) % 4, (y + d % 4) % 4
                remote(
                    fin.at[u], slot(u, sx, sy), g_s.at[root, u], g_r.at[u, sx * 4 + sy],
                    x, y, z, 1 - core,
                ).wait_recv()

    sends()
    yield


DMA = pltpu.SemaphoreType.DMA
SPREAD_SEMS = [
    DMA((3, 16)), DMA((3,)), DMA((2, 3, 4)), DMA((2, 3, 4)), DMA((2, 3, 4)), DMA((2, 3, 4)),
    DMA((3,)),
]
ALONG_SEMS = [DMA((2, CH))] * 4
REDUCE_BUFS = [
    pltpu.VMEM((2, 3, 3, 2, 2, 16, NB), F32),
    pltpu.VMEM((2, 3, 2, 2, 16, NB), F32),
    pltpu.VMEM((2, 3, 4, 16, NB), F32),
    pltpu.VMEM((2, 3, 3, 16, NB), F32),
    pltpu.VMEM((3, 32, NB), F32),
]
REDUCE_SEMS = [
    DMA((2, 3, 6)), DMA((2, 3, 6)), DMA((2, 3, 4)), DMA((2, 3, 4)), DMA((3, 3)), DMA((3, 16)),
    DMA((3,)),
]
VM = pl.BlockSpec(memory_space=pltpu.VMEM)
ANY = pl.BlockSpec(memory_space=pl.ANY)


def drive(*plan):
    for steps, count in plan:
        for _ in range(count):
            next(steps)


def spread_kernel(own, cot, strips, blocks, half, *sems):
    x, y, z, core = place()
    greet(plane_and_peer(x, y, z, core))
    ex_s, ex_r, loc, half_s, half_r = sems[-5:]
    half_copy = remote(
        cot.at[pl.ds(256 * (1 - core), 256)], half, half_s.at[0], half_r.at[0], x, y, z, 1 - core
    )
    half_copy.start()
    def over(order, u, at, ref):
        px, py, rows = piece_line(order, x, y, at)
        there = blocks.at[core, u, px, py, rows]
        return (
            remote(ref, there, ex_s.at[order, u, at], ex_r.at[order, u, at], x, y, z, 1 - core),
            pltpu.make_async_copy(ref, there, loc.at[order, u, at]),
        )

    def hand(order, u, at, ref):
        for copy in over(order, u, at, ref):
            copy.start()

    drive((spread_steps(0, own, strips, sems[:7], hand), 7))
    for order, u, at in ALL_LINES:
        px, py, rows = piece_line(order, x, y, at)
        p, cols = unit(0, u, core)
        away, here = over(order, u, at, strips.at[p, px, py, rows, cols])
        here.wait()
        away.wait_send()
        got = blocks.at[1 - core, u, px, py, rows]
        remote(
            got, got, ex_s.at[order, u, at], ex_r.at[order, u, at], x, y, z, 1 - core
        ).wait_recv()
    half_copy.wait()


def comm(collective_id, mib):
    return pltpu.CompilerParams(
        collective_id=collective_id, has_side_effects=True, vmem_limit_bytes=mib << 20
    )


def spread(factor, cot):
    return pl.pallas_call(
        spread_kernel,
        out_shape=(
            jax.ShapeDtypeStruct((3, 4, 4, 32, 1024), F32),
            jax.ShapeDtypeStruct((2, 3, 4, 4, 32, NB), F32),
            jax.ShapeDtypeStruct((256, 1024), F32),
        ),
        in_specs=[ANY, ANY],
        out_specs=(ANY, VM, VM),
        scratch_shapes=SPREAD_SEMS + [DMA((2, 3, 4))] * 3 + [DMA((1,)), DMA((1,))],
        compiler_params=comm(0, 60),
    )(factor.reshape(4, 4, 32, 1024), cot)


def with_z(x, y, z, core):
    return plane_and_peer(x, y, z, core) + [
        (x, y, (z + 1) % 4, core), (x, y, (z + 3) % 4, core)
    ]


def along_spread_kernel(src, own, _, out, strips, *sems):
    greet(with_z(*place()))
    a = along_steps(src, out, sems[7:], lax.axis_index("row") >= NP)
    s = spread_steps(1, own, strips, sems[:7])
    drive((s, 1), (a, 1), (a, 2), (s, 1), (a, 2), (s, 1), (a, 4), (s, 1), (a, 2), (a, 1), (s, 3))


def along_spread(half, factor, strips):
    out, strips = pl.pallas_call(
        along_spread_kernel,
        out_shape=(
            jax.ShapeDtypeStruct((2, 2, CH, CR, 1536), F32),
            jax.ShapeDtypeStruct((3, 4, 4, 32, 1024), F32),
        ),
        in_specs=[VM, ANY, ANY],
        out_specs=(VM, ANY),
        scratch_shapes=SPREAD_SEMS + ALONG_SEMS,
        input_output_aliases={2: 1},
        compiler_params=comm(1, 60),
    )(half.reshape(1, 2, CH, CR, 1536), factor.reshape(4, 4, 32, 1024), strips)
    return out.reshape(512, 1536), strips.reshape(1536, 1024)


def reduce_kernel(src, out, *rest):
    x, y, z, core = place()
    greet(plane_and_peer(x, y, z, core))
    bufs, sems = rest[:5], rest[5:]
    ex_s, ex_r = sems[-2:]

    def over(order, u, at, ref):
        return remote(
            ref, ref, ex_s.at[order, u, at], ex_r.at[order, u, at], x, y, z, 1 - core
        )

    def hand(order, u, at, ref):
        over(order, u, at, ref).start()

    drive((reduce_steps(0, sems[7:11], src, out, bufs, sems[:7], hand), 9))
    for order, u, at in ALL_LINES:
        px, py, rows = piece_line(order, x, y, at)
        over(order, u, at, out.at[core, u, px, py, rows]).wait_send()
        over(order, u, at, out.at[1 - core, u, px, py, rows]).wait_recv()


def reduce_rows(part):
    return pl.pallas_call(
        reduce_kernel,
        out_shape=jax.ShapeDtypeStruct((2, 3, 4, 4, 32, NB), F32),
        in_specs=[VM],
        out_specs=VM,
        scratch_shapes=REDUCE_BUFS + REDUCE_SEMS + [DMA((2, 3, 4))] * 6,
        compiler_params=comm(2, 32),
    )(part.reshape(3, 4, 4, 32, 1024))


def along_reduce_kernel(src, part, out, rest_out, *rest):
    greet(with_z(*place()))
    bufs, sems = rest[:5], rest[5:]
    a = along_steps(src, out, sems[7:], lax.axis_index("row") < NP)
    r = reduce_steps(1, None, part, rest_out, bufs, sems[:7])
    drive((a, 1), (r, 1), (a, 3), (r, 1), (a, 3), (r, 1), (a, 1), (r, 1), (a, 3), (a, 1), (r, 1))


def along_reduce(half, part):
    out, rest_out = pl.pallas_call(
        along_reduce_kernel,
        out_shape=(
            jax.ShapeDtypeStruct((2, 2, CH, CR, 1536), F32),
            jax.ShapeDtypeStruct((3, 4, 4, 32, NB), F32),
        ),
        in_specs=[VM, VM],
        out_specs=(VM, VM),
        scratch_shapes=REDUCE_BUFS + REDUCE_SEMS + ALONG_SEMS,
        compiler_params=comm(3, 40),
    )(half.reshape(1, 2, CH, CR, 1536), part.reshape(3, 4, 4, 32, 1024))
    return out.reshape(512, 1536), rest_out.reshape(3, NB, NB)


BS = 128


def invert_kernel(d_ref, o_ref):
    rows = lax.broadcasted_iota(jnp.int32, (BS, BS), 0)
    cols = lax.broadcasted_iota(jnp.int32, (BS, BS), 1)
    diag = rows == cols
    for block in range(NP * (NB // BS)):
        which, at = block // (NB // BS), pl.ds(block % (NB // BS) * BS, BS)
        base = d_ref[which, at, at]
        scale = jnp.sum(jnp.where(diag, base, 0.0), axis=1, keepdims=True)
        o_ref[which, at, at] = jnp.where(diag, 1.0 / scale, 0.0)

    def level(step, carry):
        pick = ((rows >> (step + 1)) == (cols >> (step + 1))) & (
            ((rows >> step) & 1) > ((cols >> step) & 1)
        )
        for block in range(NP * (NB // BS)):
            which, at = block // (NB // BS), pl.ds(block % (NB // BS) * BS, BS)
            have = o_ref[which, at, at]
            below = jnp.where(pick, d_ref[which, at, at], 0.0)
            o_ref[which, at, at] = have - dot(dot(have, below, HI), have, HI)
        return carry

    lax.fori_loop(0, 7, level, 0)
    size = BS
    while size < NB:
        for which in range(NP):
            for base in range(0, NB, 2 * size):
                up, down = pl.ds(base, size), pl.ds(base + size, size)
                corner = dot(
                    dot(o_ref[which, down, down], d_ref[which, down, up], HI),
                    o_ref[which, up, up], HI,
                )
                o_ref[which, down, up] = -corner
                o_ref[which, up, down] = jnp.zeros((size, size), F32)
        size *= 2


def invert(blocks):
    vm = pl.BlockSpec(memory_space=pltpu.VMEM)
    return pl.pallas_call(
        invert_kernel,
        out_shape=jax.ShapeDtypeStruct((NP, NB, NB), F32),
        in_specs=[vm],
        out_specs=vm,
        compiler_params=pltpu.CompilerParams(vmem_limit_bytes=16 << 20),
    )(blocks)


def plan():
    rows = []
    l00, l10, l20, l11, l21, l22, t00, t10, t20, t11, t21, t22, i0, i1, i2 = range(15)
    w, p, q, a2, y2, s21, s21t, a1, y1, s20, s10, s20t, s10t, a0, y0, none = range(15, 31)

    def mm(a, b, to):
        rows.append((0, a, b, none, to, 1))

    def take(a, b, to):
        rows.append((0, a, b, to, to, -1))

    def turn(a, to, add=0):
        rows.append((1, a, a, a, to, add))

    def lower(a, twice):
        rows.append((2, a, a, a, a, twice))

    def adjoint(l, i, t, a, y):
        turn(l, w)
        lower(t, 2)
        mm(w, t, p)
        lower(p, 1)
        turn(i, w)
        mm(w, p, q)
        mm(q, i, a)
        lower(a, 1)
        turn(a, y, add=1)

    adjoint(l22, i2, t22, a2, y2)
    take(y2, l21, t21)
    take(y2, l20, t20)
    mm(t21, i1, s21)
    turn(s21, s21t)
    take(s21t, l21, t11)
    take(s21t, l20, t10)
    adjoint(l11, i1, t11, a1, y1)
    take(y1, l10, t10)
    take(s21, l10, t20)
    mm(t20, i0, s20)
    mm(t10, i0, s10)
    turn(s20, s20t)
    turn(s10, s10t)
    take(s20t, l20, t00)
    take(s10t, l10, t00)
    adjoint(l00, i0, t00, a0, y0)
    coupling = ((y0, s10t, s20t), (s10, y1, s21t), (s20, s21, y2))
    result = ((a0, a0, a0), (s10, a1, a1), (s20, s21, a2))
    return rows, [x + y for x, y in zip(coupling, result)]


PLAN, PICKS = plan()
BLK = 512


def chain_kernel(plan_ref, pick_ref, l_ref, t_ref, i_ref, q_ref, z_ref, m, high, low):
    row, col = lax.axis_index("row"), lax.axis_index("col")
    for n in range(6):
        m[n] = l_ref[n]
        m[6 + n] = t_ref[n]
    for n in range(3):
        m[12 + n] = i_ref[n]
    m[30] = jnp.zeros((NB, NB), F32)

    def op(n, carry):
        kind, a, b, c, to, value = (plan_ref[n, j] for j in range(6))
        scale = value.astype(F32)

        @pl.when(kind == 0)
        def _():
            def split(i, carry):
                at = pl.ds(pl.multiple_of(i * 128, 128), 128)
                own = m[b, at]
                top = own.astype(jnp.bfloat16)
                high[0, at] = top
                high[1, at] = (own - top.astype(F32)).astype(jnp.bfloat16)
                high[2, at] = top
                own = m[a, at] * scale
                top = own.astype(jnp.bfloat16)
                low[at, :NB] = top
                low[at, NB : 2 * NB] = top
                low[at, 2 * NB :] = (own - top.astype(F32)).astype(jnp.bfloat16)
                return carry

            lax.fori_loop(0, 4, split, 0)
            right = high[...].reshape(3 * NB, NB)
            m[to] = m[c] + jnp.dot(low[...], right, preferred_element_type=F32)

        @pl.when(kind == 2)
        def _():
            def mask(i, carry):
                at = pl.ds(pl.multiple_of(i * 128, 128), 128)
                rows = lax.broadcasted_iota(jnp.int32, (128, NB), 0) + i * 128
                cols = lax.broadcasted_iota(jnp.int32, (128, NB), 1)
                own = m[a, at]
                diag = jnp.where(rows == cols, own * (0.5 * scale), 0.0)
                m[to, at] = jnp.where(rows > cols, own, diag)
                return carry

            lax.fori_loop(0, 4, mask, 0)

        @pl.when(kind == 1)
        def _():
            def turn(i, carry):
                at = pl.ds(pl.multiple_of(i * 128, 128), 128)
                m[to, :, at] = m[a, at].T + m[a, :, at] * scale
                return carry

            lax.fori_loop(0, 4, turn, 0)

        return carry

    lax.fori_loop(0, len(PLAN), op, 0)
    p = jnp.minimum(row, 2)
    half = pl.ds(pl.multiple_of(col % 2 * 256, 256), 256)
    for j in range(3):
        q_ref[:, j * NB : (j + 1) * NB] = m[pick_ref[p, j], half]
        z_ref[j] = m[pick_ref[p, 3 + j]]


def chain(blocks, near, inv):
    smem = pl.BlockSpec(memory_space=pltpu.SMEM)
    return pl.pallas_call(
        chain_kernel,
        out_shape=(
            jax.ShapeDtypeStruct((256, 3 * NB), F32),
            jax.ShapeDtypeStruct((3, NB, NB), F32),
        ),
        in_specs=[smem, smem, VM, VM, VM],
        out_specs=(VM, VM),
        scratch_shapes=[
            pltpu.VMEM((31, NB, NB), F32),
            pltpu.VMEM((3, NB, NB), jnp.bfloat16),
            pltpu.VMEM((NB, 3 * NB), jnp.bfloat16),
        ],
        compiler_params=pltpu.CompilerParams(vmem_limit_bytes=55 << 20),
    )(jnp.array(PLAN, jnp.int32), jnp.array(PICKS, jnp.int32), blocks, near, inv)


def finish_kernel(cot, solved, mixed, strips, far, near, z, out, high, low, f_high, f_low):
    row, col = lax.axis_index("row"), lax.axis_index("col")
    core = col % 2
    r = jnp.minimum(row, 2)
    lower_rows = row >= NP

    @pl.when(col < 7)
    def _():
        def split(i, carry):
            at = pl.ds(pl.multiple_of(i * 128, 128), 128)
            value = jnp.where(lower_rows, solved[at], mixed[at])
            top = value.astype(jnp.bfloat16)
            f_high[at] = top
            f_low[at] = (value - top.astype(F32)).astype(jnp.bfloat16)
            return carry

        lax.fori_loop(0, 4, split, 0)

    for h in range(2):
        cols = pl.ds(h * NB, NB)
        if h == 0:
            use_far = (core == 0) | (row == 0)
            at_far = r * (1 - core)
            at_near = jnp.maximum(r - core, 0)
            plain = col < 7
        else:
            use_far = (core == 1) & (row < 2)
            at_far = jnp.minimum(r + 1, 2)
            at_near = r * (1 - core) + 2 * core
            plain = col < 6

        @pl.when(plain)
        def _():
            def begin(i, carry):
                at = pl.ds(pl.multiple_of(i * 128, 128), 128)
                total = jnp.where(use_far, far[at_far, at], near[core, at_near, at])
                out[at, cols] = jnp.where(lower_rows, cot[at, cols], total)
                return carry

            lax.fori_loop(0, 4, begin, 0)

            def deep(k, carry):
                def split(i, carry):
                    at = pl.ds(pl.multiple_of(i * 128, 128), 128)
                    from_at = pl.ds(pl.multiple_of(k * NB + i * 128, 128), 128)
                    value = strips[from_at, cols]
                    top = value.astype(jnp.bfloat16)
                    high[at] = top
                    low[at] = (value - top.astype(F32)).astype(jnp.bfloat16)
                    return carry

                lax.fori_loop(0, 4, split, 0)
                inner = pl.ds(pl.multiple_of(k * NB, NB), NB)

                def product(i, carry):
                    at = pl.ds(pl.multiple_of(i * BLK, BLK), BLK)
                    top, rest, right = f_high[at, inner], f_low[at, inner], high[...]
                    total = jnp.dot(rest, right, preferred_element_type=F32)
                    total += jnp.dot(top, low[...], preferred_element_type=F32)
                    total += jnp.dot(top, right, preferred_element_type=F32)
                    out[at, cols] = out[at, cols] - total
                    return carry

                lax.fori_loop(0, NB // BLK, product, 0)
                return carry

            lax.fori_loop(0, NP, deep, 0)

        @pl.when(jnp.logical_not(plain))
        def _():
            def move(i, carry):
                at = pl.ds(pl.multiple_of(i * 128, 128), 128)
                if h == 0:
                    upper = jnp.where(row == 0, cot[at, cols], z[1, at])
                    out[at, cols] = jnp.where(lower_rows, solved[at, NB : 2 * NB], upper)
                else:
                    upper = jnp.where(row == 2, z[2, at], cot[at, cols])
                    last = jnp.where(lower_rows, solved[at, 2 * NB :], upper)
                    first = jnp.where(lower_rows, solved[at, :NB], z[0, at])
                    out[at, cols] = jnp.where(col == 7, last, first)
                return carry

            lax.fori_loop(0, 4, move, 0)


def finish(cot, solved, mixed, strips, far, near, z):
    return pl.pallas_call(
        finish_kernel,
        out_shape=jax.ShapeDtypeStruct((NB, 2 * NB), F32),
        in_specs=[VM] * 7,
        out_specs=VM,
        scratch_shapes=[
            pltpu.VMEM((NB, NB), jnp.bfloat16),
            pltpu.VMEM((NB, NB), jnp.bfloat16),
            pltpu.VMEM((NB, 3 * NB), jnp.bfloat16),
            pltpu.VMEM((NB, 3 * NB), jnp.bfloat16),
        ],
        compiler_params=pltpu.CompilerParams(vmem_limit_bytes=40 << 20),
    )(cot, solved, mixed, strips, far, near, z)


def shards(factor, cot):
    row = lax.axis_index("row")
    col = lax.axis_index("col")
    core = col % 2
    strips, blocks, other_half = spread(factor, cot)
    blocks = blocks.reshape(2, 3, NB, NB)
    l = {
        0: blocks[0, 0], 10: blocks[0, 1], 20: blocks[0, 2],
        11: blocks[1, 0], 21: blocks[1, 1], 22: blocks[1, 2],
    }
    inv = invert(jnp.stack([l[0], l[11], l[22]]))
    my_half = lax.dynamic_slice(cot, (core * 256, 0), (256, 1024))
    g6 = jnp.where(core == 0, my_half, other_half)
    g7 = jnp.where(core == 0, other_half, my_half)
    s2 = dot(g7[:, NB:], inv[2])
    s1 = dot(g7[:, :NB] - dot(s2, l[21]), inv[1])
    s0 = dot(g6[:, NB:] - dot(s2, l[20]) - dot(s1, l[10]), inv[0])
    solved, strips = along_spread(jnp.concatenate([s0, s1, s2], axis=1), factor, strips)
    lower_rows = row >= NP
    part = jnp.where(lower_rows, -dot_t(solved, factor), 0.0).reshape(3, NB, 1024)
    which = lax.broadcasted_iota(jnp.int32, (3, 1, 1), 0)
    part = jnp.where(which == row, cot[None], part)
    near = reduce_rows(part).reshape(2, 3, NB, NB)
    mixed_half, z = chain(blocks.reshape(6, NB, NB), near.reshape(6, NB, NB), inv)
    mixed, far = along_reduce(mixed_half, part)
    return finish(cot, solved, mixed, strips, far, near, z)


def solution(mesh):
    placed = (P("row", "col"), P("row", "col"))
    return jax.shard_map(
        shards, mesh=mesh, in_specs=placed, out_specs=P("row", "col"), check_vma=False
    )
```

```python
import jax
import jax.numpy as jnp
from jax import lax
from jax.experimental import pallas as pl
from jax.experimental.pallas import tpu as pltpu
from jax.sharding import PartitionSpec as P

NB = 512
NP = 3
MESH = pl.DeviceIdType.MESH
HI = lax.Precision.HIGHEST
MID = lax.Precision.HIGH
F32 = jnp.float32


def dot(a, b, precision=MID):
    return jnp.dot(a, b, precision=precision, preferred_element_type=F32)


def dot_t(a, b, precision=MID):
    return lax.dot_general(
        a, b, (((0,), (0,)), ((), ())), precision=precision, preferred_element_type=F32
    )


def place():
    row = lax.axis_index("row")
    col = lax.axis_index("col")
    return row // 4, row % 4, col // 2, col % 2


def remote(src, dst, send, recv, x, y, z, core):
    return pltpu.make_async_remote_copy(
        src_ref=src,
        dst_ref=dst,
        send_sem=send,
        recv_sem=recv,
        device_id=(x * 4 + y, z * 2 + core),
        device_id_type=MESH,
    )


def greet(devices):
    barrier = pltpu.get_barrier_semaphore()
    for x, y, z, core in devices:
        pl.semaphore_signal(
            barrier, inc=1, device_id=(x * 4 + y, z * 2 + core), device_id_type=MESH
        )
    pl.semaphore_wait(barrier, len(devices))


def plane_and_peer(x, y, z, core):
    out = []
    for dx in range(4):
        for dy in range(4):
            if dx or dy:
                out.append(((x + dx) % 4, (y + dy) % 4, z, core))
    return out + [(x, y, z, 1 - core)]


CH = 8
CR = 128 // CH
LEFT, RIGHT = pl.ds(0, NB), pl.ds(NB, NB)
ROWS = (pl.ds(0, 16), pl.ds(16, 16))
PAIR = (pl.ds(0, 2), pl.ds(2, 2))


def unit(part, u, core):
    if part == 0:
        p = u + core if u < 2 else 2
        off = NB * (1 - core) if u < 2 else NB
    else:
        p = u - core if u >= 1 else 0
        off = NB * core if u >= 1 else 0
    if isinstance(off, int):
        return p, pl.ds(off, NB)
    return p, pl.ds(pl.multiple_of(off, NB), NB)


def line(order, x, y, d):
    return ((x + d) % 4, y) if order == 0 else (x, (y + d) % 4)


def spread_steps(part, own, strips, sems, hand=None):
    scat_s, scat_r, one_s, one_r, two_s, two_r, loc = sems
    x, y, z, core = place()
    units = [unit(part, u, core) for u in range(NP)]

    def piece(ref, u, px, py):
        p, cols = units[u]
        if ref is own:
            return own.at[px, py, :, cols]
        return strips.at[p, px, py, :, cols]

    def scatter(u, d):
        tx, ty = (x + d // 4) % 4, (y + d % 4) % 4
        return remote(
            piece(own, u, tx, ty), piece(strips, u, tx, ty),
            scat_s.at[u, d], scat_r.at[u], tx, ty, z, core,
        )

    def keep(u):
        return pltpu.make_async_copy(piece(own, u, x, y), piece(strips, u, x, y), loc.at[u])

    roots = [(x == 0) & (y == units[u][0]) for u in range(NP)]
    for u in range(NP):

        @pl.when(roots[u])
        def _():
            keep(u).start()
            for d in range(15, 0, -1):
                scatter(u, d).start()

    yield

    for u in range(NP):

        @pl.when(roots[u])
        def _():
            keep(u).wait()

        @pl.when(jnp.logical_not(roots[u]))
        def _():
            here = piece(strips, u, x, y)
            remote(here, here, scat_s.at[u, 0], scat_r.at[u], x, y, z, 1 - core).wait_recv()

    def at(u, px, py, rows):
        p, cols = units[u]
        return strips.at[p, px, py, rows, cols]

    for _ in share_steps(at, one_s, one_r, two_s, two_r, hand):
        yield

    for u in range(NP):

        @pl.when(roots[u])
        def _():
            for d in range(1, 16):
                scatter(u, d).wait_send()

    yield


def piece_line(order, x, y, at):
    if order == 0:
        return pl.ds(0, 4), (y + at) % 4, ROWS[0]
    return (x + at) % 4, pl.ds(0, 4), ROWS[1]


ALL_LINES = [(order, u, at) for order in range(2) for u in range(NP) for at in range(4)]


def share_steps(ref_at, one_s, one_r, two_s, two_r, hand=None):
    x, y, z, core = place()
    every = [(order, u) for u in range(NP) for order in range(2)]
    first = []
    for order, u in every:
        for d in range(1, 4):
            here = ref_at(u, x, y, ROWS[order])
            tx, ty = line(order, x, y, d)
            first.append(
                remote(
                    here, here, one_s.at[order, u, d], one_r.at[order, u, d], tx, ty, z, core
                )
            )
    for copy in first:
        copy.start()
    yield

    for copy in first:
        copy.wait_recv()

    def block(order, u, at, pick):
        if order == 0:
            return ref_at(u, pick, (y + at) % 4, ROWS[0])
        return ref_at(u, (x + at) % 4, pick, ROWS[1])

    def second(order, u, kind):
        whole = pl.ds(0, 4)
        at, pick, d = (
            (0, whole, 1), (0, whole, 3), (3, PAIR[0], 1), (1, PAIR[1], 3)
        )[kind]
        ref = block(order, u, at, pick)
        tx, ty = line(1 - order, x, y, d)
        return remote(
            ref, ref, two_s.at[order, u, kind], two_r.at[order, u, kind], tx, ty, z, core
        )

    def arrival(order, u, kind):
        whole = pl.ds(0, 4)
        at, pick = ((3, whole), (1, whole), (2, PAIR[0]), (2, PAIR[1]))[kind]
        ref = block(order, u, at, pick)
        return remote(
            ref, ref, two_s.at[order, u, kind], two_r.at[order, u, kind], x, y, z, 1 - core
        )

    whole_line = pl.ds(0, 4)
    for order, u in every:
        for kind in (0, 1):
            second(order, u, kind).start()
    if hand:
        for order, u in every:
            hand(order, u, 0, block(order, u, 0, whole_line))
    yield

    for order, u in every:
        for kind in (0, 1):
            arrival(order, u, kind).wait_recv()
            second(order, u, kind + 2).start()
    if hand:
        for order, u in every:
            for at in (3, 1):
                hand(order, u, at, block(order, u, at, whole_line))
    yield

    for order, u in every:
        for kind in (2, 3):
            arrival(order, u, kind).wait_recv()
        if hand:
            hand(order, u, 2, block(order, u, 2, whole_line))
    yield

    for copy in first:
        copy.wait_send()
    for order, u in every:
        for kind in range(4):
            second(order, u, kind).wait_send()
    yield


AHEAD = 5


def along_steps(src, out, sems, used):
    ring_s, ring_r, peer_s, peer_r = sems
    x, y, z, core = place()
    up, down = (z + 1) % 4, (z + 3) % 4
    positions = (up, 3 - z)
    targets = (up, down)
    source = used & (z == 3)

    def chunk(owner, way, step):
        return out.at[pl.ds(owner, 1), way, step]

    def ring(way, step, block):
        mine = chunk(core, way, step)
        return remote(
            block, mine, ring_s.at[way, step], ring_r.at[way, step], x, y, targets[way], core
        )

    def across(way, step, block):
        mine = chunk(core, way, step)
        return remote(
            block, mine, peer_s.at[way, step], peer_r.at[way, step], x, y, z, 1 - core
        )

    def issue(step):
        for way in range(2):
            ring(way, step, src.at[:, way, step]).start()
        for way in range(2):
            across(way, step, src.at[:, way, step]).start()

    @pl.when(source)
    def _():
        for step in range(AHEAD):
            issue(step)
        out[pl.ds(core, 1)] = src[...]

    yield
    for tick in range(CH + 2):
        if tick + AHEAD < CH:

            @pl.when(source)
            def _():
                for way in range(2):
                    ring(way, tick, src.at[:, way, tick]).wait_send()
                issue(tick + AHEAD)

        for way in range(2):
            for pos in range(1, 4):
                step = tick - (pos - 1)
                if not 0 <= step < CH:
                    continue

                @pl.when(used & (positions[way] == pos))
                def _():
                    mine = chunk(core, way, step)
                    ring(way, step, mine).wait_recv()
                    if pos < 3:
                        ring(way, step, mine).start()
                    across(way, step, mine).start()

        yield

    @pl.when(used)
    def _():
        for step in range(CH):
            for way in range(2):
                mine, other = chunk(core, way, step), chunk(1 - core, way, step)
                remote(
                    mine, other, peer_s.at[way, step], peer_r.at[way, step],
                    x, y, z, 1 - core,
                ).wait()
                left = positions[way] < 3
                if step + AHEAD < CH:
                    left = left & (z != 3)

                @pl.when(left)
                def _():
                    ring(way, step, mine).wait_send()

    yield


def reduce_steps(part, wide, src, out, bufs, sems, hand=None):
    got, acc, tot, got2, fin = bufs
    one_s, one_r, two_s, two_r, g_s, g_r, loc = sems
    x, y, z, core = place()
    units = [unit(part, u, core) for u in range(NP)]
    every = [(order, u) for u in range(NP) for order in range(2)]

    def share(order, u, at, pick):
        p, cols = units[u]
        if order == 0:
            return p, (x + at) % 4, pick, ROWS[0], cols
        return p, pick, (y + at) % 4, ROWS[1], cols

    def one(order, u, kind, way):
        step = 1 if way == 0 else 3
        if kind == 0:
            ref = src.at[share(order, u, 2, PAIR[way])]
        elif kind == 1:
            ref = src.at[share(order, u, step, PAIR[1 - way])]
        else:
            ref = acc.at[order, u, way]
        tx, ty = line(order, x, y, step)
        return remote(
            ref, got.at[order, u, kind, way],
            one_s.at[order, u, kind * 2 + way], one_r.at[order, u, kind * 2 + way],
            tx, ty, z, core,
        )

    for kind in (0, 1):
        for order, u in every:
            for way in range(2):
                one(order, u, kind, way).start()
    yield

    for order, u in every:
        for way in range(2):
            one(order, u, 0, way).wait_recv()
            step = 1 if way == 0 else 3
            acc[order, u, way] = (
                src[share(order, u, step, PAIR[way])] + got[order, u, 0, way]
            )
            one(order, u, 2, way).start()
    yield

    def two(order, u, d):
        tx, ty = line(1 - order, x, y, d)
        index = ty if order == 0 else tx
        return remote(
            tot.at[order, u, index], got2.at[order, u, d - 1],
            two_s.at[order, u, d], two_r.at[order, u, d], tx, ty, z, core,
        )

    for order, u in every:
        for kind in (1, 2):
            for way in range(2):
                one(order, u, kind, way).wait_recv()
        for half in range(2):
            base = src[share(order, u, 0, PAIR[half])]
            tot[order, u, PAIR[half]] = base + (
                got[order, u, 2, half] + got[order, u, 1, 1 - half]
            )
        for d in range(1, 4):
            two(order, u, d).start()
    yield

    for order, u in every:
        for d in range(1, 4):
            two(order, u, d).wait_recv()
        here = y if order == 0 else x
        total = (tot[order, u, here] + got2[order, u, 0]) + (
            got2[order, u, 1] + got2[order, u, 2]
        )
        if wide:
            out[core, u, x, y, ROWS[order]] = total
        else:
            fin[order, u, x if order == 0 else y] = total

    def sends():
        for order, u in every:
            for kind in range(3):
                for way in range(2):
                    one(order, u, kind, way).wait_send()
            for d in range(1, 4):
                two(order, u, d).wait_send()

    if wide:

        def at(u, px, py, rows):
            return out.at[core, u, px, py, rows]

        for _ in share_steps(at, *wide, hand):
            yield
        sends()
        yield
        return

    def to_line(order, u):
        mine = fin.at[order, u, x if order == 0 else y]
        target = (0, y) if order == 0 else (x, units[u][0])
        return remote(
            mine, mine, g_s.at[0, order, u], g_r.at[0, order, u, x if order == 0 else y],
            *target, z, core,
        )

    def target_lines(order, u, px, py):
        if order == 0:
            return out.at[u, pl.ds(0, 4), py, ROWS[0]]
        return out.at[u, px, pl.ds(0, 4), ROWS[1]]

    def to_root(order, u):
        return remote(
            fin.at[order, u], target_lines(order, u, x, y), g_s.at[1, order, u],
            g_r.at[1, order, u, y if order == 0 else x], 0, units[u][0], z, core,
        )

    def keep(order, u):
        return pltpu.make_async_copy(
            fin.at[order, u], target_lines(order, u, x, y), loc.at[order, u]
        )

    def on_line(order, u):
        return x == 0 if order == 0 else y == units[u][0]

    def at_root(u):
        return (x == 0) & (y == units[u][0])

    for order, u in every:

        @pl.when(jnp.logical_not(on_line(order, u)))
        def _():
            to_line(order, u).start()

    yield

    for order, u in every:

        @pl.when(on_line(order, u))
        def _():
            for d in range(1, 4):
                index = ((x if order == 0 else y) + d) % 4
                here = fin.at[order, u, index]
                remote(
                    here, here, g_s.at[0, order, u], g_r.at[0, order, u, index],
                    x, y, z, 1 - core,
                ).wait_recv()

        @pl.when(on_line(order, u) & jnp.logical_not(at_root(u)))
        def _():
            to_root(order, u).start()

        @pl.when(at_root(u))
        def _():
            keep(order, u).start()

    yield

    for order, u in every:

        @pl.when(jnp.logical_not(on_line(order, u)))
        def _():
            to_line(order, u).wait_send()

        @pl.when(on_line(order, u) & jnp.logical_not(at_root(u)))
        def _():
            to_root(order, u).wait_send()

        @pl.when(at_root(u))
        def _():
            keep(order, u).wait()
            for d in range(1, 4):
                px, py = (x + d) % 4, (y + d) % 4
                there = target_lines(order, u, px, py)
                remote(
                    there, there, g_s.at[1, order, u],
                    g_r.at[1, order, u, py if order == 0 else px], x, y, z, 1 - core,
                ).wait_recv()

    sends()
    yield


DMA = pltpu.SemaphoreType.DMA
SPREAD_SEMS = [
    DMA((3, 16)), DMA((3,)), DMA((2, 3, 4)), DMA((2, 3, 4)), DMA((2, 3, 4)), DMA((2, 3, 4)),
    DMA((3,)),
]
ALONG_SEMS = [DMA((2, CH))] * 4
REDUCE_BUFS = [
    pltpu.VMEM((2, 3, 3, 2, 2, 16, NB), F32),
    pltpu.VMEM((2, 3, 2, 2, 16, NB), F32),
    pltpu.VMEM((2, 3, 4, 16, NB), F32),
    pltpu.VMEM((2, 3, 3, 16, NB), F32),
    pltpu.VMEM((2, 3, 4, 16, NB), F32),
]
REDUCE_SEMS = [
    DMA((2, 3, 6)), DMA((2, 3, 6)), DMA((2, 3, 4)), DMA((2, 3, 4)), DMA((2, 2, 3)), DMA((2, 2, 3, 4)),
    DMA((2, 3)),
]
VM = pl.BlockSpec(memory_space=pltpu.VMEM)
ANY = pl.BlockSpec(memory_space=pl.ANY)


def drive(*plan):
    for steps, count in plan:
        for _ in range(count):
            next(steps)


def spread_kernel(own, cot, strips, blocks, half, *sems):
    x, y, z, core = place()
    greet(plane_and_peer(x, y, z, core))
    ex_s, ex_r, loc, half_s, half_r = sems[-5:]
    half_copy = remote(
        cot.at[pl.ds(256 * (1 - core), 256)], half, half_s.at[0], half_r.at[0], x, y, z, 1 - core
    )
    half_copy.start()
    def over(order, u, at, ref):
        px, py, rows = piece_line(order, x, y, at)
        there = blocks.at[core, u, px, py, rows]
        return (
            remote(ref, there, ex_s.at[order, u, at], ex_r.at[order, u, at], x, y, z, 1 - core),
            pltpu.make_async_copy(ref, there, loc.at[order, u, at]),
        )

    def hand(order, u, at, ref):
        for copy in over(order, u, at, ref):
            copy.start()

    drive((spread_steps(0, own, strips, sems[:7], hand), 7))
    for order, u, at in ALL_LINES:
        px, py, rows = piece_line(order, x, y, at)
        p, cols = unit(0, u, core)
        away, here = over(order, u, at, strips.at[p, px, py, rows, cols])
        here.wait()
        away.wait_send()
        got = blocks.at[1 - core, u, px, py, rows]
        remote(
            got, got, ex_s.at[order, u, at], ex_r.at[order, u, at], x, y, z, 1 - core
        ).wait_recv()
    half_copy.wait()


def comm(collective_id, mib):
    return pltpu.CompilerParams(
        collective_id=collective_id, has_side_effects=True, vmem_limit_bytes=mib << 20
    )


def spread(factor, cot):
    return pl.pallas_call(
        spread_kernel,
        out_shape=(
            jax.ShapeDtypeStruct((3, 4, 4, 32, 1024), F32),
            jax.ShapeDtypeStruct((2, 3, 4, 4, 32, NB), F32),
            jax.ShapeDtypeStruct((256, 1024), F32),
        ),
        in_specs=[ANY, ANY],
        out_specs=(ANY, VM, VM),
        scratch_shapes=SPREAD_SEMS + [DMA((2, 3, 4))] * 3 + [DMA((1,)), DMA((1,))],
        compiler_params=comm(0, 60),
    )(factor.reshape(4, 4, 32, 1024), cot)


def with_z(x, y, z, core):
    return plane_and_peer(x, y, z, core) + [
        (x, y, (z + 1) % 4, core), (x, y, (z + 3) % 4, core)
    ]


def along_spread_kernel(src, own, _, out, strips, *sems):
    greet(with_z(*place()))
    a = along_steps(src, out, sems[7:], lax.axis_index("row") >= NP)
    s = spread_steps(1, own, strips, sems[:7])
    drive((s, 1), (a, 1), (a, 2), (s, 1), (a, 2), (s, 1), (a, 4), (s, 1), (a, 2), (a, 1), (s, 3))


def along_spread(half, factor, strips):
    out, strips = pl.pallas_call(
        along_spread_kernel,
        out_shape=(
            jax.ShapeDtypeStruct((2, 2, CH, CR, 1536), F32),
            jax.ShapeDtypeStruct((3, 4, 4, 32, 1024), F32),
        ),
        in_specs=[VM, ANY, ANY],
        out_specs=(VM, ANY),
        scratch_shapes=SPREAD_SEMS + ALONG_SEMS,
        input_output_aliases={2: 1},
        compiler_params=comm(1, 60),
    )(half.reshape(1, 2, CH, CR, 1536), factor.reshape(4, 4, 32, 1024), strips)
    return out.reshape(512, 1536), strips.reshape(1536, 1024)


def reduce_kernel(src, out, *rest):
    x, y, z, core = place()
    greet(plane_and_peer(x, y, z, core))
    bufs, sems = rest[:5], rest[5:]
    ex_s, ex_r = sems[-2:]

    def over(order, u, at, ref):
        return remote(
            ref, ref, ex_s.at[order, u, at], ex_r.at[order, u, at], x, y, z, 1 - core
        )

    def hand(order, u, at, ref):
        over(order, u, at, ref).start()

    drive((reduce_steps(0, sems[7:11], src, out, bufs, sems[:7], hand), 9))
    for order, u, at in ALL_LINES:
        px, py, rows = piece_line(order, x, y, at)
        over(order, u, at, out.at[core, u, px, py, rows]).wait_send()
        over(order, u, at, out.at[1 - core, u, px, py, rows]).wait_recv()


def reduce_rows(part):
    return pl.pallas_call(
        reduce_kernel,
        out_shape=jax.ShapeDtypeStruct((2, 3, 4, 4, 32, NB), F32),
        in_specs=[VM],
        out_specs=VM,
        scratch_shapes=REDUCE_BUFS + REDUCE_SEMS + [DMA((2, 3, 4))] * 6,
        compiler_params=comm(2, 32),
    )(part.reshape(3, 4, 4, 32, 1024))


def along_reduce_kernel(src, part, out, rest_out, *rest):
    greet(with_z(*place()))
    bufs, sems = rest[:5], rest[5:]
    a = along_steps(src, out, sems[7:], lax.axis_index("row") < NP)
    r = reduce_steps(1, None, part, rest_out, bufs, sems[:7])
    drive((r, 1), (a, 3), (r, 1), (a, 3), (r, 1), (a, 2), (r, 1), (a, 1), (r, 1), (a, 3), (r, 1))


def along_reduce(half, part):
    out, rest_out = pl.pallas_call(
        along_reduce_kernel,
        out_shape=(
            jax.ShapeDtypeStruct((2, 2, CH, CR, 1536), F32),
            jax.ShapeDtypeStruct((3, 4, 4, 32, NB), F32),
        ),
        in_specs=[VM, VM],
        out_specs=(VM, VM),
        scratch_shapes=REDUCE_BUFS + REDUCE_SEMS + ALONG_SEMS,
        compiler_params=comm(3, 40),
    )(half.reshape(1, 2, CH, CR, 1536), part.reshape(3, 4, 4, 32, 1024))
    return out.reshape(512, 1536), rest_out.reshape(3, NB, NB)


BS = 128


def invert_kernel(d_ref, o_ref):
    rows = lax.broadcasted_iota(jnp.int32, (BS, BS), 0)
    cols = lax.broadcasted_iota(jnp.int32, (BS, BS), 1)
    diag = rows == cols
    for block in range(NP * (NB // BS)):
        which, at = block // (NB // BS), pl.ds(block % (NB // BS) * BS, BS)
        base = d_ref[which, at, at]
        scale = jnp.sum(jnp.where(diag, base, 0.0), axis=1, keepdims=True)
        o_ref[which, at, at] = jnp.where(diag, 1.0 / scale, 0.0)

    def level(step, carry):
        pick = ((rows >> (step + 1)) == (cols >> (step + 1))) & (
            ((rows >> step) & 1) > ((cols >> step) & 1)
        )
        for block in range(NP * (NB // BS)):
            which, at = block // (NB // BS), pl.ds(block % (NB // BS) * BS, BS)
            have = o_ref[which, at, at]
            below = jnp.where(pick, d_ref[which, at, at], 0.0)
            o_ref[which, at, at] = have - dot(dot(have, below, HI), have, HI)
        return carry

    lax.fori_loop(0, 7, level, 0)
    size = BS
    while size < NB:
        for which in range(NP):
            for base in range(0, NB, 2 * size):
                up, down = pl.ds(base, size), pl.ds(base + size, size)
                corner = dot(
                    dot(o_ref[which, down, down], d_ref[which, down, up], HI),
                    o_ref[which, up, up], HI,
                )
                o_ref[which, down, up] = -corner
                o_ref[which, up, down] = jnp.zeros((size, size), F32)
        size *= 2


def invert(blocks):
    vm = pl.BlockSpec(memory_space=pltpu.VMEM)
    return pl.pallas_call(
        invert_kernel,
        out_shape=jax.ShapeDtypeStruct((NP, NB, NB), F32),
        in_specs=[vm],
        out_specs=vm,
        compiler_params=pltpu.CompilerParams(vmem_limit_bytes=16 << 20),
    )(blocks)


def plan():
    rows = []
    l00, l10, l20, l11, l21, l22, t00, t10, t20, t11, t21, t22, i0, i1, i2 = range(15)
    w, p, q, a2, y2, s21, s21t, a1, y1, s20, s10, s20t, s10t, a0, y0, none = range(15, 31)

    def mm(a, b, to):
        rows.append((0, a, b, none, to, 1))

    def take(a, b, to):
        rows.append((0, a, b, to, to, -1))

    def turn(a, to, add=0):
        rows.append((1, a, a, a, to, add))

    def lower(a, twice):
        rows.append((2, a, a, a, a, twice))

    def adjoint(l, i, t, a, y):
        turn(l, w)
        lower(t, 2)
        mm(w, t, p)
        lower(p, 1)
        turn(i, w)
        mm(w, p, q)
        mm(q, i, a)
        lower(a, 1)
        turn(a, y, add=1)

    adjoint(l22, i2, t22, a2, y2)
    take(y2, l21, t21)
    take(y2, l20, t20)
    mm(t21, i1, s21)
    turn(s21, s21t)
    take(s21t, l21, t11)
    take(s21t, l20, t10)
    adjoint(l11, i1, t11, a1, y1)
    take(y1, l10, t10)
    take(s21, l10, t20)
    mm(t20, i0, s20)
    mm(t10, i0, s10)
    turn(s20, s20t)
    turn(s10, s10t)
    take(s20t, l20, t00)
    take(s10t, l10, t00)
    adjoint(l00, i0, t00, a0, y0)
    coupling = ((y0, s10t, s20t), (s10, y1, s21t), (s20, s21, y2))
    result = ((a0, a0, a0), (s10, a1, a1), (s20, s21, a2))
    return rows, [x + y for x, y in zip(coupling, result)]


PLAN, PICKS = plan()
BLK = 512


def chain_kernel(plan_ref, pick_ref, l_ref, t_ref, i_ref, q_ref, z_ref, m, high, low):
    row, col = lax.axis_index("row"), lax.axis_index("col")
    for n in range(6):
        m[n] = l_ref[n]
        m[6 + n] = t_ref[n]
    for n in range(3):
        m[12 + n] = i_ref[n]
    m[30] = jnp.zeros((NB, NB), F32)

    def op(n, carry):
        kind, a, b, c, to, value = (plan_ref[n, j] for j in range(6))
        scale = value.astype(F32)

        @pl.when(kind == 0)
        def _():
            def split(i, carry):
                at = pl.ds(pl.multiple_of(i * 128, 128), 128)
                own = m[b, at]
                top = own.astype(jnp.bfloat16)
                high[0, at] = top
                high[1, at] = (own - top.astype(F32)).astype(jnp.bfloat16)
                high[2, at] = top
                own = m[a, at] * scale
                top = own.astype(jnp.bfloat16)
                low[at, :NB] = top
                low[at, NB : 2 * NB] = top
                low[at, 2 * NB :] = (own - top.astype(F32)).astype(jnp.bfloat16)
                return carry

            lax.fori_loop(0, 4, split, 0)
            right = high[...].reshape(3 * NB, NB)
            m[to] = m[c] + jnp.dot(low[...], right, preferred_element_type=F32)

        @pl.when(kind == 2)
        def _():
            def mask(i, carry):
                at = pl.ds(pl.multiple_of(i * 128, 128), 128)
                rows = lax.broadcasted_iota(jnp.int32, (128, NB), 0) + i * 128
                cols = lax.broadcasted_iota(jnp.int32, (128, NB), 1)
                own = m[a, at]
                diag = jnp.where(rows == cols, own * (0.5 * scale), 0.0)
                m[to, at] = jnp.where(rows > cols, own, diag)
                return carry

            lax.fori_loop(0, 4, mask, 0)

        @pl.when(kind == 1)
        def _():
            def turn(i, carry):
                at = pl.ds(pl.multiple_of(i * 128, 128), 128)
                m[to, :, at] = m[a, at].T + m[a, :, at] * scale
                return carry

            lax.fori_loop(0, 4, turn, 0)

        return carry

    lax.fori_loop(0, len(PLAN), op, 0)
    p = jnp.minimum(row, 2)
    half = pl.ds(pl.multiple_of(col % 2 * 256, 256), 256)
    for j in range(3):
        q_ref[:, j * NB : (j + 1) * NB] = m[pick_ref[p, j], half]
        z_ref[j] = m[pick_ref[p, 3 + j]]


def chain(blocks, near, inv):
    smem = pl.BlockSpec(memory_space=pltpu.SMEM)
    return pl.pallas_call(
        chain_kernel,
        out_shape=(
            jax.ShapeDtypeStruct((256, 3 * NB), F32),
            jax.ShapeDtypeStruct((3, NB, NB), F32),
        ),
        in_specs=[smem, smem, VM, VM, VM],
        out_specs=(VM, VM),
        scratch_shapes=[
            pltpu.VMEM((31, NB, NB), F32),
            pltpu.VMEM((3, NB, NB), jnp.bfloat16),
            pltpu.VMEM((NB, 3 * NB), jnp.bfloat16),
        ],
        compiler_params=pltpu.CompilerParams(vmem_limit_bytes=55 << 20),
    )(jnp.array(PLAN, jnp.int32), jnp.array(PICKS, jnp.int32), blocks, near, inv)


def finish_kernel(cot, solved, mixed, strips, far, near, z, out, high, low, f_high, f_low):
    row, col = lax.axis_index("row"), lax.axis_index("col")
    core = col % 2
    r = jnp.minimum(row, 2)
    lower_rows = row >= NP

    @pl.when(col < 7)
    def _():
        def split(i, carry):
            at = pl.ds(pl.multiple_of(i * 128, 128), 128)
            value = jnp.where(lower_rows, solved[at], mixed[at])
            top = value.astype(jnp.bfloat16)
            f_high[at] = top
            f_low[at] = (value - top.astype(F32)).astype(jnp.bfloat16)
            return carry

        lax.fori_loop(0, 4, split, 0)

    for h in range(2):
        cols = pl.ds(h * NB, NB)
        if h == 0:
            use_far = (core == 0) | (row == 0)
            at_far = r * (1 - core)
            at_near = jnp.maximum(r - core, 0)
            plain = col < 7
        else:
            use_far = (core == 1) & (row < 2)
            at_far = jnp.minimum(r + 1, 2)
            at_near = r * (1 - core) + 2 * core
            plain = col < 6

        @pl.when(plain)
        def _():
            def begin(i, carry):
                at = pl.ds(pl.multiple_of(i * 128, 128), 128)
                total = jnp.where(use_far, far[at_far, at], near[core, at_near, at])
                out[at, cols] = jnp.where(lower_rows, cot[at, cols], total)
                return carry

            lax.fori_loop(0, 4, begin, 0)

            def deep(k, carry):
                def split(i, carry):
                    at = pl.ds(pl.multiple_of(i * 128, 128), 128)
                    from_at = pl.ds(pl.multiple_of(k * NB + i * 128, 128), 128)
                    value = strips[from_at, cols]
                    top = value.astype(jnp.bfloat16)
                    high[at] = top
                    low[at] = (value - top.astype(F32)).astype(jnp.bfloat16)
                    return carry

                lax.fori_loop(0, 4, split, 0)
                inner = pl.ds(pl.multiple_of(k * NB, NB), NB)

                def product(i, carry):
                    at = pl.ds(pl.multiple_of(i * BLK, BLK), BLK)
                    top, rest, right = f_high[at, inner], f_low[at, inner], high[...]
                    total = jnp.dot(rest, right, preferred_element_type=F32)
                    total += jnp.dot(top, low[...], preferred_element_type=F32)
                    total += jnp.dot(top, right, preferred_element_type=F32)
                    out[at, cols] = out[at, cols] - total
                    return carry

                lax.fori_loop(0, NB // BLK, product, 0)
                return carry

            lax.fori_loop(0, NP, deep, 0)

        @pl.when(jnp.logical_not(plain))
        def _():
            def move(i, carry):
                at = pl.ds(pl.multiple_of(i * 128, 128), 128)
                if h == 0:
                    upper = jnp.where(row == 0, cot[at, cols], z[1, at])
                    out[at, cols] = jnp.where(lower_rows, solved[at, NB : 2 * NB], upper)
                else:
                    upper = jnp.where(row == 2, z[2, at], cot[at, cols])
                    last = jnp.where(lower_rows, solved[at, 2 * NB :], upper)
                    first = jnp.where(lower_rows, solved[at, :NB], z[0, at])
                    out[at, cols] = jnp.where(col == 7, last, first)
                return carry

            lax.fori_loop(0, 4, move, 0)


def finish(cot, solved, mixed, strips, far, near, z):
    return pl.pallas_call(
        finish_kernel,
        out_shape=jax.ShapeDtypeStruct((NB, 2 * NB), F32),
        in_specs=[VM] * 7,
        out_specs=VM,
        scratch_shapes=[
            pltpu.VMEM((NB, NB), jnp.bfloat16),
            pltpu.VMEM((NB, NB), jnp.bfloat16),
            pltpu.VMEM((NB, 3 * NB), jnp.bfloat16),
            pltpu.VMEM((NB, 3 * NB), jnp.bfloat16),
        ],
        compiler_params=pltpu.CompilerParams(vmem_limit_bytes=40 << 20),
    )(cot, solved, mixed, strips, far, near, z)


def shards(factor, cot):
    row = lax.axis_index("row")
    col = lax.axis_index("col")
    core = col % 2
    strips, blocks, other_half = spread(factor, cot)
    blocks = blocks.reshape(2, 3, NB, NB)
    l = {
        0: blocks[0, 0], 10: blocks[0, 1], 20: blocks[0, 2],
        11: blocks[1, 0], 21: blocks[1, 1], 22: blocks[1, 2],
    }
    inv = invert(jnp.stack([l[0], l[11], l[22]]))
    my_half = lax.dynamic_slice(cot, (core * 256, 0), (256, 1024))
    g6 = jnp.where(core == 0, my_half, other_half)
    g7 = jnp.where(core == 0, other_half, my_half)
    s2 = dot(g7[:, NB:], inv[2])
    s1 = dot(g7[:, :NB] - dot(s2, l[21]), inv[1])
    s0 = dot(g6[:, NB:] - dot(s2, l[20]) - dot(s1, l[10]), inv[0])
    solved, strips = along_spread(jnp.concatenate([s0, s1, s2], axis=1), factor, strips)
    lower_rows = row >= NP
    part = jnp.where(lower_rows, -dot_t(solved, factor), 0.0).reshape(3, NB, 1024)
    which = lax.broadcasted_iota(jnp.int32, (3, 1, 1), 0)
    part = jnp.where(which == row, cot[None], part)
    near = reduce_rows(part).reshape(2, 3, NB, NB)
    mixed_half, z = chain(blocks.reshape(6, NB, NB), near.reshape(6, NB, NB), inv)
    mixed, far = along_reduce(mixed_half, part)
    return finish(cot, solved, mixed, strips, far, near, z)


def solution(mesh):
    placed = (P("row", "col"), P("row", "col"))
    return jax.shard_map(
        shards, mesh=mesh, in_specs=placed, out_specs=P("row", "col"), check_vma=False
    )
```

```python
import jax
import jax.numpy as jnp
from jax import lax
from jax.experimental import pallas as pl
from jax.experimental.pallas import tpu as pltpu
from jax.sharding import PartitionSpec as P

NB = 512
NP = 3
MESH = pl.DeviceIdType.MESH
HI = lax.Precision.HIGHEST
MID = lax.Precision.HIGH
F32 = jnp.float32


def dot(a, b, precision=MID):
    return jnp.dot(a, b, precision=precision, preferred_element_type=F32)


def dot_t(a, b, precision=MID):
    return lax.dot_general(
        a, b, (((0,), (0,)), ((), ())), precision=precision, preferred_element_type=F32
    )


def place():
    row = lax.axis_index("row")
    col = lax.axis_index("col")
    return row // 4, row % 4, col // 2, col % 2


def remote(src, dst, send, recv, x, y, z, core):
    return pltpu.make_async_remote_copy(
        src_ref=src,
        dst_ref=dst,
        send_sem=send,
        recv_sem=recv,
        device_id=(x * 4 + y, z * 2 + core),
        device_id_type=MESH,
    )


def greet(devices):
    barrier = pltpu.get_barrier_semaphore()
    for x, y, z, core in devices:
        pl.semaphore_signal(
            barrier, inc=1, device_id=(x * 4 + y, z * 2 + core), device_id_type=MESH
        )
    pl.semaphore_wait(barrier, len(devices))


def plane_and_peer(x, y, z, core):
    out = []
    for dx in range(4):
        for dy in range(4):
            if dx or dy:
                out.append(((x + dx) % 4, (y + dy) % 4, z, core))
    return out + [(x, y, z, 1 - core)]


CH = 8
CR = 128 // CH
LEFT, RIGHT = pl.ds(0, NB), pl.ds(NB, NB)
ROWS = (pl.ds(0, 16), pl.ds(16, 16))
PAIR = (pl.ds(0, 2), pl.ds(2, 2))


def unit(part, u, core):
    if part == 0:
        p = u + core if u < 2 else 2
        off = NB * (1 - core) if u < 2 else NB
    else:
        p = u - core if u >= 1 else 0
        off = NB * core if u >= 1 else 0
    if isinstance(off, int):
        return p, pl.ds(off, NB)
    return p, pl.ds(pl.multiple_of(off, NB), NB)


def line(order, x, y, d):
    return ((x + d) % 4, y) if order == 0 else (x, (y + d) % 4)


def spread_steps(part, own, strips, sems, hand=None):
    scat_s, scat_r, one_s, one_r, two_s, two_r, loc = sems
    x, y, z, core = place()
    units = [unit(part, u, core) for u in range(NP)]

    def piece(ref, u, px, py):
        p, cols = units[u]
        if ref is own:
            return own.at[px, py, :, cols]
        return strips.at[p, px, py, :, cols]

    def scatter(u, d):
        tx, ty = (x + d // 4) % 4, (y + d % 4) % 4
        return remote(
            piece(own, u, tx, ty), piece(strips, u, tx, ty),
            scat_s.at[u, d], scat_r.at[u], tx, ty, z, core,
        )

    def keep(u):
        return pltpu.make_async_copy(piece(own, u, x, y), piece(strips, u, x, y), loc.at[u])

    roots = [(x == 0) & (y == units[u][0]) for u in range(NP)]
    for u in range(NP):

        @pl.when(roots[u])
        def _():
            keep(u).start()
            for d in range(15, 0, -1):
                scatter(u, d).start()

    yield

    for u in range(NP):

        @pl.when(roots[u])
        def _():
            keep(u).wait()

        @pl.when(jnp.logical_not(roots[u]))
        def _():
            here = piece(strips, u, x, y)
            remote(here, here, scat_s.at[u, 0], scat_r.at[u], x, y, z, 1 - core).wait_recv()

    def at(u, px, py, rows):
        p, cols = units[u]
        return strips.at[p, px, py, rows, cols]

    for _ in share_steps(at, one_s, one_r, two_s, two_r, hand):
        yield

    for u in range(NP):

        @pl.when(roots[u])
        def _():
            for d in range(1, 16):
                scatter(u, d).wait_send()

    yield


def piece_line(order, x, y, at):
    if order == 0:
        return pl.ds(0, 4), (y + at) % 4, ROWS[0]
    return (x + at) % 4, pl.ds(0, 4), ROWS[1]


ALL_LINES = [(order, u, at) for order in range(2) for u in range(NP) for at in range(4)]


def share_steps(ref_at, one_s, one_r, two_s, two_r, hand=None):
    x, y, z, core = place()
    every = [(order, u) for u in range(NP) for order in range(2)]
    first = []
    for order, u in every:
        for d in range(1, 4):
            here = ref_at(u, x, y, ROWS[order])
            tx, ty = line(order, x, y, d)
            first.append(
                remote(
                    here, here, one_s.at[order, u, d], one_r.at[order, u, d], tx, ty, z, core
                )
            )
    for copy in first:
        copy.start()
    yield

    for copy in first:
        copy.wait_recv()

    def block(order, u, at, pick):
        if order == 0:
            return ref_at(u, pick, (y + at) % 4, ROWS[0])
        return ref_at(u, (x + at) % 4, pick, ROWS[1])

    def second(order, u, kind):
        whole = pl.ds(0, 4)
        at, pick, d = (
            (0, whole, 1), (0, whole, 3), (3, PAIR[0], 1), (1, PAIR[1], 3)
        )[kind]
        ref = block(order, u, at, pick)
        tx, ty = line(1 - order, x, y, d)
        return remote(
            ref, ref, two_s.at[order, u, kind], two_r.at[order, u, kind], tx, ty, z, core
        )

    def arrival(order, u, kind):
        whole = pl.ds(0, 4)
        at, pick = ((3, whole), (1, whole), (2, PAIR[0]), (2, PAIR[1]))[kind]
        ref = block(order, u, at, pick)
        return remote(
            ref, ref, two_s.at[order, u, kind], two_r.at[order, u, kind], x, y, z, 1 - core
        )

    whole_line = pl.ds(0, 4)
    for order, u in every:
        for kind in (0, 1):
            second(order, u, kind).start()
    if hand:
        for order, u in every:
            hand(order, u, 0, block(order, u, 0, whole_line))
    yield

    for order, u in every:
        for kind in (0, 1):
            arrival(order, u, kind).wait_recv()
            second(order, u, kind + 2).start()
    if hand:
        for order, u in every:
            for at in (3, 1):
                hand(order, u, at, block(order, u, at, whole_line))
    yield

    for order, u in every:
        for kind in (2, 3):
            arrival(order, u, kind).wait_recv()
        if hand:
            hand(order, u, 2, block(order, u, 2, whole_line))
    yield

    for copy in first:
        copy.wait_send()
    for order, u in every:
        for kind in range(4):
            second(order, u, kind).wait_send()
    yield


AHEAD = 5


def along_steps(src, out, sems, used):
    ring_s, ring_r, peer_s, peer_r = sems
    x, y, z, core = place()
    up, down = (z + 1) % 4, (z + 3) % 4
    positions = (up, 3 - z)
    targets = (up, down)
    source = used & (z == 3)

    def chunk(owner, way, step):
        return out.at[pl.ds(owner, 1), way, step]

    def ring(way, step, block):
        mine = chunk(core, way, step)
        return remote(
            block, mine, ring_s.at[way, step], ring_r.at[way, step], x, y, targets[way], core
        )

    def across(way, step, block):
        mine = chunk(core, way, step)
        return remote(
            block, mine, peer_s.at[way, step], peer_r.at[way, step], x, y, z, 1 - core
        )

    def issue(step):
        for way in range(2):
            ring(way, step, src.at[:, way, step]).start()
        for way in range(2):
            across(way, step, src.at[:, way, step]).start()

    @pl.when(source)
    def _():
        for step in range(AHEAD):
            issue(step)
        out[pl.ds(core, 1)] = src[...]

    yield
    for tick in range(CH + 2):
        if tick + AHEAD < CH:

            @pl.when(source)
            def _():
                for way in range(2):
                    ring(way, tick, src.at[:, way, tick]).wait_send()
                issue(tick + AHEAD)

        for way in range(2):
            for pos in range(1, 4):
                step = tick - (pos - 1)
                if not 0 <= step < CH:
                    continue

                @pl.when(used & (positions[way] == pos))
                def _():
                    mine = chunk(core, way, step)
                    ring(way, step, mine).wait_recv()
                    if pos < 3:
                        ring(way, step, mine).start()
                    across(way, step, mine).start()

        yield

    @pl.when(used)
    def _():
        for step in range(CH):
            for way in range(2):
                mine, other = chunk(core, way, step), chunk(1 - core, way, step)
                remote(
                    mine, other, peer_s.at[way, step], peer_r.at[way, step],
                    x, y, z, 1 - core,
                ).wait()
                left = positions[way] < 3
                if step + AHEAD < CH:
                    left = left & (z != 3)

                @pl.when(left)
                def _():
                    ring(way, step, mine).wait_send()

    yield


def reduce_steps(part, wide, src, out, bufs, sems, hand=None):
    got, acc, tot, got2, fin = bufs
    one_s, one_r, two_s, two_r, g_s, g_r, loc = sems
    x, y, z, core = place()
    units = [unit(part, u, core) for u in range(NP)]
    every = [(order, u) for u in range(NP) for order in range(2)]

    def share(order, u, at, pick):
        p, cols = units[u]
        if order == 0:
            return p, (x + at) % 4, pick, ROWS[0], cols
        return p, pick, (y + at) % 4, ROWS[1], cols

    def one(order, u, kind, way):
        step = 1 if way == 0 else 3
        if kind == 0:
            ref = src.at[share(order, u, 2, PAIR[way])]
        elif kind == 1:
            ref = src.at[share(order, u, step, PAIR[1 - way])]
        else:
            ref = acc.at[order, u, way]
        tx, ty = line(order, x, y, step)
        return remote(
            ref, got.at[order, u, kind, way],
            one_s.at[order, u, kind * 2 + way], one_r.at[order, u, kind * 2 + way],
            tx, ty, z, core,
        )

    for kind in (0, 1):
        for order, u in every:
            for way in range(2):
                one(order, u, kind, way).start()
    yield

    for order, u in every:
        for way in range(2):
            one(order, u, 0, way).wait_recv()
            step = 1 if way == 0 else 3
            acc[order, u, way] = (
                src[share(order, u, step, PAIR[way])] + got[order, u, 0, way]
            )
            one(order, u, 2, way).start()
    yield

    def two(order, u, d):
        tx, ty = line(1 - order, x, y, d)
        index = ty if order == 0 else tx
        return remote(
            tot.at[order, u, index], got2.at[order, u, d - 1],
            two_s.at[order, u, d], two_r.at[order, u, d], tx, ty, z, core,
        )

    for order, u in every:
        for kind in (1, 2):
            for way in range(2):
                one(order, u, kind, way).wait_recv()
        for half in range(2):
            base = src[share(order, u, 0, PAIR[half])]
            tot[order, u, PAIR[half]] = base + (
                got[order, u, 2, half] + got[order, u, 1, 1 - half]
            )
        for d in range(1, 4):
            two(order, u, d).start()
    yield

    for order, u in every:
        for d in range(1, 4):
            two(order, u, d).wait_recv()
        here = y if order == 0 else x
        total = (tot[order, u, here] + got2[order, u, 0]) + (
            got2[order, u, 1] + got2[order, u, 2]
        )
        if wide:
            out[core, u, x, y, ROWS[order]] = total
        else:
            fin[order, u, x if order == 0 else y] = total

    def sends():
        for order, u in every:
            for kind in range(3):
                for way in range(2):
                    one(order, u, kind, way).wait_send()
            for d in range(1, 4):
                two(order, u, d).wait_send()

    if wide:

        def at(u, px, py, rows):
            return out.at[core, u, px, py, rows]

        for _ in share_steps(at, *wide, hand):
            yield
        sends()
        yield
        return

    def to_line(order, u):
        mine = fin.at[order, u, x if order == 0 else y]
        target = (0, y) if order == 0 else (x, units[u][0])
        return remote(
            mine, mine, g_s.at[0, order, u], g_r.at[0, order, u, x if order == 0 else y],
            *target, z, core,
        )

    def target_lines(order, u, px, py):
        if order == 0:
            return out.at[u, pl.ds(0, 4), py, ROWS[0]]
        return out.at[u, px, pl.ds(0, 4), ROWS[1]]

    def to_root(order, u):
        return remote(
            fin.at[order, u], target_lines(order, u, x, y), g_s.at[1, order, u],
            g_r.at[1, order, u, y if order == 0 else x], 0, units[u][0], z, core,
        )

    def keep(order, u):
        return pltpu.make_async_copy(
            fin.at[order, u], target_lines(order, u, x, y), loc.at[order, u]
        )

    def on_line(order, u):
        return x == 0 if order == 0 else y == units[u][0]

    def at_root(u):
        return (x == 0) & (y == units[u][0])

    for order, u in every:

        @pl.when(jnp.logical_not(on_line(order, u)))
        def _():
            to_line(order, u).start()

    yield

    for order, u in every:

        @pl.when(on_line(order, u))
        def _():
            for d in range(1, 4):
                index = ((x if order == 0 else y) + d) % 4
                here = fin.at[order, u, index]
                remote(
                    here, here, g_s.at[0, order, u], g_r.at[0, order, u, index],
                    x, y, z, 1 - core,
                ).wait_recv()

        @pl.when(on_line(order, u) & jnp.logical_not(at_root(u)))
        def _():
            to_root(order, u).start()

        @pl.when(at_root(u))
        def _():
            keep(order, u).start()

    yield

    for order, u in every:

        @pl.when(jnp.logical_not(on_line(order, u)))
        def _():
            to_line(order, u).wait_send()

        @pl.when(on_line(order, u) & jnp.logical_not(at_root(u)))
        def _():
            to_root(order, u).wait_send()

        @pl.when(at_root(u))
        def _():
            keep(order, u).wait()
            for d in range(1, 4):
                px, py = (x + d) % 4, (y + d) % 4
                there = target_lines(order, u, px, py)
                remote(
                    there, there, g_s.at[1, order, u],
                    g_r.at[1, order, u, py if order == 0 else px], x, y, z, 1 - core,
                ).wait_recv()

    sends()
    yield


DMA = pltpu.SemaphoreType.DMA
SPREAD_SEMS = [
    DMA((3, 16)), DMA((3,)), DMA((2, 3, 4)), DMA((2, 3, 4)), DMA((2, 3, 4)), DMA((2, 3, 4)),
    DMA((3,)),
]
ALONG_SEMS = [DMA((2, CH))] * 4
REDUCE_BUFS = [
    pltpu.VMEM((2, 3, 3, 2, 2, 16, NB), F32),
    pltpu.VMEM((2, 3, 2, 2, 16, NB), F32),
    pltpu.VMEM((2, 3, 4, 16, NB), F32),
    pltpu.VMEM((2, 3, 3, 16, NB), F32),
    pltpu.VMEM((2, 3, 4, 16, NB), F32),
]
REDUCE_SEMS = [
    DMA((2, 3, 6)), DMA((2, 3, 6)), DMA((2, 3, 4)), DMA((2, 3, 4)), DMA((2, 2, 3)), DMA((2, 2, 3, 4)),
    DMA((2, 3)),
]
VM = pl.BlockSpec(memory_space=pltpu.VMEM)
ANY = pl.BlockSpec(memory_space=pl.ANY)


def drive(*plan):
    for steps, count in plan:
        for _ in range(count):
            next(steps)


def spread_kernel(own, cot, strips, blocks, half, *sems):
    x, y, z, core = place()
    greet(plane_and_peer(x, y, z, core))
    ex_s, ex_r, loc, half_s, half_r = sems[-5:]
    half_copy = remote(
        cot.at[pl.ds(256 * (1 - core), 256)], half, half_s.at[0], half_r.at[0], x, y, z, 1 - core
    )
    half_copy.start()
    def over(order, u, at, ref):
        px, py, rows = piece_line(order, x, y, at)
        there = blocks.at[core, u, px, py, rows]
        return (
            remote(ref, there, ex_s.at[order, u, at], ex_r.at[order, u, at], x, y, z, 1 - core),
            pltpu.make_async_copy(ref, there, loc.at[order, u, at]),
        )

    def hand(order, u, at, ref):
        for copy in over(order, u, at, ref):
            copy.start()

    drive((spread_steps(0, own, strips, sems[:7], hand), 7))
    for order, u, at in ALL_LINES:
        px, py, rows = piece_line(order, x, y, at)
        p, cols = unit(0, u, core)
        away, here = over(order, u, at, strips.at[p, px, py, rows, cols])
        here.wait()
        away.wait_send()
        got = blocks.at[1 - core, u, px, py, rows]
        remote(
            got, got, ex_s.at[order, u, at], ex_r.at[order, u, at], x, y, z, 1 - core
        ).wait_recv()
    half_copy.wait()


def comm(collective_id, mib):
    return pltpu.CompilerParams(
        collective_id=collective_id, has_side_effects=True, vmem_limit_bytes=mib << 20
    )


def spread(factor, cot):
    return pl.pallas_call(
        spread_kernel,
        out_shape=(
            jax.ShapeDtypeStruct((3, 4, 4, 32, 1024), F32),
            jax.ShapeDtypeStruct((2, 3, 4, 4, 32, NB), F32),
            jax.ShapeDtypeStruct((256, 1024), F32),
        ),
        in_specs=[ANY, ANY],
        out_specs=(ANY, VM, VM),
        scratch_shapes=SPREAD_SEMS + [DMA((2, 3, 4))] * 3 + [DMA((1,)), DMA((1,))],
        compiler_params=comm(0, 60),
    )(factor.reshape(4, 4, 32, 1024), cot)


def with_z(x, y, z, core):
    return plane_and_peer(x, y, z, core) + [
        (x, y, (z + 1) % 4, core), (x, y, (z + 3) % 4, core)
    ]


def along_spread_kernel(src, own, _, out, strips, *sems):
    greet(with_z(*place()))
    a = along_steps(src, out, sems[7:], lax.axis_index("row") >= NP)
    s = spread_steps(1, own, strips, sems[:7])
    drive((s, 1), (a, 5), (s, 1), (a, 2), (s, 1), (a, 3), (s, 1), (a, 1), (s, 1), (a, 1), (s, 2))


def along_spread(half, factor, strips):
    out, strips = pl.pallas_call(
        along_spread_kernel,
        out_shape=(
            jax.ShapeDtypeStruct((2, 2, CH, CR, 1536), F32),
            jax.ShapeDtypeStruct((3, 4, 4, 32, 1024), F32),
        ),
        in_specs=[VM, ANY, ANY],
        out_specs=(VM, ANY),
        scratch_shapes=SPREAD_SEMS + ALONG_SEMS,
        input_output_aliases={2: 1},
        compiler_params=comm(1, 60),
    )(half.reshape(1, 2, CH, CR, 1536), factor.reshape(4, 4, 32, 1024), strips)
    return out.reshape(512, 1536), strips.reshape(1536, 1024)


def reduce_kernel(src, out, *rest):
    x, y, z, core = place()
    greet(plane_and_peer(x, y, z, core))
    bufs, sems = rest[:5], rest[5:]
    ex_s, ex_r = sems[-2:]

    def over(order, u, at, ref):
        return remote(
            ref, ref, ex_s.at[order, u, at], ex_r.at[order, u, at], x, y, z, 1 - core
        )

    def hand(order, u, at, ref):
        over(order, u, at, ref).start()

    drive((reduce_steps(0, sems[7:11], src, out, bufs, sems[:7], hand), 9))
    for order, u, at in ALL_LINES:
        px, py, rows = piece_line(order, x, y, at)
        over(order, u, at, out.at[core, u, px, py, rows]).wait_send()
        over(order, u, at, out.at[1 - core, u, px, py, rows]).wait_recv()


def reduce_rows(part):
    return pl.pallas_call(
        reduce_kernel,
        out_shape=jax.ShapeDtypeStruct((2, 3, 4, 4, 32, NB), F32),
        in_specs=[VM],
        out_specs=VM,
        scratch_shapes=REDUCE_BUFS + REDUCE_SEMS + [DMA((2, 3, 4))] * 6,
        compiler_params=comm(2, 32),
    )(part.reshape(3, 4, 4, 32, 1024))


def along_reduce_kernel(src, part, out, rest_out, *rest):
    greet(with_z(*place()))
    bufs, sems = rest[:5], rest[5:]
    a = along_steps(src, out, sems[7:], lax.axis_index("row") < NP)
    r = reduce_steps(1, None, part, rest_out, bufs, sems[:7])
    drive((r, 1), (a, 3), (r, 1), (a, 3), (r, 1), (a, 2), (r, 1), (a, 1), (r, 1), (a, 3), (r, 1))


def along_reduce(half, part):
    out, rest_out = pl.pallas_call(
        along_reduce_kernel,
        out_shape=(
            jax.ShapeDtypeStruct((2, 2, CH, CR, 1536), F32),
            jax.ShapeDtypeStruct((3, 4, 4, 32, NB), F32),
        ),
        in_specs=[VM, VM],
        out_specs=(VM, VM),
        scratch_shapes=REDUCE_BUFS + REDUCE_SEMS + ALONG_SEMS,
        compiler_params=comm(3, 40),
    )(half.reshape(1, 2, CH, CR, 1536), part.reshape(3, 4, 4, 32, 1024))
    return out.reshape(512, 1536), rest_out.reshape(3, NB, NB)


BS = 128


def invert_kernel(d_ref, o_ref):
    rows = lax.broadcasted_iota(jnp.int32, (BS, BS), 0)
    cols = lax.broadcasted_iota(jnp.int32, (BS, BS), 1)
    diag = rows == cols
    for block in range(NP * (NB // BS)):
        which, at = block // (NB // BS), pl.ds(block % (NB // BS) * BS, BS)
        base = d_ref[which, at, at]
        scale = jnp.sum(jnp.where(diag, base, 0.0), axis=1, keepdims=True)
        o_ref[which, at, at] = jnp.where(diag, 1.0 / scale, 0.0)

    def level(step, carry):
        pick = ((rows >> (step + 1)) == (cols >> (step + 1))) & (
            ((rows >> step) & 1) > ((cols >> step) & 1)
        )
        for block in range(NP * (NB // BS)):
            which, at = block // (NB // BS), pl.ds(block % (NB // BS) * BS, BS)
            have = o_ref[which, at, at]
            below = jnp.where(pick, d_ref[which, at, at], 0.0)
            o_ref[which, at, at] = have - dot(dot(have, below, HI), have, HI)
        return carry

    lax.fori_loop(0, 7, level, 0)
    size = BS
    while size < NB:
        for which in range(NP):
            for base in range(0, NB, 2 * size):
                up, down = pl.ds(base, size), pl.ds(base + size, size)
                corner = dot(
                    dot(o_ref[which, down, down], d_ref[which, down, up], HI),
                    o_ref[which, up, up], HI,
                )
                o_ref[which, down, up] = -corner
                o_ref[which, up, down] = jnp.zeros((size, size), F32)
        size *= 2


def invert(blocks):
    vm = pl.BlockSpec(memory_space=pltpu.VMEM)
    return pl.pallas_call(
        invert_kernel,
        out_shape=jax.ShapeDtypeStruct((NP, NB, NB), F32),
        in_specs=[vm],
        out_specs=vm,
        compiler_params=pltpu.CompilerParams(vmem_limit_bytes=16 << 20),
    )(blocks)


def plan():
    rows = []
    l00, l10, l20, l11, l21, l22, t00, t10, t20, t11, t21, t22, i0, i1, i2 = range(15)
    w, p, q, a2, y2, s21, s21t, a1, y1, s20, s10, s20t, s10t, a0, y0, none = range(15, 31)

    def mm(a, b, to):
        rows.append((0, a, b, none, to, 1))

    def take(a, b, to):
        rows.append((0, a, b, to, to, -1))

    def turn(a, to, add=0):
        rows.append((1, a, a, a, to, add))

    def lower(a, twice):
        rows.append((2, a, a, a, a, twice))

    def adjoint(l, i, t, a, y):
        turn(l, w)
        lower(t, 2)
        mm(w, t, p)
        lower(p, 1)
        turn(i, w)
        mm(w, p, q)
        mm(q, i, a)
        lower(a, 1)
        turn(a, y, add=1)

    adjoint(l22, i2, t22, a2, y2)
    take(y2, l21, t21)
    take(y2, l20, t20)
    mm(t21, i1, s21)
    turn(s21, s21t)
    take(s21t, l21, t11)
    take(s21t, l20, t10)
    adjoint(l11, i1, t11, a1, y1)
    take(y1, l10, t10)
    take(s21, l10, t20)
    mm(t20, i0, s20)
    mm(t10, i0, s10)
    turn(s20, s20t)
    turn(s10, s10t)
    take(s20t, l20, t00)
    take(s10t, l10, t00)
    adjoint(l00, i0, t00, a0, y0)
    coupling = ((y0, s10t, s20t), (s10, y1, s21t), (s20, s21, y2))
    result = ((a0, a0, a0), (s10, a1, a1), (s20, s21, a2))
    return rows, [x + y for x, y in zip(coupling, result)]


PLAN, PICKS = plan()
BLK = 512


def chain_kernel(plan_ref, pick_ref, l_ref, t_ref, i_ref, q_ref, z_ref, m, high, low):
    row, col = lax.axis_index("row"), lax.axis_index("col")
    for n in range(6):
        m[n] = l_ref[n]
        m[6 + n] = t_ref[n]
    for n in range(3):
        m[12 + n] = i_ref[n]
    m[30] = jnp.zeros((NB, NB), F32)

    def op(n, carry):
        kind, a, b, c, to, value = (plan_ref[n, j] for j in range(6))
        scale = value.astype(F32)

        @pl.when(kind == 0)
        def _():
            def split(i, carry):
                at = pl.ds(pl.multiple_of(i * 128, 128), 128)
                own = m[b, at]
                top = own.astype(jnp.bfloat16)
                high[0, at] = top
                high[1, at] = (own - top.astype(F32)).astype(jnp.bfloat16)
                high[2, at] = top
                own = m[a, at] * scale
                top = own.astype(jnp.bfloat16)
                low[at, :NB] = top
                low[at, NB : 2 * NB] = top
                low[at, 2 * NB :] = (own - top.astype(F32)).astype(jnp.bfloat16)
                return carry

            lax.fori_loop(0, 4, split, 0)
            right = high[...].reshape(3 * NB, NB)
            m[to] = m[c] + jnp.dot(low[...], right, preferred_element_type=F32)

        @pl.when(kind == 2)
        def _():
            def mask(i, carry):
                at = pl.ds(pl.multiple_of(i * 128, 128), 128)
                rows = lax.broadcasted_iota(jnp.int32, (128, NB), 0) + i * 128
                cols = lax.broadcasted_iota(jnp.int32, (128, NB), 1)
                own = m[a, at]
                diag = jnp.where(rows == cols, own * (0.5 * scale), 0.0)
                m[to, at] = jnp.where(rows > cols, own, diag)
                return carry

            lax.fori_loop(0, 4, mask, 0)

        @pl.when(kind == 1)
        def _():
            def turn(i, carry):
                at = pl.ds(pl.multiple_of(i * 128, 128), 128)
                m[to, :, at] = m[a, at].T + m[a, :, at] * scale
                return carry

            lax.fori_loop(0, 4, turn, 0)

        return carry

    lax.fori_loop(0, len(PLAN), op, 0)
    p = jnp.minimum(row, 2)
    half = pl.ds(pl.multiple_of(col % 2 * 256, 256), 256)
    for j in range(3):
        q_ref[:, j * NB : (j + 1) * NB] = m[pick_ref[p, j], half]
        z_ref[j] = m[pick_ref[p, 3 + j]]


def chain(blocks, near, inv):
    smem = pl.BlockSpec(memory_space=pltpu.SMEM)
    return pl.pallas_call(
        chain_kernel,
        out_shape=(
            jax.ShapeDtypeStruct((256, 3 * NB), F32),
            jax.ShapeDtypeStruct((3, NB, NB), F32),
        ),
        in_specs=[smem, smem, VM, VM, VM],
        out_specs=(VM, VM),
        scratch_shapes=[
            pltpu.VMEM((31, NB, NB), F32),
            pltpu.VMEM((3, NB, NB), jnp.bfloat16),
            pltpu.VMEM((NB, 3 * NB), jnp.bfloat16),
        ],
        compiler_params=pltpu.CompilerParams(vmem_limit_bytes=55 << 20),
    )(jnp.array(PLAN, jnp.int32), jnp.array(PICKS, jnp.int32), blocks, near, inv)


def finish_kernel(cot, solved, mixed, strips, far, near, z, out, high, low, f_high, f_low):
    row, col = lax.axis_index("row"), lax.axis_index("col")
    core = col % 2
    r = jnp.minimum(row, 2)
    lower_rows = row >= NP

    @pl.when(col < 7)
    def _():
        def split(i, carry):
            at = pl.ds(pl.multiple_of(i * 128, 128), 128)
            value = jnp.where(lower_rows, solved[at], mixed[at])
            top = value.astype(jnp.bfloat16)
            f_high[at] = top
            f_low[at] = (value - top.astype(F32)).astype(jnp.bfloat16)
            return carry

        lax.fori_loop(0, 4, split, 0)

    for h in range(2):
        cols = pl.ds(h * NB, NB)
        if h == 0:
            use_far = (core == 0) | (row == 0)
            at_far = r * (1 - core)
            at_near = jnp.maximum(r - core, 0)
            plain = col < 7
        else:
            use_far = (core == 1) & (row < 2)
            at_far = jnp.minimum(r + 1, 2)
            at_near = r * (1 - core) + 2 * core
            plain = col < 6

        @pl.when(plain)
        def _():
            def begin(i, carry):
                at = pl.ds(pl.multiple_of(i * 128, 128), 128)
                total = jnp.where(use_far, far[at_far, at], near[core, at_near, at])
                out[at, cols] = jnp.where(lower_rows, cot[at, cols], total)
                return carry

            lax.fori_loop(0, 4, begin, 0)

            def deep(k, carry):
                def split(i, carry):
                    at = pl.ds(pl.multiple_of(i * 128, 128), 128)
                    from_at = pl.ds(pl.multiple_of(k * NB + i * 128, 128), 128)
                    value = strips[from_at, cols]
                    top = value.astype(jnp.bfloat16)
                    high[at] = top
                    low[at] = (value - top.astype(F32)).astype(jnp.bfloat16)
                    return carry

                lax.fori_loop(0, 4, split, 0)
                inner = pl.ds(pl.multiple_of(k * NB, NB), NB)

                def product(i, carry):
                    at = pl.ds(pl.multiple_of(i * BLK, BLK), BLK)
                    top, rest, right = f_high[at, inner], f_low[at, inner], high[...]
                    total = jnp.dot(rest, right, preferred_element_type=F32)
                    total += jnp.dot(top, low[...], preferred_element_type=F32)
                    total += jnp.dot(top, right, preferred_element_type=F32)
                    out[at, cols] = out[at, cols] - total
                    return carry

                lax.fori_loop(0, NB // BLK, product, 0)
                return carry

            lax.fori_loop(0, NP, deep, 0)

        @pl.when(jnp.logical_not(plain))
        def _():
            def move(i, carry):
                at = pl.ds(pl.multiple_of(i * 128, 128), 128)
                if h == 0:
                    upper = jnp.where(row == 0, cot[at, cols], z[1, at])
                    out[at, cols] = jnp.where(lower_rows, solved[at, NB : 2 * NB], upper)
                else:
                    upper = jnp.where(row == 2, z[2, at], cot[at, cols])
                    last = jnp.where(lower_rows, solved[at, 2 * NB :], upper)
                    first = jnp.where(lower_rows, solved[at, :NB], z[0, at])
                    out[at, cols] = jnp.where(col == 7, last, first)
                return carry

            lax.fori_loop(0, 4, move, 0)


def finish(cot, solved, mixed, strips, far, near, z):
    return pl.pallas_call(
        finish_kernel,
        out_shape=jax.ShapeDtypeStruct((NB, 2 * NB), F32),
        in_specs=[VM] * 7,
        out_specs=VM,
        scratch_shapes=[
            pltpu.VMEM((NB, NB), jnp.bfloat16),
            pltpu.VMEM((NB, NB), jnp.bfloat16),
            pltpu.VMEM((NB, 3 * NB), jnp.bfloat16),
            pltpu.VMEM((NB, 3 * NB), jnp.bfloat16),
        ],
        compiler_params=pltpu.CompilerParams(vmem_limit_bytes=40 << 20),
    )(cot, solved, mixed, strips, far, near, z)


def shards(factor, cot):
    row = lax.axis_index("row")
    col = lax.axis_index("col")
    core = col % 2
    strips, blocks, other_half = spread(factor, cot)
    blocks = blocks.reshape(2, 3, NB, NB)
    l = {
        0: blocks[0, 0], 10: blocks[0, 1], 20: blocks[0, 2],
        11: blocks[1, 0], 21: blocks[1, 1], 22: blocks[1, 2],
    }
    inv = invert(jnp.stack([l[0], l[11], l[22]]))
    my_half = lax.dynamic_slice(cot, (core * 256, 0), (256, 1024))
    g6 = jnp.where(core == 0, my_half, other_half)
    g7 = jnp.where(core == 0, other_half, my_half)
    s2 = dot(g7[:, NB:], inv[2])
    s1 = dot(g7[:, :NB] - dot(s2, l[21]), inv[1])
    s0 = dot(g6[:, NB:] - dot(s2, l[20]) - dot(s1, l[10]), inv[0])
    solved, strips = along_spread(jnp.concatenate([s0, s1, s2], axis=1), factor, strips)
    lower_rows = row >= NP
    part = jnp.where(lower_rows, -dot_t(solved, factor), 0.0).reshape(3, NB, 1024)
    which = lax.broadcasted_iota(jnp.int32, (3, 1, 1), 0)
    part = jnp.where(which == row, cot[None], part)
    near = reduce_rows(part).reshape(2, 3, NB, NB)
    mixed_half, z = chain(blocks.reshape(6, NB, NB), near.reshape(6, NB, NB), inv)
    mixed, far = along_reduce(mixed_half, part)
    return finish(cot, solved, mixed, strips, far, near, z)


def solution(mesh):
    placed = (P("row", "col"), P("row", "col"))
    return jax.shard_map(
        shards, mesh=mesh, in_specs=placed, out_specs=P("row", "col"), check_vma=False
    )
```

```python
import jax
import jax.numpy as jnp
from jax import lax
from jax.experimental import pallas as pl
from jax.experimental.pallas import tpu as pltpu
from jax.sharding import PartitionSpec as P

NB = 512
NP = 3
MESH = pl.DeviceIdType.MESH
HI = lax.Precision.HIGHEST
MID = lax.Precision.HIGH
F32 = jnp.float32


def dot(a, b, precision=MID):
    return jnp.dot(a, b, precision=precision, preferred_element_type=F32)


def dot_t(a, b, precision=MID):
    return lax.dot_general(
        a, b, (((0,), (0,)), ((), ())), precision=precision, preferred_element_type=F32
    )


def place():
    row = lax.axis_index("row")
    col = lax.axis_index("col")
    return row // 4, row % 4, col // 2, col % 2


def remote(src, dst, send, recv, x, y, z, core):
    return pltpu.make_async_remote_copy(
        src_ref=src,
        dst_ref=dst,
        send_sem=send,
        recv_sem=recv,
        device_id=(x * 4 + y, z * 2 + core),
        device_id_type=MESH,
    )


def greet(devices):
    barrier = pltpu.get_barrier_semaphore()
    for x, y, z, core in devices:
        pl.semaphore_signal(
            barrier, inc=1, device_id=(x * 4 + y, z * 2 + core), device_id_type=MESH
        )
    pl.semaphore_wait(barrier, len(devices))


def plane_and_peer(x, y, z, core):
    out = []
    for dx in range(4):
        for dy in range(4):
            if dx or dy:
                out.append(((x + dx) % 4, (y + dy) % 4, z, core))
    return out + [(x, y, z, 1 - core)]


CH = 8
CR = 128 // CH
LEFT, RIGHT = pl.ds(0, NB), pl.ds(NB, NB)
ROWS = (pl.ds(0, 16), pl.ds(16, 16))
PAIR = (pl.ds(0, 2), pl.ds(2, 2))


def unit(part, u, core):
    if part == 0:
        p = u + core if u < 2 else 2
        off = NB * (1 - core) if u < 2 else NB
    else:
        p = u - core if u >= 1 else 0
        off = NB * core if u >= 1 else 0
    if isinstance(off, int):
        return p, pl.ds(off, NB)
    return p, pl.ds(pl.multiple_of(off, NB), NB)


def line(order, x, y, d):
    return ((x + d) % 4, y) if order == 0 else (x, (y + d) % 4)


def spread_steps(part, own, strips, sems, hand=None):
    scat_s, scat_r, one_s, one_r, two_s, two_r, loc = sems
    x, y, z, core = place()
    units = [unit(part, u, core) for u in range(NP)]

    def piece(ref, u, px, py):
        p, cols = units[u]
        if ref is own:
            return own.at[px, py, :, cols]
        return strips.at[p, px, py, :, cols]

    def scatter(u, d):
        tx, ty = (x + d // 4) % 4, (y + d % 4) % 4
        return remote(
            piece(own, u, tx, ty), piece(strips, u, tx, ty),
            scat_s.at[u, d], scat_r.at[u], tx, ty, z, core,
        )

    def keep(u):
        return pltpu.make_async_copy(piece(own, u, x, y), piece(strips, u, x, y), loc.at[u])

    roots = [(x == 0) & (y == units[u][0]) for u in range(NP)]
    for u in range(NP):

        @pl.when(roots[u])
        def _():
            keep(u).start()
            for d in range(15, 0, -1):
                scatter(u, d).start()

    yield

    for u in range(NP):

        @pl.when(roots[u])
        def _():
            keep(u).wait()

        @pl.when(jnp.logical_not(roots[u]))
        def _():
            here = piece(strips, u, x, y)
            remote(here, here, scat_s.at[u, 0], scat_r.at[u], x, y, z, 1 - core).wait_recv()

    def at(u, px, py, rows):
        p, cols = units[u]
        return strips.at[p, px, py, rows, cols]

    for _ in share_steps(at, one_s, one_r, two_s, two_r, hand):
        yield

    for u in range(NP):

        @pl.when(roots[u])
        def _():
            for d in range(1, 16):
                scatter(u, d).wait_send()

    yield


def piece_line(order, x, y, at):
    if order == 0:
        return pl.ds(0, 4), (y + at) % 4, ROWS[0]
    return (x + at) % 4, pl.ds(0, 4), ROWS[1]


ALL_LINES = [(order, u, at) for order in range(2) for u in range(NP) for at in range(4)]


def share_steps(ref_at, one_s, one_r, two_s, two_r, hand=None):
    x, y, z, core = place()
    every = [(order, u) for u in range(NP) for order in range(2)]
    first = []
    for order, u in every:
        for d in range(1, 4):
            here = ref_at(u, x, y, ROWS[order])
            tx, ty = line(order, x, y, d)
            first.append(
                remote(
                    here, here, one_s.at[order, u, d], one_r.at[order, u, d], tx, ty, z, core
                )
            )
    for copy in first:
        copy.start()
    yield

    for copy in first:
        copy.wait_recv()

    def block(order, u, at, pick):
        if order == 0:
            return ref_at(u, pick, (y + at) % 4, ROWS[0])
        return ref_at(u, (x + at) % 4, pick, ROWS[1])

    def second(order, u, kind):
        whole = pl.ds(0, 4)
        at, pick, d = (
            (0, whole, 1), (0, whole, 3), (3, PAIR[0], 1), (1, PAIR[1], 3)
        )[kind]
        ref = block(order, u, at, pick)
        tx, ty = line(1 - order, x, y, d)
        return remote(
            ref, ref, two_s.at[order, u, kind], two_r.at[order, u, kind], tx, ty, z, core
        )

    def arrival(order, u, kind):
        whole = pl.ds(0, 4)
        at, pick = ((3, whole), (1, whole), (2, PAIR[0]), (2, PAIR[1]))[kind]
        ref = block(order, u, at, pick)
        return remote(
            ref, ref, two_s.at[order, u, kind], two_r.at[order, u, kind], x, y, z, 1 - core
        )

    whole_line = pl.ds(0, 4)
    for order, u in every:
        for kind in (0, 1):
            second(order, u, kind).start()
    if hand:
        for order, u in every:
            hand(order, u, 0, block(order, u, 0, whole_line))
    yield

    for order, u in every:
        for kind in (0, 1):
            arrival(order, u, kind).wait_recv()
            second(order, u, kind + 2).start()
    if hand:
        for order, u in every:
            for at in (3, 1):
                hand(order, u, at, block(order, u, at, whole_line))
    yield

    for order, u in every:
        for kind in (2, 3):
            arrival(order, u, kind).wait_recv()
        if hand:
            hand(order, u, 2, block(order, u, 2, whole_line))
    yield

    for copy in first:
        copy.wait_send()
    for order, u in every:
        for kind in range(4):
            second(order, u, kind).wait_send()
    yield


AHEAD = 5


def along_steps(src, out, sems, used):
    ring_s, ring_r, peer_s, peer_r = sems
    x, y, z, core = place()
    up, down = (z + 1) % 4, (z + 3) % 4
    positions = (up, 3 - z)
    targets = (up, down)
    source = used & (z == 3)

    def chunk(owner, way, step):
        return out.at[pl.ds(owner, 1), way, step]

    def ring(way, step, block):
        mine = chunk(core, way, step)
        return remote(
            block, mine, ring_s.at[way, step], ring_r.at[way, step], x, y, targets[way], core
        )

    def across(way, step, block):
        mine = chunk(core, way, step)
        return remote(
            block, mine, peer_s.at[way, step], peer_r.at[way, step], x, y, z, 1 - core
        )

    def issue(step):
        for way in range(2):
            ring(way, step, src.at[:, way, step]).start()
        for way in range(2):
            across(way, step, src.at[:, way, step]).start()

    @pl.when(source)
    def _():
        for step in range(AHEAD):
            issue(step)
        out[pl.ds(core, 1)] = src[...]

    yield
    for tick in range(CH + 2):
        if tick + AHEAD < CH:

            @pl.when(source)
            def _():
                for way in range(2):
                    ring(way, tick, src.at[:, way, tick]).wait_send()
                issue(tick + AHEAD)

        for way in range(2):
            for pos in range(1, 4):
                step = tick - (pos - 1)
                if not 0 <= step < CH:
                    continue

                @pl.when(used & (positions[way] == pos))
                def _():
                    mine = chunk(core, way, step)
                    ring(way, step, mine).wait_recv()
                    if pos < 3:
                        ring(way, step, mine).start()
                    across(way, step, mine).start()

        yield

    @pl.when(used)
    def _():
        for step in range(CH):
            for way in range(2):
                mine, other = chunk(core, way, step), chunk(1 - core, way, step)
                remote(
                    mine, other, peer_s.at[way, step], peer_r.at[way, step],
                    x, y, z, 1 - core,
                ).wait()
                left = positions[way] < 3
                if step + AHEAD < CH:
                    left = left & (z != 3)

                @pl.when(left)
                def _():
                    ring(way, step, mine).wait_send()

    yield


def reduce_steps(part, wide, src, out, bufs, sems, hand=None):
    got, acc, tot, got2, fin = bufs
    one_s, one_r, two_s, two_r, g_s, g_r, loc = sems
    x, y, z, core = place()
    units = [unit(part, u, core) for u in range(NP)]
    every = [(order, u) for u in range(NP) for order in range(2)]

    def share(order, u, at, pick):
        p, cols = units[u]
        if order == 0:
            return p, (x + at) % 4, pick, ROWS[0], cols
        return p, pick, (y + at) % 4, ROWS[1], cols

    def one(order, u, kind, way):
        step = 1 if way == 0 else 3
        if kind == 0:
            ref = src.at[share(order, u, 2, PAIR[way])]
        elif kind == 1:
            ref = src.at[share(order, u, step, PAIR[1 - way])]
        else:
            ref = acc.at[order, u, way]
        tx, ty = line(order, x, y, step)
        return remote(
            ref, got.at[order, u, kind, way],
            one_s.at[order, u, kind * 2 + way], one_r.at[order, u, kind * 2 + way],
            tx, ty, z, core,
        )

    for kind in (0, 1):
        for order, u in every:
            for way in range(2):
                one(order, u, kind, way).start()
    yield

    for order, u in every:
        for way in range(2):
            one(order, u, 0, way).wait_recv()
            step = 1 if way == 0 else 3
            acc[order, u, way] = (
                src[share(order, u, step, PAIR[way])] + got[order, u, 0, way]
            )
            one(order, u, 2, way).start()
    yield

    def two(order, u, d):
        tx, ty = line(1 - order, x, y, d)
        index = ty if order == 0 else tx
        return remote(
            tot.at[order, u, index], got2.at[order, u, d - 1],
            two_s.at[order, u, d], two_r.at[order, u, d], tx, ty, z, core,
        )

    for order, u in every:
        for kind in (1, 2):
            for way in range(2):
                one(order, u, kind, way).wait_recv()
        for half in range(2):
            base = src[share(order, u, 0, PAIR[half])]
            tot[order, u, PAIR[half]] = base + (
                got[order, u, 2, half] + got[order, u, 1, 1 - half]
            )
        for d in range(1, 4):
            two(order, u, d).start()
    yield

    for order, u in every:
        for d in range(1, 4):
            two(order, u, d).wait_recv()
        here = y if order == 0 else x
        total = (tot[order, u, here] + got2[order, u, 0]) + (
            got2[order, u, 1] + got2[order, u, 2]
        )
        if wide:
            out[core, u, x, y, ROWS[order]] = total
        else:
            fin[order, u, x if order == 0 else y] = total

    def sends():
        for order, u in every:
            for kind in range(3):
                for way in range(2):
                    one(order, u, kind, way).wait_send()
            for d in range(1, 4):
                two(order, u, d).wait_send()

    if wide:

        def at(u, px, py, rows):
            return out.at[core, u, px, py, rows]

        for _ in share_steps(at, *wide, hand):
            yield
        sends()
        yield
        return

    def to_line(order, u):
        mine = fin.at[order, u, x if order == 0 else y]
        target = (0, y) if order == 0 else (x, units[u][0])
        return remote(
            mine, mine, g_s.at[0, order, u], g_r.at[0, order, u, x if order == 0 else y],
            *target, z, core,
        )

    def target_lines(order, u, px, py):
        if order == 0:
            return out.at[u, pl.ds(0, 4), py, ROWS[0]]
        return out.at[u, px, pl.ds(0, 4), ROWS[1]]

    def to_root(order, u):
        return remote(
            fin.at[order, u], target_lines(order, u, x, y), g_s.at[1, order, u],
            g_r.at[1, order, u, y if order == 0 else x], 0, units[u][0], z, core,
        )

    def keep(order, u):
        return pltpu.make_async_copy(
            fin.at[order, u], target_lines(order, u, x, y), loc.at[order, u]
        )

    def on_line(order, u):
        return x == 0 if order == 0 else y == units[u][0]

    def at_root(u):
        return (x == 0) & (y == units[u][0])

    for order, u in every:

        @pl.when(jnp.logical_not(on_line(order, u)))
        def _():
            to_line(order, u).start()

    yield

    for order, u in every:

        @pl.when(on_line(order, u))
        def _():
            for d in range(1, 4):
                index = ((x if order == 0 else y) + d) % 4
                here = fin.at[order, u, index]
                remote(
                    here, here, g_s.at[0, order, u], g_r.at[0, order, u, index],
                    x, y, z, 1 - core,
                ).wait_recv()

        @pl.when(on_line(order, u) & jnp.logical_not(at_root(u)))
        def _():
            to_root(order, u).start()

        @pl.when(at_root(u))
        def _():
            keep(order, u).start()

    yield

    for order, u in every:

        @pl.when(jnp.logical_not(on_line(order, u)))
        def _():
            to_line(order, u).wait_send()

        @pl.when(on_line(order, u) & jnp.logical_not(at_root(u)))
        def _():
            to_root(order, u).wait_send()

        @pl.when(at_root(u))
        def _():
            keep(order, u).wait()
            for d in range(1, 4):
                px, py = (x + d) % 4, (y + d) % 4
                there = target_lines(order, u, px, py)
                remote(
                    there, there, g_s.at[1, order, u],
                    g_r.at[1, order, u, py if order == 0 else px], x, y, z, 1 - core,
                ).wait_recv()

    sends()
    yield


DMA = pltpu.SemaphoreType.DMA
SPREAD_SEMS = [
    DMA((3, 16)), DMA((3,)), DMA((2, 3, 4)), DMA((2, 3, 4)), DMA((2, 3, 4)), DMA((2, 3, 4)),
    DMA((3,)),
]
ALONG_SEMS = [DMA((2, CH))] * 4
REDUCE_BUFS = [
    pltpu.VMEM((2, 3, 3, 2, 2, 16, NB), F32),
    pltpu.VMEM((2, 3, 2, 2, 16, NB), F32),
    pltpu.VMEM((2, 3, 4, 16, NB), F32),
    pltpu.VMEM((2, 3, 3, 16, NB), F32),
    pltpu.VMEM((2, 3, 4, 16, NB), F32),
]
REDUCE_SEMS = [
    DMA((2, 3, 6)), DMA((2, 3, 6)), DMA((2, 3, 4)), DMA((2, 3, 4)), DMA((2, 2, 3)), DMA((2, 2, 3, 4)),
    DMA((2, 3)),
]
VM = pl.BlockSpec(memory_space=pltpu.VMEM)
ANY = pl.BlockSpec(memory_space=pl.ANY)


def drive(*plan):
    for steps, count in plan:
        for _ in range(count):
            next(steps)


def spread_kernel(own, cot, strips, blocks, half, *sems):
    x, y, z, core = place()
    greet(plane_and_peer(x, y, z, core))
    ex_s, ex_r, loc, half_s, half_r = sems[-5:]
    half_copy = remote(
        cot.at[pl.ds(256 * (1 - core), 256)], half, half_s.at[0], half_r.at[0], x, y, z, 1 - core
    )
    half_copy.start()
    def over(order, u, at, ref):
        px, py, rows = piece_line(order, x, y, at)
        there = blocks.at[core, u, px, py, rows]
        return (
            remote(ref, there, ex_s.at[order, u, at], ex_r.at[order, u, at], x, y, z, 1 - core),
            pltpu.make_async_copy(ref, there, loc.at[order, u, at]),
        )

    def hand(order, u, at, ref):
        for copy in over(order, u, at, ref):
            copy.start()

    drive((spread_steps(0, own, strips, sems[:7], hand), 7))
    for order, u, at in ALL_LINES:
        px, py, rows = piece_line(order, x, y, at)
        p, cols = unit(0, u, core)
        away, here = over(order, u, at, strips.at[p, px, py, rows, cols])
        here.wait()
        away.wait_send()
        got = blocks.at[1 - core, u, px, py, rows]
        remote(
            got, got, ex_s.at[order, u, at], ex_r.at[order, u, at], x, y, z, 1 - core
        ).wait_recv()
    half_copy.wait()


def comm(collective_id, mib):
    return pltpu.CompilerParams(
        collective_id=collective_id, has_side_effects=True, vmem_limit_bytes=mib << 20
    )


def spread(factor, cot):
    return pl.pallas_call(
        spread_kernel,
        out_shape=(
            jax.ShapeDtypeStruct((3, 4, 4, 32, 1024), F32),
            jax.ShapeDtypeStruct((2, 3, 4, 4, 32, NB), F32),
            jax.ShapeDtypeStruct((256, 1024), F32),
        ),
        in_specs=[ANY, ANY],
        out_specs=(ANY, VM, VM),
        scratch_shapes=SPREAD_SEMS + [DMA((2, 3, 4))] * 3 + [DMA((1,)), DMA((1,))],
        compiler_params=comm(0, 32),
    )(factor.reshape(4, 4, 32, 1024), cot)


def with_z(x, y, z, core):
    return plane_and_peer(x, y, z, core) + [
        (x, y, (z + 1) % 4, core), (x, y, (z + 3) % 4, core)
    ]


def along_spread_kernel(src, own, _, out, strips, *sems):
    greet(with_z(*place()))
    a = along_steps(src, out, sems[7:], lax.axis_index("row") >= NP)
    s = spread_steps(1, own, strips, sems[:7])
    drive((s, 1), (a, 5), (s, 1), (a, 2), (s, 1), (a, 3), (s, 1), (a, 1), (s, 1), (a, 1), (s, 2))


def along_spread(half, factor, strips):
    out, strips = pl.pallas_call(
        along_spread_kernel,
        out_shape=(
            jax.ShapeDtypeStruct((2, 2, CH, CR, 1536), F32),
            jax.ShapeDtypeStruct((3, 4, 4, 32, 1024), F32),
        ),
        in_specs=[VM, ANY, ANY],
        out_specs=(VM, ANY),
        scratch_shapes=SPREAD_SEMS + ALONG_SEMS,
        input_output_aliases={2: 1},
        compiler_params=comm(1, 16),
    )(half.reshape(1, 2, CH, CR, 1536), factor.reshape(4, 4, 32, 1024), strips)
    return out.reshape(512, 1536), strips.reshape(1536, 1024)


def reduce_kernel(src, out, *rest):
    x, y, z, core = place()
    greet(plane_and_peer(x, y, z, core))
    bufs, sems = rest[:5], rest[5:]
    ex_s, ex_r = sems[-2:]

    def over(order, u, at, ref):
        return remote(
            ref, ref, ex_s.at[order, u, at], ex_r.at[order, u, at], x, y, z, 1 - core
        )

    def hand(order, u, at, ref):
        over(order, u, at, ref).start()

    drive((reduce_steps(0, sems[7:11], src, out, bufs, sems[:7], hand), 9))
    for order, u, at in ALL_LINES:
        px, py, rows = piece_line(order, x, y, at)
        over(order, u, at, out.at[core, u, px, py, rows]).wait_send()
        over(order, u, at, out.at[1 - core, u, px, py, rows]).wait_recv()


def reduce_rows(part):
    return pl.pallas_call(
        reduce_kernel,
        out_shape=jax.ShapeDtypeStruct((2, 3, 4, 4, 32, NB), F32),
        in_specs=[VM],
        out_specs=VM,
        scratch_shapes=REDUCE_BUFS + REDUCE_SEMS + [DMA((2, 3, 4))] * 6,
        compiler_params=comm(2, 32),
    )(part.reshape(3, 4, 4, 32, 1024))


def along_reduce_kernel(src, part, out, rest_out, *rest):
    greet(with_z(*place()))
    bufs, sems = rest[:5], rest[5:]
    a = along_steps(src, out, sems[7:], lax.axis_index("row") < NP)
    r = reduce_steps(1, None, part, rest_out, bufs, sems[:7])
    drive((r, 1), (a, 3), (r, 1), (a, 3), (r, 1), (a, 2), (r, 1), (a, 1), (r, 1), (a, 3), (r, 1))


def along_reduce(half, part):
    out, rest_out = pl.pallas_call(
        along_reduce_kernel,
        out_shape=(
            jax.ShapeDtypeStruct((2, 2, CH, CR, 1536), F32),
            jax.ShapeDtypeStruct((3, 4, 4, 32, NB), F32),
        ),
        in_specs=[VM, VM],
        out_specs=(VM, VM),
        scratch_shapes=REDUCE_BUFS + REDUCE_SEMS + ALONG_SEMS,
        compiler_params=comm(3, 40),
    )(half.reshape(1, 2, CH, CR, 1536), part.reshape(3, 4, 4, 32, 1024))
    return out.reshape(512, 1536), rest_out.reshape(3, NB, NB)


BS = 128


def invert_kernel(d_ref, o_ref):
    rows = lax.broadcasted_iota(jnp.int32, (BS, BS), 0)
    cols = lax.broadcasted_iota(jnp.int32, (BS, BS), 1)
    diag = rows == cols
    for block in range(NP * (NB // BS)):
        which, at = block // (NB // BS), pl.ds(block % (NB // BS) * BS, BS)
        base = d_ref[which, at, at]
        scale = jnp.sum(jnp.where(diag, base, 0.0), axis=1, keepdims=True)
        o_ref[which, at, at] = jnp.where(diag, 1.0 / scale, 0.0)

    def level(step, carry):
        pick = ((rows >> (step + 1)) == (cols >> (step + 1))) & (
            ((rows >> step) & 1) > ((cols >> step) & 1)
        )
        for block in range(NP * (NB // BS)):
            which, at = block // (NB // BS), pl.ds(block % (NB // BS) * BS, BS)
            have = o_ref[which, at, at]
            below = jnp.where(pick, d_ref[which, at, at], 0.0)
            o_ref[which, at, at] = have - dot(dot(have, below, HI), have, HI)
        return carry

    lax.fori_loop(0, 7, level, 0)
    size = BS
    while size < NB:
        for which in range(NP):
            for base in range(0, NB, 2 * size):
                up, down = pl.ds(base, size), pl.ds(base + size, size)
                corner = dot(
                    dot(o_ref[which, down, down], d_ref[which, down, up], HI),
                    o_ref[which, up, up], HI,
                )
                o_ref[which, down, up] = -corner
                o_ref[which, up, down] = jnp.zeros((size, size), F32)
        size *= 2


def invert(blocks):
    vm = pl.BlockSpec(memory_space=pltpu.VMEM)
    return pl.pallas_call(
        invert_kernel,
        out_shape=jax.ShapeDtypeStruct((NP, NB, NB), F32),
        in_specs=[vm],
        out_specs=vm,
        compiler_params=pltpu.CompilerParams(vmem_limit_bytes=16 << 20),
    )(blocks)


def plan():
    rows = []
    l00, l10, l20, l11, l21, l22, t00, t10, t20, t11, t21, t22, i0, i1, i2 = range(15)
    w, p, q, a2, y2, s21, s21t, a1, y1, s20, s10, s20t, s10t, a0, y0, none = range(15, 31)

    def mm(a, b, to):
        rows.append((0, a, b, none, to, 1))

    def take(a, b, to):
        rows.append((0, a, b, to, to, -1))

    def turn(a, to, add=0):
        rows.append((1, a, a, a, to, add))

    def lower(a, twice):
        rows.append((2, a, a, a, a, twice))

    def adjoint(l, i, t, a, y):
        turn(l, w)
        lower(t, 2)
        mm(w, t, p)
        lower(p, 1)
        turn(i, w)
        mm(w, p, q)
        mm(q, i, a)
        lower(a, 1)
        turn(a, y, add=1)

    adjoint(l22, i2, t22, a2, y2)
    take(y2, l21, t21)
    take(y2, l20, t20)
    mm(t21, i1, s21)
    turn(s21, s21t)
    take(s21t, l21, t11)
    take(s21t, l20, t10)
    adjoint(l11, i1, t11, a1, y1)
    take(y1, l10, t10)
    take(s21, l10, t20)
    mm(t20, i0, s20)
    mm(t10, i0, s10)
    turn(s20, s20t)
    turn(s10, s10t)
    take(s20t, l20, t00)
    take(s10t, l10, t00)
    adjoint(l00, i0, t00, a0, y0)
    coupling = ((y0, s10t, s20t), (s10, y1, s21t), (s20, s21, y2))
    result = ((a0, a0, a0), (s10, a1, a1), (s20, s21, a2))
    return rows, [x + y for x, y in zip(coupling, result)]


PLAN, PICKS = plan()
BLK = 512


def chain_kernel(plan_ref, pick_ref, l_ref, t_ref, i_ref, q_ref, z_ref, m, high, low):
    row, col = lax.axis_index("row"), lax.axis_index("col")
    for n in range(6):
        m[n] = l_ref[n]
        m[6 + n] = t_ref[n]
    for n in range(3):
        m[12 + n] = i_ref[n]
    m[30] = jnp.zeros((NB, NB), F32)

    def op(n, carry):
        kind, a, b, c, to, value = (plan_ref[n, j] for j in range(6))
        scale = value.astype(F32)

        @pl.when(kind == 0)
        def _():
            def split(i, carry):
                at = pl.ds(pl.multiple_of(i * 128, 128), 128)
                own = m[b, at]
                top = own.astype(jnp.bfloat16)
                high[0, at] = top
                high[1, at] = (own - top.astype(F32)).astype(jnp.bfloat16)
                high[2, at] = top
                own = m[a, at] * scale
                top = own.astype(jnp.bfloat16)
                low[at, :NB] = top
                low[at, NB : 2 * NB] = top
                low[at, 2 * NB :] = (own - top.astype(F32)).astype(jnp.bfloat16)
                return carry

            lax.fori_loop(0, 4, split, 0)
            right = high[...].reshape(3 * NB, NB)
            m[to] = m[c] + jnp.dot(low[...], right, preferred_element_type=F32)

        @pl.when(kind == 2)
        def _():
            def mask(i, carry):
                at = pl.ds(pl.multiple_of(i * 128, 128), 128)
                rows = lax.broadcasted_iota(jnp.int32, (128, NB), 0) + i * 128
                cols = lax.broadcasted_iota(jnp.int32, (128, NB), 1)
                own = m[a, at]
                diag = jnp.where(rows == cols, own * (0.5 * scale), 0.0)
                m[to, at] = jnp.where(rows > cols, own, diag)
                return carry

            lax.fori_loop(0, 4, mask, 0)

        @pl.when(kind == 1)
        def _():
            def turn(i, carry):
                at = pl.ds(pl.multiple_of(i * 128, 128), 128)
                m[to, :, at] = m[a, at].T + m[a, :, at] * scale
                return carry

            lax.fori_loop(0, 4, turn, 0)

        return carry

    lax.fori_loop(0, len(PLAN), op, 0)
    p = jnp.minimum(row, 2)
    half = pl.ds(pl.multiple_of(col % 2 * 256, 256), 256)
    for j in range(3):
        q_ref[:, j * NB : (j + 1) * NB] = m[pick_ref[p, j], half]
        z_ref[j] = m[pick_ref[p, 3 + j]]


def chain(blocks, near, inv):
    smem = pl.BlockSpec(memory_space=pltpu.SMEM)
    return pl.pallas_call(
        chain_kernel,
        out_shape=(
            jax.ShapeDtypeStruct((256, 3 * NB), F32),
            jax.ShapeDtypeStruct((3, NB, NB), F32),
        ),
        in_specs=[smem, smem, VM, VM, VM],
        out_specs=(VM, VM),
        scratch_shapes=[
            pltpu.VMEM((31, NB, NB), F32),
            pltpu.VMEM((3, NB, NB), jnp.bfloat16),
            pltpu.VMEM((NB, 3 * NB), jnp.bfloat16),
        ],
        compiler_params=pltpu.CompilerParams(vmem_limit_bytes=55 << 20),
    )(jnp.array(PLAN, jnp.int32), jnp.array(PICKS, jnp.int32), blocks, near, inv)


def finish_kernel(cot, solved, mixed, strips, far, near, z, out, high, low, f_high, f_low):
    row, col = lax.axis_index("row"), lax.axis_index("col")
    core = col % 2
    r = jnp.minimum(row, 2)
    lower_rows = row >= NP

    @pl.when(col < 7)
    def _():
        def split(i, carry):
            at = pl.ds(pl.multiple_of(i * 128, 128), 128)
            value = jnp.where(lower_rows, solved[at], mixed[at])
            top = value.astype(jnp.bfloat16)
            f_high[at] = top
            f_low[at] = (value - top.astype(F32)).astype(jnp.bfloat16)
            return carry

        lax.fori_loop(0, 4, split, 0)

    for h in range(2):
        cols = pl.ds(h * NB, NB)
        if h == 0:
            use_far = (core == 0) | (row == 0)
            at_far = r * (1 - core)
            at_near = jnp.maximum(r - core, 0)
            plain = col < 7
        else:
            use_far = (core == 1) & (row < 2)
            at_far = jnp.minimum(r + 1, 2)
            at_near = r * (1 - core) + 2 * core
            plain = col < 6

        @pl.when(plain)
        def _():
            def begin(i, carry):
                at = pl.ds(pl.multiple_of(i * 128, 128), 128)
                total = jnp.where(use_far, far[at_far, at], near[core, at_near, at])
                out[at, cols] = jnp.where(lower_rows, cot[at, cols], total)
                return carry

            lax.fori_loop(0, 4, begin, 0)

            def deep(k, carry):
                def split(i, carry):
                    at = pl.ds(pl.multiple_of(i * 128, 128), 128)
                    from_at = pl.ds(pl.multiple_of(k * NB + i * 128, 128), 128)
                    value = strips[from_at, cols]
                    top = value.astype(jnp.bfloat16)
                    high[at] = top
                    low[at] = (value - top.astype(F32)).astype(jnp.bfloat16)
                    return carry

                lax.fori_loop(0, 4, split, 0)
                inner = pl.ds(pl.multiple_of(k * NB, NB), NB)

                def product(i, carry):
                    at = pl.ds(pl.multiple_of(i * BLK, BLK), BLK)
                    top, rest, right = f_high[at, inner], f_low[at, inner], high[...]
                    total = jnp.dot(rest, right, preferred_element_type=F32)
                    total += jnp.dot(top, low[...], preferred_element_type=F32)
                    total += jnp.dot(top, right, preferred_element_type=F32)
                    out[at, cols] = out[at, cols] - total
                    return carry

                lax.fori_loop(0, NB // BLK, product, 0)
                return carry

            lax.fori_loop(0, NP, deep, 0)

        @pl.when(jnp.logical_not(plain))
        def _():
            def move(i, carry):
                at = pl.ds(pl.multiple_of(i * 128, 128), 128)
                if h == 0:
                    upper = jnp.where(row == 0, cot[at, cols], z[1, at])
                    out[at, cols] = jnp.where(lower_rows, solved[at, NB : 2 * NB], upper)
                else:
                    upper = jnp.where(row == 2, z[2, at], cot[at, cols])
                    last = jnp.where(lower_rows, solved[at, 2 * NB :], upper)
                    first = jnp.where(lower_rows, solved[at, :NB], z[0, at])
                    out[at, cols] = jnp.where(col == 7, last, first)
                return carry

            lax.fori_loop(0, 4, move, 0)


def finish(cot, solved, mixed, strips, far, near, z):
    return pl.pallas_call(
        finish_kernel,
        out_shape=jax.ShapeDtypeStruct((NB, 2 * NB), F32),
        in_specs=[VM] * 7,
        out_specs=VM,
        scratch_shapes=[
            pltpu.VMEM((NB, NB), jnp.bfloat16),
            pltpu.VMEM((NB, NB), jnp.bfloat16),
            pltpu.VMEM((NB, 3 * NB), jnp.bfloat16),
            pltpu.VMEM((NB, 3 * NB), jnp.bfloat16),
        ],
        compiler_params=pltpu.CompilerParams(vmem_limit_bytes=40 << 20),
    )(cot, solved, mixed, strips, far, near, z)


def shards(factor, cot):
    row = lax.axis_index("row")
    col = lax.axis_index("col")
    core = col % 2
    strips, blocks, other_half = spread(factor, cot)
    blocks = blocks.reshape(2, 3, NB, NB)
    l = {
        0: blocks[0, 0], 10: blocks[0, 1], 20: blocks[0, 2],
        11: blocks[1, 0], 21: blocks[1, 1], 22: blocks[1, 2],
    }
    inv = invert(jnp.stack([l[0], l[11], l[22]]))
    my_half = lax.dynamic_slice(cot, (core * 256, 0), (256, 1024))
    g6 = jnp.where(core == 0, my_half, other_half)
    g7 = jnp.where(core == 0, other_half, my_half)
    s2 = dot(g7[:, NB:], inv[2])
    s1 = dot(g7[:, :NB] - dot(s2, l[21]), inv[1])
    s0 = dot(g6[:, NB:] - dot(s2, l[20]) - dot(s1, l[10]), inv[0])
    solved, strips = along_spread(jnp.concatenate([s0, s1, s2], axis=1), factor, strips)
    lower_rows = row >= NP
    part = jnp.where(lower_rows, -dot_t(solved, factor), 0.0).reshape(3, NB, 1024)
    which = lax.broadcasted_iota(jnp.int32, (3, 1, 1), 0)
    part = jnp.where(which == row, cot[None], part)
    near = reduce_rows(part).reshape(2, 3, NB, NB)
    mixed_half, z = chain(blocks.reshape(6, NB, NB), near.reshape(6, NB, NB), inv)
    mixed, far = along_reduce(mixed_half, part)
    return finish(cot, solved, mixed, strips, far, near, z)


def solution(mesh):
    placed = (P("row", "col"), P("row", "col"))
    return jax.shard_map(
        shards, mesh=mesh, in_specs=placed, out_specs=P("row", "col"), check_vma=False
    )
```
